256 devices in a mesh: grp: 8 (over z), tp: 32 (over x, y, core).
Axes of the slice: x: 4, y: 4, z: 8, core: 2. Of those that a mesh axis runs over, the one named last changes fastest.
Arguments:
- hidden_in: bfloat16 [1024, 3584], P(('grp', 'tp')), may hold values from -6 to 6
- norm_gains: float32 [4, 3584], replicated, may hold values from 0.25 to 1.75
- w_qkv: bfloat16 [3584, 8192], P(None, 'tp'), may hold values from -0.09375 to 0.09375
- w_out: bfloat16 [4096, 3584], P('tp'), may hold values from -0.09375 to 0.09375
- w_gate_up: bfloat16 [2, 3584, 8192], P(None, None, 'tp'), may hold values from -0.09375 to 0.09375
- w_down: bfloat16 [8192, 3584], P('tp'), may hold values from -0.0625 to 0.0625
- prompt_keys: bfloat16 [32768, 2048], P(('grp', 'tp')), may hold values from -480 to 480, as said below
- prompt_values: bfloat16 [32768, 2048], P(('grp', 'tp')), may hold values from -6 to 6
- tail_keys: bfloat16 [1024, 64, 2048], P(('grp', 'tp')), may hold values from -480 to 480, as said below
- tail_values: bfloat16 [1024, 64, 2048], P(('grp', 'tp')), may hold values from -6 to 6
- prompt_len: int32 [80], replicated, may hold values from 1 to 4087, as said below
- group_home: int32 [80], replicated, may hold values from 0 to 7, as said below
- req_group: int32 [1024], P('grp'), may hold values from 0 to 79, as said below
- tail_len: int32 [1024], P('grp'), may hold values from 1 to 64, 32768 in all
Outputs:
- layer_out: bfloat16 [1024, 3584], P(('grp', 'tp'))
The draws below stay inside these ranges and needn't reach their ends.
Inputs may be any that keep to these rules, and one draw needn't show every extreme that they name: `group_home`: each grp device is home to exactly 10 groups. `prompt_len`: the prompts of the groups homed on one grp device lie one after another in order of group id from the first of that device's 4096 cache positions; together they hold at most 4096 positions, exactly 4096 on one home in every draw, where one group holds 4087 of them. `req_group`: of the 128 requests held by one grp device, at most 32 belong to groups homed on any one grp device; in every draw one home receives exactly 32 requests from every grp device. `prompt_keys`: cached keys, already rotated. `tail_keys`: cached keys, already rotated.
All inputs are finite; a program needn't handle non-finite values. No bound on the sum of `tail_len` on one device may be relied on, other than what follows from the above.
Results may differ from the reference program's by a relative error of at most 0.015.
Values may be sent and summed in bfloat16 or wider, within the bound.
A program may use at most 128 MiB of HBM per device.

```python
import math
import jax
import jax.numpy as jnp
import numpy as np
from jax import lax

D = 3584
HEADS = 16
KV_HEADS = 8
HEAD_DIM = 256
FF = 8192
TAIL = 64
REQ_DEV = 128
GROUPS_DEV = 10
GROUPS = 80
REQS = 1024
CAP = 4096
TOTAL_POS = 32768
SLOTS = 32
QKV = 8192
N_GRP = 8


def scaled_keys(base_key, row_total):
    key_list = jax.random.split(base_key, 6)
    width = KV_HEADS * HEAD_DIM
    quiet_scale = jnp.exp(jax.random.uniform(key_list[0], (row_total, KV_HEADS, 1), jnp.float32, math.log(0.1), 0.0))
    loud_scale = jnp.exp(jax.random.uniform(key_list[4], (row_total, KV_HEADS, 1), jnp.float32, math.log(8.0), math.log(40.0)))
    marked = jax.random.randint(key_list[5], (row_total, KV_HEADS, 1), 0, 64) == 0
    head_scale = jnp.where(marked, loud_scale, quiet_scale)
    col_scale = jnp.exp(jax.random.uniform(key_list[1], (width,), jnp.float32, math.log(0.3), math.log(3.0)))
    base_part = jnp.clip(jax.random.normal(key_list[2], (row_total, width), jnp.float32), -4.0, 4.0)
    shaped = (base_part * col_scale[None, :]).reshape(row_total, KV_HEADS, HEAD_DIM) * head_scale
    return shaped.reshape(row_total, width).astype(jnp.bfloat16)


def draw_prompt_keys(key, part):
    return scaled_keys(jax.random.fold_in(key, 101), TOTAL_POS)


def draw_tail_keys(key, part):
    return scaled_keys(jax.random.fold_in(key, 202), REQS * TAIL).reshape(REQS, TAIL, KV_HEADS * HEAD_DIM)


def layout(key):
    key_list = jax.random.split(jax.random.fold_in(key, 7), 7)
    group_order = jax.random.permutation(key_list[0], GROUPS)
    rank_home = jnp.arange(GROUPS, dtype=jnp.int32) // GROUPS_DEV
    group_home = jnp.zeros((GROUPS,), jnp.int32).at[group_order].set(rank_home)
    full_home = jax.random.randint(key_list[1], (), 0, N_GRP)
    totals = jax.random.randint(key_list[2], (N_GRP,), CAP // 4, CAP + 1)
    totals = jnp.where(jnp.arange(N_GRP, dtype=jnp.int32) == full_home, CAP, totals)
    weights = jax.random.randint(key_list[3], (GROUPS,), 1, 16)
    group_ids = jnp.arange(GROUPS, dtype=jnp.int32)
    same_home = group_home[:, None] == group_home[None, :]
    upto = group_ids[None, :] <= group_ids[:, None]
    cum_in = jnp.sum(jnp.where(same_home & upto, weights[None, :], 0), axis=1)
    cum_ex = cum_in - weights
    whole_weight = jnp.sum(jnp.where(same_home, weights[None, :], 0), axis=1)
    spare = totals[group_home] - GROUPS_DEV
    prompt_len = 1 + spare * cum_in // whole_weight - spare * cum_ex // whole_weight
    long_group = group_order[full_home * GROUPS_DEV]
    on_full = group_home == full_home
    full_lens = jnp.where(group_ids == long_group, CAP - GROUPS_DEV + 1, 1)
    prompt_len = jnp.where(on_full, full_lens, prompt_len)
    star_home = jax.random.randint(key_list[4], (), 0, N_GRP)

    def block_homes(block_key):
        pair = jax.random.split(block_key)
        others = (star_home + 1 + jnp.arange((N_GRP - 1) * SLOTS, dtype=jnp.int32) // SLOTS) % N_GRP
        picked = jax.random.permutation(pair[0], others)[:REQ_DEV - SLOTS]
        homes = jnp.concatenate([jnp.full((SLOTS,), star_home, jnp.int32), picked])
        return jax.random.permutation(pair[1], homes)
    req_homes = jax.vmap(block_homes)(jax.random.split(key_list[5], N_GRP)).reshape(REQS)
    member = jax.random.randint(key_list[6], (REQS,), 0, GROUPS_DEV)
    req_group = group_order[req_homes * GROUPS_DEV + member]
    return (group_home, prompt_len.astype(jnp.int32), req_group.astype(jnp.int32))


def draw_group_home(key, part):
    return layout(key)[0]


def draw_prompt_len(key, part):
    return layout(key)[1]


def draw_req_group(key, part):
    return layout(key)[2]


def steps_of(key, dims, shards, least, high):
    level = 1.0
    for dim, shards_of in shards:
        steps = jax.random.uniform(jax.random.fold_in(jax.random.fold_in(key, 6), dim), (shards_of,), jnp.float32, least / len(shards), high / len(shards))
        level = level * jnp.repeat(jnp.exp(steps), dims[dim] // shards_of).reshape((-1,) + (1,) * (len(dims) - 1 - dim))
    return level


def split_up(amount, total, limit, slope):
    portions = [(1 << 20) // math.isqrt(standing ** slope) + 1 for standing in range(2, amount + 1)]
    surplus, counts = total - limit - (amount - 1), [1] * (amount - 1)
    while surplus > 0:
        movable = [i for i in range(amount - 1) if counts[i] < limit]
        whole, remaining = sum([portions[i] for i in movable]), surplus
        for i in movable:
            extra = min(limit - counts[i], max(1, remaining * portions[i] // whole), surplus)
            counts[i] = counts[i] + extra
            surplus = surplus - extra
    return np.array([limit] + counts)


def ragged(own_key, number_of, total, limit, skew):
    if number_of == 2:
        one = jax.random.randint(own_key, (), max(1, total - limit), min(limit, total - 1) + 1)
        return jnp.stack([one, total - one])
    tallies = jnp.asarray(split_up(number_of, total, limit, skew), jnp.int32)
    twos = (number_of - 1) // 2
    source_of, sink = tallies[1:1 + 2 * twos:2], tallies[2:2 + 2 * twos:2]
    margin = jnp.minimum(source_of - 1, limit - sink)
    passed = jax.random.randint(jax.random.fold_in(own_key, 1), (twos,), 0, 1 << 20) % (margin + 1)
    tallies = tallies.at[1:1 + 2 * twos:2].set(source_of - passed).at[2:2 + 2 * twos:2].set(sink + passed)
    return tallies[jax.random.permutation(jax.random.fold_in(own_key, 2), number_of)]


def noise(stream_key, shape, scale, reach, cuts=(), held_as=jnp.bfloat16):
    loudness = steps_of(stream_key, shape, cuts, -0.22, 0.18) if cuts else 1.0
    entries = jax.random.normal(stream_key, shape, jnp.float32) * scale * loudness
    return jnp.minimum(jnp.maximum(entries, -reach), reach).astype(held_as)


def setup_inputs(seed: int = 0) -> dict:
    streams_of = jax.random.split(jax.random.key(seed), 15)
    return {
        "hidden_in": noise(streams_of[0], (REQS, D), 1.0, 6.0, ((0, 256),)),
        "norm_gains": jnp.clip(1.0 + 0.15 * jax.random.normal(streams_of[1], (4, D), jnp.float32), 0.25, 1.75),
        "w_qkv": noise(streams_of[2], (D, QKV), D ** -0.5, 0.09375, ((1, 32),)),
        "w_out": noise(streams_of[3], (HEADS * HEAD_DIM, D), (HEADS * HEAD_DIM) ** -0.5, 0.09375, ((0, 32),)),
        "w_gate_up": noise(streams_of[4], (2, D, FF), D ** -0.5, 0.09375, ((2, 32),)),
        "w_down": noise(streams_of[5], (FF, D), FF ** -0.5, 0.0625, ((0, 32),)),
        "prompt_keys": draw_prompt_keys(jax.random.fold_in(streams_of[14], 71), 0),
        "prompt_values": noise(streams_of[7], (TOTAL_POS, KV_HEADS * HEAD_DIM), 1.0, 6.0, ((0, 256),)),
        "tail_keys": draw_tail_keys(jax.random.fold_in(streams_of[14], 71), 0),
        "tail_values": noise(streams_of[9], (REQS, TAIL, KV_HEADS * HEAD_DIM), 1.0, 6.0, ((0, 256),)),
        "prompt_len": draw_prompt_len(jax.random.fold_in(streams_of[14], 71), 0),
        "group_home": draw_group_home(jax.random.fold_in(streams_of[14], 71), 0),
        "req_group": draw_req_group(jax.random.fold_in(streams_of[14], 71), 0),
        "tail_len": ragged(streams_of[13], REQS, REQS * (TAIL // 2), TAIL, 1).astype(jnp.int32),
    }


NORM_EPS = 1e-06
SOFT_CAP = 50.0

def rms_scale(values, gain_row):
    values = values.astype(jnp.float32)
    return values * lax.rsqrt(lax.optimization_barrier(jnp.mean(values * values, axis=-1, keepdims=True)) + NORM_EPS) * gain_row

def rotate(head_rows, position):
    half_width = head_rows.shape[-1] // 2
    freq_index = jnp.arange(half_width).astype(jnp.float32)
    frequency = jnp.exp(freq_index * (-math.log(10000.0) / half_width))
    angles = position.astype(jnp.float32)[:, None] * frequency[None, :]
    cosine = jnp.cos(angles)[:, None, :]
    sine_part = jnp.sin(angles)[:, None, :]
    head_rows = head_rows.astype(jnp.float32)
    first_half = head_rows[..., :half_width]
    second = head_rows[..., half_width:]
    return jnp.concatenate([first_half * cosine - second * sine_part, second * cosine + first_half * sine_part], axis=-1)

def capped(scores):
    return SOFT_CAP * jnp.tanh(scores * HEAD_DIM ** (-0.5) / SOFT_CAP)

def rounded(values):
    return lax.optimization_barrier(values.astype(jnp.bfloat16)).astype(jnp.float32)

def shared_part(queries, key_rows, value_rows, visible):
    scores = capped(jnp.einsum('nkjd,pkd->nkjp', queries, key_rows, precision=lax.Precision.HIGHEST))
    exponent = jnp.where(visible[:, None, None, :], jnp.exp(scores), 0.0)
    numerator = jnp.einsum('nkjp,pkd->nkjd', rounded(exponent), value_rows, precision=lax.Precision.HIGHEST)
    return (numerator, lax.optimization_barrier(jnp.sum(exponent, axis=-1)))

def own_part(queries, key_rows, value_rows, visible):
    scores = capped(jnp.einsum('nkjd,npkd->nkjp', queries, key_rows, precision=lax.Precision.HIGHEST))
    exponent = jnp.where(visible[:, None, None, :], jnp.exp(scores), 0.0)
    numerator = jnp.einsum('nkjp,npkd->nkjd', rounded(exponent), value_rows, precision=lax.Precision.HIGHEST)
    return (numerator, lax.optimization_barrier(jnp.sum(exponent, axis=-1)))

def reference(hidden_in, norm_gains, w_qkv, w_out, w_gate_up, w_down, prompt_keys, prompt_values, tail_keys, tail_values, prompt_len, group_home, req_group, tail_len):
    req_total = hidden_in.shape[0]
    q_width = HEADS * HEAD_DIM
    kv_width = KV_HEADS * HEAD_DIM
    normed = rms_scale(hidden_in, norm_gains[0]).astype(jnp.bfloat16)
    projected_qkv = jnp.dot(normed, w_qkv, preferred_element_type=jnp.float32).astype(jnp.bfloat16)
    position = prompt_len[req_group] + tail_len
    queries = rotate(projected_qkv[:, :q_width].reshape(req_total, HEADS, HEAD_DIM), position).astype(jnp.bfloat16)
    key_new = rotate(projected_qkv[:, q_width:q_width + kv_width].reshape(req_total, KV_HEADS, HEAD_DIM), position).astype(jnp.bfloat16)
    value_new = projected_qkv[:, q_width + kv_width:].reshape(req_total, KV_HEADS, HEAD_DIM)
    group_ids = jnp.arange(GROUPS)
    same_home = group_home[:, None] == group_home[None, :]
    starts = lax.optimization_barrier(jnp.sum(jnp.where(same_home & (group_ids[None, :] < group_ids[:, None]), prompt_len[None, :], 0), axis=1))
    req_home = group_home[req_group]
    req_start = starts[req_group]
    req_len = prompt_len[req_group]
    offsets = jnp.arange(CAP)
    tail_index = jnp.arange(TAIL)

    def attend_block(request_block):
        query_blk, key_blk, value_blk, home_blk, start_blk, len_blk, tkey_blk, tvalue_blk, tlen_blk = request_block
        query_heads = query_blk.astype(jnp.float32).reshape(-1, KV_HEADS, 2, HEAD_DIM)
        block_size = query_heads.shape[0]

        def per_home(running, home_index):
            first_pos = (home_index * CAP).astype(jnp.int32)
            key_rows = lax.dynamic_slice_in_dim(prompt_keys, first_pos, CAP, 0).astype(jnp.float32).reshape(CAP, KV_HEADS, HEAD_DIM)
            value_rows = lax.dynamic_slice_in_dim(prompt_values, first_pos, CAP, 0).astype(jnp.float32).reshape(CAP, KV_HEADS, HEAD_DIM)
            visible = (home_blk[:, None] == home_index) & (offsets[None, :] >= start_blk[:, None]) & (offsets[None, :] < (start_blk + len_blk)[:, None])
            part_num, part_den = shared_part(query_heads, key_rows, value_rows, visible)
            return ((running[0] + part_num, running[1] + part_den), None)
        initial = (jnp.zeros((block_size, KV_HEADS, 2, HEAD_DIM), jnp.float32), jnp.zeros((block_size, KV_HEADS, 2), jnp.float32))
        (numerator, denominator), _ = lax.scan(per_home, initial, jnp.arange(N_GRP, dtype=jnp.int32))
        tail_num, tail_den = own_part(query_heads, tkey_blk.astype(jnp.float32).reshape(block_size, TAIL, KV_HEADS, HEAD_DIM), tvalue_blk.astype(jnp.float32).reshape(block_size, TAIL, KV_HEADS, HEAD_DIM), tail_index[None, :] < tlen_blk[:, None])
        self_exp = jnp.exp(capped(jnp.einsum('nkjd,nkd->nkj', query_heads, key_blk.astype(jnp.float32), precision=lax.Precision.HIGHEST)))
        self_num = rounded(self_exp)[..., None] * value_blk.astype(jnp.float32)[:, :, None, :]
        numerator = numerator + tail_num + self_num
        denominator = denominator + tail_den + self_exp
        return (numerator / denominator[..., None]).astype(jnp.bfloat16).reshape(block_size, q_width)
    request_blocks = (queries.reshape(N_GRP, REQ_DEV, HEADS, HEAD_DIM), key_new.reshape(N_GRP, REQ_DEV, KV_HEADS, HEAD_DIM), value_new.reshape(N_GRP, REQ_DEV, KV_HEADS, HEAD_DIM), req_home.reshape(N_GRP, REQ_DEV), req_start.reshape(N_GRP, REQ_DEV), req_len.reshape(N_GRP, REQ_DEV), tail_keys.reshape(N_GRP, REQ_DEV, TAIL, kv_width), tail_values.reshape(N_GRP, REQ_DEV, TAIL, kv_width), tail_len.reshape(N_GRP, REQ_DEV))
    attn = lax.map(attend_block, request_blocks).reshape(req_total, q_width)
    attn_proj = jnp.dot(attn, w_out, preferred_element_type=jnp.float32)
    resid = (hidden_in.astype(jnp.float32) + rms_scale(attn_proj, norm_gains[1])).astype(jnp.bfloat16)
    ffn_in = rms_scale(resid, norm_gains[2]).astype(jnp.bfloat16)
    gate_part = jnp.dot(ffn_in, w_gate_up[0], preferred_element_type=jnp.float32)
    up_part = jnp.dot(ffn_in, w_gate_up[1], preferred_element_type=jnp.float32)
    hidden = (jax.nn.gelu(gate_part, approximate=True) * up_part).astype(jnp.bfloat16)
    ffn_proj = jnp.dot(hidden, w_down, preferred_element_type=jnp.float32)
    return (resid.astype(jnp.float32) + rms_scale(ffn_proj, norm_gains[3])).astype(jnp.bfloat16)
```

```python
import functools
import math

import jax
import jax.numpy as jnp
from jax import lax
from jax.experimental import pallas as pl
from jax.experimental.pallas import tpu as pltpu
from jax.sharding import PartitionSpec as P

HEADS = 16
KV_HEADS = 8
HEAD_DIM = 256
SLOTS = 32
NORM_EPS = 1e-06
SOFT_CAP = 50.0
MESH = pl.DeviceIdType.MESH
F32 = jnp.float32
BF16 = jnp.bfloat16


def rms_scale(values, gain_row):
    values = values.astype(F32)
    return (
        values * lax.rsqrt(jnp.mean(values * values, axis=-1, keepdims=True) + NORM_EPS) * gain_row
    )


def capped(scores):
    return SOFT_CAP * jnp.tanh(scores * HEAD_DIM ** (-0.5) / SOFT_CAP)


def lookup(lookup_table, index_list):
    matches = index_list[:, None] == jnp.arange(lookup_table.shape[0], dtype=jnp.int32)[None, :]
    return jnp.sum(jnp.where(matches, lookup_table[None, :], 0), axis=1)


def group_starts(prompt_len, group_home):
    group_ids = jnp.arange(prompt_len.shape[0], dtype=jnp.int32)
    same_home = group_home[:, None] == group_home[None, :]
    earlier = group_ids[None, :] < group_ids[:, None]
    return jnp.sum(jnp.where(same_home & earlier, prompt_len[None, :], 0), axis=1)


def enter(axis, n):
    me = lax.axis_index(axis)
    barrier = pltpu.get_barrier_semaphore()

    def greet(step, carry):
        pl.semaphore_signal(
            barrier, inc=1, device_id={axis: lax.rem(me + step, n)}, device_id_type=MESH
        )
        return carry

    lax.fori_loop(1, n, greet, 0)
    pl.semaphore_wait(barrier, n - 1)


def all_copies(axis, n, source, target, send_sem, recv_sem):
    me = lax.axis_index(axis)

    def outgoing(step):
        peer = lax.rem(me + step, n)
        return pltpu.make_async_remote_copy(
            src_ref=source(peer),
            dst_ref=target.at[me],
            send_sem=send_sem.at[step],
            recv_sem=recv_sem.at[me],
            device_id={axis: peer},
            device_id_type=MESH,
        )

    def incoming(step):
        peer = lax.rem(me + n - step, n)
        return pltpu.make_async_remote_copy(
            src_ref=source(me),
            dst_ref=target.at[peer],
            send_sem=send_sem.at[step],
            recv_sem=recv_sem.at[peer],
            device_id={axis: peer},
            device_id_type=MESH,
        )

    local = pltpu.make_async_copy(source(me), target.at[me], send_sem.at[0])

    def start():
        def one(step, carry):
            outgoing(step).start()
            return carry

        lax.fori_loop(1, n, one, 0)
        local.start()

    def finish():
        def one(step, carry):
            incoming(step).wait_recv()
            outgoing(step).wait_send()
            return carry

        local.wait()
        lax.fori_loop(1, n, one, 0)

    return start, finish


def vmem():
    return pl.BlockSpec(memory_space=pltpu.VMEM)


def params(which):
    return pltpu.CompilerParams(collective_id=which, has_side_effects=True)


def gather(x, axis, n, which):
    def kernel(x_ref, y_ref, send_sem, recv_sem):
        enter(axis, n)
        start, finish = all_copies(axis, n, lambda d: x_ref, y_ref, send_sem, recv_sem)
        start()
        finish()

    return pl.pallas_call(
        kernel,
        out_shape=jax.ShapeDtypeStruct((n, *x.shape), x.dtype),
        in_specs=[vmem()],
        out_specs=vmem(),
        scratch_shapes=[pltpu.SemaphoreType.DMA((n,)), pltpu.SemaphoreType.DMA((n,))],
        compiler_params=params(which),
        name=f"gather{which}",
    )(x)


def swap(x, axis, n, which):
    def kernel(x_ref, y_ref, send_sem, recv_sem):
        enter(axis, n)
        start, finish = all_copies(axis, n, lambda d: x_ref.at[d], y_ref, send_sem, recv_sem)
        start()
        finish()

    return pl.pallas_call(
        kernel,
        out_shape=jax.ShapeDtypeStruct(x.shape, x.dtype),
        in_specs=[vmem()],
        out_specs=vmem(),
        scratch_shapes=[pltpu.SemaphoreType.DMA((n,)), pltpu.SemaphoreType.DMA((n,))],
        compiler_params=params(which),
        name=f"swap{which}",
    )(x)


def place_of(me):
    x, y, core = me // 8, lax.rem(me // 2, 4), lax.rem(me, 2)
    return x, y, core, jnp.where(core == 0, y, 4 + x)


def server_of(head, m):
    return jnp.where(head < 4, (m * 4 + head) * 2, ((head - 4) * 4 + m) * 2 + 1)


def spread_heads(head_rows, n, which):
    rows = head_rows.shape[0]
    own = rows // n

    def kernel(slab_ref, head_ref, own_ref, pair_ref, send_sem, recv_sem, out_sem, in_sem):
        me = lax.axis_index("tp")
        enter("tp", n)
        start, finish = all_copies(
            "tp", n, lambda d: slab_ref.at[d], own_ref, send_sem, recv_sem
        )
        index = lax.rem(me, 2)

        def to_server(m):
            return pltpu.make_async_remote_copy(
                src_ref=head_ref,
                dst_ref=pair_ref.at[index],
                send_sem=out_sem.at[m],
                recv_sem=in_sem.at[index],
                device_id={"tp": server_of(me // 2, m)},
                device_id_type=MESH,
            )

        def local(i):
            return pltpu.make_async_copy(head_ref, pair_ref.at[i], out_sem.at[4])

        for m in range(4):

            @pl.when((me < HEADS) & (server_of(me // 2, m) != me))
            def _():
                to_server(m).start()

        start()
        served = place_of(me)[3]
        for i in range(2):

            @pl.when(2 * served + i == me)
            def _():
                local(i).start()
                local(i).wait()

            @pl.when(2 * served + i != me)
            def _():
                pltpu.make_async_remote_copy(
                    src_ref=head_ref,
                    dst_ref=pair_ref.at[i],
                    send_sem=out_sem.at[5],
                    recv_sem=in_sem.at[i],
                    device_id={"tp": 2 * served + i},
                    device_id_type=MESH,
                ).wait_recv()

        for m in range(4):

            @pl.when((me < HEADS) & (server_of(me // 2, m) != me))
            def _():
                to_server(m).wait_send()

        finish()

    return pl.pallas_call(
        kernel,
        out_shape=[
            jax.ShapeDtypeStruct((n, own, HEAD_DIM), BF16),
            jax.ShapeDtypeStruct((2, rows, HEAD_DIM), BF16),
        ],
        in_specs=[vmem(), vmem()],
        out_specs=[vmem(), vmem()],
        scratch_shapes=[
            pltpu.SemaphoreType.DMA((n,)),
            pltpu.SemaphoreType.DMA((n,)),
            pltpu.SemaphoreType.DMA((6,)),
            pltpu.SemaphoreType.DMA((2,)),
        ],
        compiler_params=params(which),
        name="spread_heads",
    )(head_rows.reshape(n, own, HEAD_DIM), head_rows)


def spread_caches(keys, values, which):
    rows = keys.shape[0]

    def kernel(key_ref, value_ref, keys_ref, values_ref, send_sem, recv_sem, local_sem):
        me = lax.axis_index("tp")
        n = KV_HEADS
        x, y, core, served = place_of(me)
        barrier = pltpu.get_barrier_semaphore()

        def server(head):
            return jnp.where(head < 4, (x * 4 + head) * 2, ((head - 4) * 4 + y) * 2 + 1)

        def source(slot):
            return jnp.where(
                core == 0, (x * 4 + slot // 2) * 2 + lax.rem(slot, 2), (slot // 2 * 4 + y) * 2 + lax.rem(slot, 2)
            )

        for step in range(1, 8):
            pl.semaphore_signal(
                barrier, inc=1, device_id={"tp": x * 8 + lax.rem(me + step, 8)}, device_id_type=MESH
            )
        for step in range(1, 4):
            for other in range(2):
                mate = (lax.rem(x + step, 4) * 4 + y) * 2 + other
                pl.semaphore_signal(barrier, inc=1, device_id={"tp": mate}, device_id_type=MESH)
        pl.semaphore_wait(barrier, 13)

        def copies(head):
            slot = jnp.where(head < 4, y, x) * 2 + core
            columns = pl.ds(pl.multiple_of(head * HEAD_DIM, HEAD_DIM), HEAD_DIM)
            for i, (src, dst) in enumerate(((key_ref, keys_ref), (value_ref, values_ref))):
                yield pltpu.make_async_remote_copy(
                    src_ref=src.at[:, columns],
                    dst_ref=dst.at[slot],
                    send_sem=send_sem.at[i, head],
                    recv_sem=recv_sem.at[i, slot],
                    device_id={"tp": server(head)},
                    device_id_type=MESH,
                )

        def locals_(head):
            slot = jnp.where(core == 0, y, x) * 2 + core
            columns = pl.ds(pl.multiple_of(head * HEAD_DIM, HEAD_DIM), HEAD_DIM)
            for i, (src, dst) in enumerate(((key_ref, keys_ref), (value_ref, values_ref))):
                yield pltpu.make_async_copy(src.at[:, columns], dst.at[slot], local_sem.at[i])

        def arrivals(slot):
            for i, (src, dst) in enumerate(((key_ref, keys_ref), (value_ref, values_ref))):
                yield pltpu.make_async_remote_copy(
                    src_ref=src.at[:, :HEAD_DIM],
                    dst_ref=dst.at[slot],
                    send_sem=send_sem.at[i, 0],
                    recv_sem=recv_sem.at[i, slot],
                    device_id={"tp": source(slot)},
                    device_id_type=MESH,
                )

        for head in range(n):

            @pl.when(server(head) != me)
            def _():
                for copy in copies(head):
                    copy.start()

            @pl.when(server(head) == me)
            def _():
                for copy in locals_(head):
                    copy.start()

        for head in range(n):

            @pl.when(server(head) == me)
            def _():
                for copy in locals_(head):
                    copy.wait()

        for slot in range(n):

            @pl.when(source(slot) != me)
            def _():
                for copy in arrivals(slot):
                    copy.wait_recv()

        for head in range(n):

            @pl.when(server(head) != me)
            def _():
                for copy in copies(head):
                    copy.wait_send()

    block = jax.ShapeDtypeStruct((KV_HEADS, rows, HEAD_DIM), BF16)
    return pl.pallas_call(
        kernel,
        out_shape=[block, block],
        in_specs=[vmem(), vmem()],
        out_specs=[vmem(), vmem()],
        scratch_shapes=[
            pltpu.SemaphoreType.DMA((2, KV_HEADS)),
            pltpu.SemaphoreType.DMA((2, KV_HEADS)),
            pltpu.SemaphoreType.DMA((2,)),
        ],
        compiler_params=params(which),
        name="spread_caches",
    )(keys, values)


def join_parts(slabs, parts, n, which):
    rows = parts.shape[1]

    def kernel(slab_ref, part_ref, own_ref, sums_ref, send_sem, recv_sem, out_sem, in_sem, local_sem):
        me = lax.axis_index("tp")
        enter("tp", n)
        x, y, core, served = place_of(me)
        quarter = jnp.where(core == 0, x, y)
        start, finish = all_copies(
            "tp", n, lambda d: slab_ref.at[d], own_ref, send_sem, recv_sem
        )

        def outgoing(i):
            return pltpu.make_async_remote_copy(
                src_ref=part_ref.at[i],
                dst_ref=sums_ref.at[quarter],
                send_sem=out_sem.at[i],
                recv_sem=in_sem.at[quarter],
                device_id={"tp": 4 * served + i},
                device_id_type=MESH,
            )

        def local(i):
            return pltpu.make_async_copy(part_ref.at[i], sums_ref.at[quarter], local_sem)

        def incoming(m):
            return pltpu.make_async_remote_copy(
                src_ref=part_ref.at[0],
                dst_ref=sums_ref.at[m],
                send_sem=out_sem.at[0],
                recv_sem=in_sem.at[m],
                device_id={"tp": server_of(me // 4, m)},
                device_id_type=MESH,
            )

        for i in range(4):

            @pl.when(4 * served + i != me)
            def _():
                outgoing(i).start()

        start()
        for i in range(4):

            @pl.when(4 * served + i == me)
            def _():
                local(i).start()
                local(i).wait()

        for m in range(4):

            @pl.when(server_of(me // 4, m) != me)
            def _():
                incoming(m).wait_recv()

        for i in range(4):

            @pl.when(4 * served + i != me)
            def _():
                outgoing(i).wait_send()

        finish()

    return pl.pallas_call(
        kernel,
        out_shape=[
            jax.ShapeDtypeStruct(slabs.shape, BF16),
            jax.ShapeDtypeStruct((4, rows, HEAD_DIM), BF16),
        ],
        in_specs=[vmem(), vmem()],
        out_specs=[vmem(), vmem()],
        scratch_shapes=[
            pltpu.SemaphoreType.DMA((n,)),
            pltpu.SemaphoreType.DMA((n,)),
            pltpu.SemaphoreType.DMA((4,)),
            pltpu.SemaphoreType.DMA((4,)),
            pltpu.SemaphoreType.DMA,
        ],
        compiler_params=params(which),
        name="join_parts",
    )(slabs, parts)


def two_words(total):
    high = total.astype(BF16)
    low = (total - lax.optimization_barrier(high).astype(F32)).astype(BF16)
    zeros = jnp.zeros((*total.shape[:-1], 126), BF16)
    return jnp.concatenate([high, low, zeros], axis=-1)


def per_device(
    n,
    planes,
    hidden_in,
    norm_gains,
    w_qkv,
    w_out,
    w_gate_up,
    w_down,
    prompt_keys,
    prompt_values,
    tail_keys,
    tail_values,
    prompt_len,
    group_home,
    req_group,
    tail_len,
):
    me = lax.axis_index("tp")
    x, y, core, _ = place_of(me)
    own, width = hidden_in.shape
    rows = own * n
    normed = rms_scale(hidden_in, norm_gains[0]).astype(BF16)
    key_blocks, value_blocks = spread_caches(prompt_keys, prompt_values, 1)
    normed_all = gather(normed, "tp", n, 0).reshape(rows, width)
    head_rows = jnp.dot(normed_all, w_qkv, preferred_element_type=F32).astype(BF16)

    req_len = lookup(prompt_len, req_group)
    position = req_len + tail_len
    half = HEAD_DIM // 2
    frequency = jnp.exp(jnp.arange(half).astype(F32) * (-math.log(10000.0) / half))
    angles = position.astype(F32)[:, None] * frequency[None, :]
    cosine, sine = jnp.cos(angles), jnp.sin(angles)
    first, second = head_rows[:, :half].astype(F32), head_rows[:, half:].astype(F32)
    rotated = jnp.concatenate(
        [first * cosine - second * sine, second * cosine + first * sine], axis=-1
    ).astype(BF16)
    head_rows = jnp.where(me < HEADS + KV_HEADS, rotated, head_rows)
    own_heads, pair = spread_heads(head_rows, n, 2)

    req_home = lookup(group_home, req_group)
    req_start = lookup(group_starts(prompt_len, group_home), req_group)
    order = jnp.arange(rows, dtype=jnp.int32)
    before = (req_home[None, :] == req_home[:, None]) & (order[None, :] < order[:, None])
    slot = req_home * SLOTS + jnp.sum(before.astype(jnp.int32), axis=1)
    pick = (jnp.arange(planes * SLOTS, dtype=jnp.int32)[:, None] == slot[None, :]).astype(BF16)
    stop = req_start + req_len
    bounds = jnp.stack([req_start // 64, req_start % 64, stop // 64, stop % 64], axis=1).astype(BF16)
    bounds = jnp.pad(bounds, ((0, 0), (0, 124)))
    visit = jnp.concatenate([pair[0], pair[1], bounds], axis=1)
    visit = jnp.dot(pick, visit, preferred_element_type=F32).astype(BF16)
    guests = swap(visit.reshape(planes, SLOTS, 2 * HEAD_DIM + 128), "grp", planes, 3)
    guests = guests.reshape(planes * SLOTS, 2 * HEAD_DIM + 128)

    limits = guests[:, 2 * HEAD_DIM : 2 * HEAD_DIM + 4].astype(F32)
    begin = limits[:, 0:1] * 64 + limits[:, 1:2]
    end = limits[:, 2:3] * 64 + limits[:, 3:4]
    block = jnp.arange(KV_HEADS, dtype=jnp.int32)
    block_device = jnp.where(
        core == 0, (x * 4 + block // 2) * 2 + block % 2, (block // 2 * 4 + y) * 2 + block % 2
    )
    piece = prompt_keys.shape[0]
    spot = (block_device[:, None] * piece + jnp.arange(piece, dtype=jnp.int32)[None, :]).reshape(1, -1)
    spot = spot.astype(F32)
    visible = (spot >= begin) & (spot < end)
    block_keys = key_blocks.reshape(-1, HEAD_DIM)
    block_values = value_blocks.reshape(-1, HEAD_DIM)
    nums, dens = [], []
    for i in range(2):
        query = guests[:, i * HEAD_DIM : (i + 1) * HEAD_DIM]
        scores = capped(
            lax.dot_general(query, block_keys, (((1,), (1,)), ((), ())), preferred_element_type=F32)
        )
        expo = jnp.where(visible, jnp.exp(scores), 0.0)
        nums.append(jnp.dot(expo.astype(BF16), block_values, preferred_element_type=F32).astype(BF16))
        dens.append(jnp.sum(expo, axis=-1, keepdims=True))
    den_words = jnp.concatenate(
        [two_words(dens[0])[:, :2], two_words(dens[1])[:, :2], jnp.zeros((planes * SLOTS, 124), BF16)],
        axis=-1,
    )
    reply = jnp.concatenate([nums[0], nums[1], den_words], axis=1)
    replies = swap(reply.reshape(planes, SLOTS, 2 * HEAD_DIM + 128), "grp", planes, 4)
    replies = replies.reshape(planes * SLOTS, 2 * HEAD_DIM + 128)
    back = lax.dot_general(
        pick, replies, (((0,), (0,)), ((), ())), preferred_element_type=F32
    ).astype(BF16)
    pad = jnp.zeros((rows, 126), BF16)
    parts = jnp.stack(
        [
            jnp.concatenate(
                [
                    back[:, i * 128 : (i + 1) * 128],
                    back[:, 2 * HEAD_DIM + (i // 2) * 2 : 2 * HEAD_DIM + (i // 2) * 2 + 2],
                    pad,
                ],
                axis=1,
            )
            for i in range(4)
        ]
    )

    queries = own_heads[:HEADS].reshape(KV_HEADS, 2, own, HEAD_DIM)
    own_keys, own_values = own_heads[HEADS : HEADS + KV_HEADS], own_heads[HEADS + KV_HEADS :]
    tail = tail_keys.shape[1]
    own_len = lax.dynamic_slice_in_dim(tail_len, me * own, own, 0)
    seen = jnp.arange(tail, dtype=jnp.int32)[None, :] < own_len[:, None]
    tails = tail_keys.reshape(own, tail, KV_HEADS, HEAD_DIM)
    tail_rows = tail_values.reshape(own, tail, KV_HEADS, HEAD_DIM)
    expo = jnp.exp(capped(jnp.einsum("kjnd,npkd->nkjp", queries, tails, preferred_element_type=F32)))
    expo = jnp.where(seen[:, None, None, :], expo, 0.0)
    own_num = jnp.einsum("nkjp,npkd->kjnd", expo.astype(BF16), tail_rows, preferred_element_type=F32)
    own_den = jnp.sum(expo, axis=-1).transpose(1, 2, 0)
    self_exp = jnp.exp(
        capped(jnp.sum(queries.astype(F32) * own_keys[:, None].astype(F32), axis=-1))
    )
    self_weight = lax.optimization_barrier(self_exp.astype(BF16)).astype(F32)
    own_num = own_num + self_weight[..., None] * own_values[:, None].astype(F32)
    own_den = (own_den + self_exp).reshape(HEADS, own, 1)
    own_num = own_num.astype(BF16).reshape(HEADS, own, 2, 128).transpose(0, 2, 1, 3)
    den_lanes = jnp.broadcast_to(two_words(own_den)[:, None], (HEADS, 2, own, 128))
    slabs = jnp.concatenate([own_num, den_lanes], axis=-1).reshape(n, own, 256)

    mine, sums = join_parts(slabs, parts, n, 5)
    total = mine.reshape(rows, 256).astype(F32) + jnp.sum(sums.astype(F32), axis=0)
    attn_share = (total[:, :128] / (total[:, 128:129] + total[:, 129:130])).astype(BF16)
    partial = jnp.dot(attn_share, w_out, preferred_element_type=F32).astype(BF16)
    attn_proj = jnp.sum(swap(partial.reshape(n, own, width), "tp", n, 6).astype(F32), axis=0)
    resid = (hidden_in.astype(F32) + rms_scale(attn_proj, norm_gains[1])).astype(BF16)
    ffn_in = rms_scale(resid, norm_gains[2]).astype(BF16)
    ffn_all = gather(ffn_in, "tp", n, 7).reshape(rows, width)
    gate = jnp.dot(ffn_all, w_gate_up[0], preferred_element_type=F32)
    up = jnp.dot(ffn_all, w_gate_up[1], preferred_element_type=F32)
    hidden_units = (jax.nn.gelu(gate, approximate=True) * up).astype(BF16)
    partial = jnp.dot(hidden_units, w_down, preferred_element_type=F32).astype(BF16)
    ffn_proj = jnp.sum(swap(partial.reshape(n, own, width), "tp", n, 8).astype(F32), axis=0)
    return (resid.astype(F32) + rms_scale(ffn_proj, norm_gains[3])).astype(BF16)


def solution(mesh):
    in_specs = (
        P(("grp", "tp"), None),
        P(),
        P(None, "tp"),
        P("tp", None),
        P(None, None, "tp"),
        P("tp", None),
        P(("grp", "tp"), None),
        P(("grp", "tp"), None),
        P(("grp", "tp"), None, None),
        P(("grp", "tp"), None, None),
        P(),
        P(),
        P("grp"),
        P("grp"),
    )
    return jax.shard_map(
        functools.partial(per_device, mesh.shape["tp"], mesh.shape["grp"]),
        mesh=mesh,
        in_specs=in_specs,
        out_specs=P(("grp", "tp"), None),
        check_vma=False,
    )
```

```python
import functools
import math

import jax
import jax.numpy as jnp
from jax import lax
from jax.experimental import pallas as pl
from jax.experimental.pallas import tpu as pltpu
from jax.sharding import PartitionSpec as P

HEADS = 16
KV_HEADS = 8
HEAD_DIM = 256
HALF = HEAD_DIM // 2
SLOTS = 32
CHIPS = 16
NORM_EPS = 1e-06
SOFT_CAP = 50.0
WIDE = 2 * HEAD_DIM + 128
MESH = pl.DeviceIdType.MESH
F32 = jnp.float32
BF16 = jnp.bfloat16
CHIP_STEPS = (1, 15, 2, 14, 3, 13, 4, 12, 5, 11, 6, 10, 7, 9, 8)
PLANE_STEPS = (4, 3, 5, 2, 6, 1, 7)


def rms_scale(values, gain_row):
    values = values.astype(F32)
    return (
        values * lax.rsqrt(jnp.mean(values * values, axis=-1, keepdims=True) + NORM_EPS) * gain_row
    )


def capped_exp(scores):
    return jnp.exp(SOFT_CAP * jnp.tanh(scores * (HEAD_DIM ** (-0.5) / SOFT_CAP)))


def lookup(lookup_table, index_list):
    matches = index_list[:, None] == jnp.arange(lookup_table.shape[0], dtype=jnp.int32)[None, :]
    return jnp.sum(jnp.where(matches, lookup_table[None, :], 0), axis=1)


def group_starts(prompt_len, group_home):
    group_ids = jnp.arange(prompt_len.shape[0], dtype=jnp.int32)
    same_home = group_home[:, None] == group_home[None, :]
    earlier = group_ids[None, :] < group_ids[:, None]
    return jnp.sum(jnp.where(same_home & earlier, prompt_len[None, :], 0), axis=1)


def remote(src, dst, send_sem, recv_sem, axis, peer):
    return pltpu.make_async_remote_copy(
        src_ref=src,
        dst_ref=dst,
        send_sem=send_sem,
        recv_sem=recv_sem,
        device_id={axis: peer},
        device_id_type=MESH,
    )


def server_of(head, m):
    return jnp.where(head < 4, (m * 4 + head) * 2, ((head - 4) * 4 + m) * 2 + 1)


def layer_kernel(
    n,
    planes,
    hidden_ref,
    gains_ref,
    cosine_ref,
    sine_ref,
    pick_ref,
    pick_t_ref,
    bounds_ref,
    seen_ref,
    w_qkv_hbm,
    w_out_hbm,
    w_gate_up_hbm,
    w_down_hbm,
    keys_hbm,
    values_hbm,
    tail_keys_hbm,
    tail_values_hbm,
    out_ref,
    w_qkv_ref,
    w_out_ref,
    w_gate_up_ref,
    w_down_ref,
    keys_ref,
    values_ref,
    tail_keys_ref,
    tail_values_ref,
    slab_ref,
    slabs_ref,
    rows_ref,
    key_blocks,
    value_blocks,
    head_ref,
    head_slabs,
    own_heads,
    pair_ref,
    visit_ref,
    guest_ref,
    reply_ref,
    answer_ref,
    query_f,
    key_f,
    value_f,
    own_f,
    own_out,
    mine_ref,
    mine_f,
    parts_ref,
    sums_ref,
    part_ref,
    half_ref,
    chip_ref,
    got_ref,
    load_sem,
    ag_send,
    ag_recv,
    fw_send,
    fw_recv,
    kv_send,
    kv_recv,
    sp_send,
    sp_recv,
    pr_send,
    pr_recv,
    z_send,
    z_recv,
    own_send,
    own_recv,
    jn_send,
    jn_recv,
    hf_send,
    hf_recv,
    rs_send,
    rs_recv,
    self_sem,
):
    me = lax.axis_index("tp")
    plane = lax.axis_index("grp")
    chip, core = me // 2, lax.rem(me, 2)
    x, y = chip // 4, lax.rem(chip, 4)
    partner = chip * 2 + 1 - core
    served = jnp.where(core == 0, y, 4 + x)
    quarter = jnp.where(core == 0, x, y)
    own, width = hidden_ref.shape
    rows = own * n

    loads = [
        pltpu.make_async_copy(src, dst, load_sem.at[i])
        for i, (src, dst) in enumerate(
            (
                (keys_hbm, keys_ref),
                (values_hbm, values_ref),
                (w_qkv_hbm, w_qkv_ref),
                (tail_keys_hbm, tail_keys_ref),
                (tail_values_hbm, tail_values_ref),
                (w_out_hbm, w_out_ref),
                (w_gate_up_hbm, w_gate_up_ref),
                (w_down_hbm, w_down_ref),
            )
        )
    ]
    for load in loads:
        load.start()

    barrier = pltpu.get_barrier_semaphore()
    for step in range(1, n):
        pl.semaphore_signal(
            barrier, inc=1, device_id={"tp": lax.rem(me + step, n)}, device_id_type=MESH
        )
    for step in range(1, planes):
        pl.semaphore_signal(
            barrier, inc=1, device_id={"grp": lax.rem(plane + step, planes)}, device_id_type=MESH
        )
    slab_ref[0] = rms_scale(hidden_ref[...], gains_ref[0:1, :]).astype(BF16)
    pl.semaphore_wait(barrier, n - 1 + planes - 1)

    def at_chip(step):
        return lax.rem(chip + step, CHIPS) * 2 + core

    def from_chip(step):
        return lax.rem(chip + CHIPS - step, CHIPS) * 2 + core

    def gather_copy(turn, step):
        return remote(
            slab_ref.at[turn],
            slabs_ref.at[turn, me],
            ag_send.at[turn, step],
            ag_recv.at[turn, step],
            "tp",
            at_chip(step),
        )

    def forward_copy(turn, step):
        source = from_chip(step)
        return remote(
            slab_ref.at[turn] if step == 0 else slabs_ref.at[turn, source],
            slabs_ref.at[turn, source],
            fw_send.at[turn, step],
            fw_recv.at[turn, step],
            "tp",
            partner,
        )

    def gather_start(turn):
        for step in CHIP_STEPS:
            gather_copy(turn, step).start()
        forward_copy(turn, 0).start()
        slabs_ref[turn, me] = slab_ref[turn]

    def gather_finish(turn):
        for step in CHIP_STEPS:
            gather_copy(turn, step).wait_recv()
            forward_copy(turn, step).start()
        for step in (0, *CHIP_STEPS):
            forward_copy(turn, step).wait_recv()
        for group in range(rows // 16):
            four = [slabs_ref[turn, group * 4 + i].astype(F32) for i in range(4)]
            rows_ref[group * 16 : group * 16 + 16, :] = jnp.concatenate(four, axis=0).astype(BF16)

    def gather_drain(turn):
        for step in CHIP_STEPS:
            gather_copy(turn, step).wait_send()
        for step in (0, *CHIP_STEPS):
            forward_copy(turn, step).wait_send()

    def half_copy(turn, step):
        group = pl.ds(lax.rem(x + step, 4) * 4, 4)
        return remote(
            part_ref.at[turn, 1 - core, group],
            half_ref.at[turn, group],
            hf_send.at[turn, step],
            hf_recv.at[turn, step],
            "tp",
            partner,
        )

    def scatter_copy(turn, step):
        target = lax.rem(chip + step, CHIPS)
        return remote(
            chip_ref.at[turn, target],
            got_ref.at[turn, chip],
            rs_send.at[turn, step],
            rs_recv.at[turn, step],
            "tp",
            target * 2 + core,
        )

    def project(turn, left, weight_ref):
        def chunk(j, carry):
            columns = pl.ds(pl.multiple_of(j * 512, 512), 512)
            block = jnp.dot(left, weight_ref[:, columns], preferred_element_type=F32)
            for d in range(n):
                part_ref[turn, d % 2, d // 2, :, columns] = block[own * d : own * d + own, :].astype(BF16)
            return carry

        lax.fori_loop(0, width // 512, chunk, 0)

    def reduce_scatter(turn):
        for step in (0, 1, 2, 3):
            half_copy(turn, step).start()
        for step in (0, 1, 2, 3):
            half_copy(turn, step).wait_recv()
        for step in (0, *CHIP_STEPS):
            target = lax.rem(chip + step, CHIPS)
            both = part_ref[turn, core, target].astype(F32) + half_ref[turn, target].astype(F32)
            chip_ref[turn, target] = both.astype(BF16)
            if step:
                scatter_copy(turn, step).start()
        total = chip_ref[turn, chip].astype(F32)
        for step in CHIP_STEPS:
            scatter_copy(turn, step).wait_recv()
            total = total + got_ref[turn, lax.rem(chip + CHIPS - step, CHIPS)].astype(F32)
        return total

    def scatter_drain(turn):
        for step in (0, 1, 2, 3):
            half_copy(turn, step).wait_send()
        for step in CHIP_STEPS:
            scatter_copy(turn, step).wait_send()

    gather_start(0)

    def kv_server(head):
        return jnp.where(head < 4, (x * 4 + head) * 2, ((head - 4) * 4 + y) * 2 + 1)

    def kv_source(slot):
        mate = lax.rem(slot, 2)
        return jnp.where(core == 0, (x * 4 + slot // 2) * 2 + mate, (slot // 2 * 4 + y) * 2 + mate)

    pieces = ((keys_ref, key_blocks), (values_ref, value_blocks))
    piece = keys_ref.shape[0]

    def kv_copy(i, head):
        slot = (y if head < 4 else x) * 2 + core
        return remote(
            pieces[i][0].at[:, head * HEAD_DIM : (head + 1) * HEAD_DIM],
            pieces[i][1].at[pl.ds(slot * piece, piece)],
            kv_send.at[i, head],
            kv_recv.at[i, slot],
            "tp",
            kv_server(head),
        )

    def kv_local(i, head):
        slot = (y if head < 4 else x) * 2 + core
        return pltpu.make_async_copy(
            pieces[i][0].at[:, head * HEAD_DIM : (head + 1) * HEAD_DIM],
            pieces[i][1].at[pl.ds(slot * piece, piece)],
            self_sem.at[i],
        )

    def kv_arrival(i, slot):
        return remote(
            pieces[i][0].at[:, :HEAD_DIM],
            pieces[i][1].at[slot * piece : (slot + 1) * piece],
            kv_send.at[i, 0],
            kv_recv.at[i, slot],
            "tp",
            kv_source(slot),
        )

    for i in range(2):
        loads[i].wait()
        for head in range(KV_HEADS):

            @pl.when(kv_server(head) != me)
            def _():
                kv_copy(i, head).start()

            @pl.when(kv_server(head) == me)
            def _():
                kv_local(i, head).start()

    gather_finish(0)
    loads[2].wait()
    head_rows = jnp.dot(rows_ref[...], w_qkv_ref[...], preferred_element_type=F32)
    head_rows = head_rows.astype(BF16).astype(F32)
    first, second = head_rows[:, :HALF], head_rows[:, HALF:]
    cosine, sine = cosine_ref[...], sine_ref[...]
    rotated = jnp.concatenate(
        [first * cosine - second * sine, second * cosine + first * sine], axis=-1
    )
    head_rows = jnp.where(me < HEADS + KV_HEADS, rotated, head_rows)
    head_ref[...] = head_rows.astype(BF16)

    index = lax.rem(me, 2)

    def to_server(m):
        return remote(
            head_ref,
            pair_ref.at[index],
            pr_send.at[m],
            pr_recv.at[index],
            "tp",
            server_of(chip, m),
        )

    for m in range(4):

        @pl.when((me < HEADS) & (server_of(chip, m) != me))
        def _():
            to_server(m).start()

    for d in range(n):
        head_slabs[d] = head_rows[own * d : own * d + own, :].astype(BF16)

    def owner_copy(step):
        peer = lax.rem(me + step, n)
        return remote(
            head_slabs.at[peer], own_heads.at[me], sp_send.at[step], sp_recv.at[step], "tp", peer
        )

    for step in range(1, n):
        owner_copy(step).start()
    own_heads[me] = head_slabs[me]

    for i in range(2):

        @pl.when(2 * served + i == me)
        def _():
            pair_ref[i] = head_ref[...]

        @pl.when(2 * served + i != me)
        def _():
            remote(
                head_ref, pair_ref.at[i], pr_send.at[0], pr_recv.at[i], "tp", 2 * served + i
            ).wait_recv()

    pick = pick_ref[...]
    for i in range(2):
        chosen = jnp.dot(pick, pair_ref[i], preferred_element_type=F32)
        visit_ref[:, i * HEAD_DIM : (i + 1) * HEAD_DIM] = chosen.astype(BF16)
    visit_ref[:, 2 * HEAD_DIM :] = jnp.dot(
        pick, bounds_ref[...], preferred_element_type=F32
    ).astype(BF16)

    def z_copy(turn, step):
        peer = lax.rem(plane + step, planes)
        src, dst = ((visit_ref, guest_ref), (reply_ref, answer_ref))[turn]
        return remote(
            src.at[pl.ds(peer * SLOTS, SLOTS)],
            dst.at[pl.ds(plane * SLOTS, SLOTS)],
            z_send.at[turn, step],
            z_recv.at[turn, step],
            "grp",
            peer,
        )

    here = pl.ds(pl.multiple_of(plane * SLOTS, SLOTS), SLOTS)
    for step in PLANE_STEPS:
        z_copy(0, step).start()
    guest_ref[here, :] = visit_ref[here, :]

    for step in range(1, n):
        owner_copy(step).wait_recv()
    for head in range(HEADS):
        block = own_heads[head].astype(F32)
        for r in range(own):
            query_f[r, head : head + 1, :] = block[r : r + 1, :]
    for head in range(KV_HEADS):
        new_key = own_heads[HEADS + head].astype(F32)
        new_value = own_heads[HEADS + KV_HEADS + head].astype(F32)
        for r in range(own):
            for i in range(2):
                spot = 2 * head + i
                key_f[r, spot : spot + 1, :] = new_key[r : r + 1, :]
                value_f[r, spot : spot + 1, :] = new_value[r : r + 1, :]
    loads[3].wait()
    loads[4].wait()
    head_of_row = lax.broadcasted_iota(jnp.int32, (HEADS, HEAD_DIM), 0) // 2
    for r in range(own):
        query = query_f[r]
        spread = jnp.concatenate(
            [jnp.where(head_of_row == k, query, 0.0) for k in range(KV_HEADS)], axis=1
        ).astype(BF16)
        scores = lax.dot_general(
            spread, tail_keys_ref[r], (((1,), (1,)), ((), ())), preferred_element_type=F32
        )
        expo = capped_exp(scores) * seen_ref[r : r + 1, :]
        every = jnp.dot(expo.astype(BF16), tail_values_ref[r], preferred_element_type=F32)
        num = jnp.zeros((HEADS, HEAD_DIM), F32)
        for k in range(KV_HEADS):
            num = jnp.where(head_of_row == k, every[:, k * HEAD_DIM : (k + 1) * HEAD_DIM], num)
        self_exp = capped_exp(jnp.sum(query * key_f[r], axis=-1, keepdims=True))
        num = num + self_exp.astype(BF16).astype(F32) * value_f[r]
        den = jnp.sum(expo, axis=-1, keepdims=True) + self_exp
        den = jnp.broadcast_to(den, (HEADS, 128))
        for head in range(HEADS):
            own_f[head, r : r + 1, :HEAD_DIM] = num[head : head + 1, :]
            own_f[head, r : r + 1, HEAD_DIM:] = den[head : head + 1, :]
    lane = lax.broadcasted_iota(jnp.int32, (own, 128), 1)
    for head in range(HEADS):
        den = own_f[head, :, HEAD_DIM:]
        high = den.astype(BF16).astype(F32)
        words = jnp.where(lane == 0, high, jnp.where(lane == 1, den - high, 0.0)).astype(BF16)
        for i in range(2):
            own_out[2 * head + i, :, :128] = own_f[head, :, i * 128 : (i + 1) * 128].astype(BF16)
            own_out[2 * head + i, :, 128:] = words

    def column_copy(step):
        peer = lax.rem(me + step, n)
        return remote(
            own_out.at[peer], mine_ref.at[me], own_send.at[step], own_recv.at[step], "tp", peer
        )

    for step in range(1, n):
        column_copy(step).start()
    mine_ref[me] = own_out[me]

    for i in range(2):
        for head in range(KV_HEADS):

            @pl.when(kv_server(head) == me)
            def _():
                kv_local(i, head).wait()

        for slot in range(KV_HEADS):

            @pl.when(kv_source(slot) != me)
            def _():
                kv_arrival(i, slot).wait_recv()

    for step in PLANE_STEPS:
        z_copy(0, step).wait_recv()
    at = lax.broadcasted_iota(jnp.int32, (1, KV_HEADS * piece), 1)
    block = at // piece
    pair_of, mate = block // 2, lax.rem(block, 2)
    device = jnp.where(core == 0, (x * 4 + pair_of) * 2 + mate, (pair_of * 4 + y) * 2 + mate)
    spot = (device * piece + lax.rem(at, piece)).astype(F32)
    many = planes * SLOTS // 2
    lanes = lax.broadcasted_iota(jnp.int32, (many, 128), 1)
    for j in range(2):
        part = slice(j * many, (j + 1) * many)
        limits = guest_ref[part, 2 * HEAD_DIM :].astype(F32)
        begin = limits[:, 0:1] * 64 + limits[:, 1:2]
        end = limits[:, 2:3] * 64 + limits[:, 3:4]
        visible = (spot >= begin) & (spot < end)
        words = jnp.zeros((many, 128), F32)
        for i in range(2):
            span = slice(i * HEAD_DIM, (i + 1) * HEAD_DIM)
            scores = lax.dot_general(
                guest_ref[part, span],
                key_blocks[...],
                (((1,), (1,)), ((), ())),
                preferred_element_type=F32,
            )
            expo = jnp.where(visible, capped_exp(scores), 0.0)
            num = jnp.dot(expo.astype(BF16), value_blocks[...], preferred_element_type=F32)
            reply_ref[part, span] = num.astype(BF16)
            den = jnp.sum(expo, axis=-1, keepdims=True)
            high = den.astype(BF16).astype(F32)
            words = jnp.where(lanes == 2 * i, high, words)
            words = jnp.where(lanes == 2 * i + 1, den - high, words)
        reply_ref[part, 2 * HEAD_DIM :] = words.astype(BF16)
    for step in PLANE_STEPS:
        z_copy(1, step).start()
    answer_ref[here, :] = reply_ref[here, :]
    for step in PLANE_STEPS:
        z_copy(1, step).wait_recv()

    back = jnp.dot(pick_t_ref[...], answer_ref[...], preferred_element_type=F32).astype(BF16)
    for i in range(4):
        parts_ref[i, :, :128] = back[:, i * 128 : (i + 1) * 128]
        parts_ref[i, :, 128:] = back[:, 2 * HEAD_DIM :]

    def join_copy(i):
        return remote(
            parts_ref.at[i],
            sums_ref.at[quarter],
            jn_send.at[i],
            jn_recv.at[quarter],
            "tp",
            4 * served + i,
        )

    for i in range(4):

        @pl.when(4 * served + i != me)
        def _():
            join_copy(i).start()

        @pl.when(4 * served + i == me)
        def _():
            sums_ref[quarter] = parts_ref[i]

    for step in range(1, n):
        column_copy(step).wait_recv()
    for p in range(n // 2):
        mine_f[2 * own * p : 2 * own * (p + 1), :] = jnp.concatenate(
            [mine_ref[2 * p].astype(F32), mine_ref[2 * p + 1].astype(F32)], axis=0
        )
    for m in range(4):

        @pl.when(server_of(me // 4, m) != me)
        def _():
            remote(
                parts_ref.at[0],
                sums_ref.at[m],
                jn_send.at[0],
                jn_recv.at[m],
                "tp",
                server_of(me // 4, m),
            ).wait_recv()

    num = mine_f[:, :128]
    den = mine_f[:, 128:129] + mine_f[:, 129:130]
    lower = lax.rem(me, 4) < 2
    for m in range(4):
        num = num + sums_ref[m, :, :128].astype(F32)
        words = sums_ref[m, :, 128:].astype(F32)
        den = den + jnp.where(lower, words[:, 0:1] + words[:, 1:2], words[:, 2:3] + words[:, 3:4])
    attn = (num / den).astype(BF16)

    loads[5].wait()
    project(0, attn, w_out_ref)
    attn_proj = reduce_scatter(0)
    resid = hidden_ref[...].astype(F32) + rms_scale(attn_proj, gains_ref[1:2, :])
    resid = resid.astype(BF16).astype(F32)
    slab_ref[1] = rms_scale(resid, gains_ref[2:3, :]).astype(BF16)
    gather_start(1)
    gather_finish(1)
    loads[6].wait()
    loads[7].wait()
    gate = jnp.dot(rows_ref[...], w_gate_up_ref[0], preferred_element_type=F32)
    up = jnp.dot(rows_ref[...], w_gate_up_ref[1], preferred_element_type=F32)
    bent = jnp.tanh(math.sqrt(2.0 / math.pi) * (gate + 0.044715 * gate * gate * gate))
    hidden_units = (0.5 * gate * (1.0 + bent) * up).astype(BF16)
    project(1, hidden_units, w_down_ref)
    ffn_proj = reduce_scatter(1)
    out_ref[...] = (resid + rms_scale(ffn_proj, gains_ref[3:4, :])).astype(BF16)

    for turn in range(2):
        gather_drain(turn)
        scatter_drain(turn)
        for step in PLANE_STEPS:
            z_copy(turn, step).wait_send()
    for i in range(2):
        for head in range(KV_HEADS):

            @pl.when(kv_server(head) != me)
            def _():
                kv_copy(i, head).wait_send()

    for m in range(4):

        @pl.when((me < HEADS) & (server_of(chip, m) != me))
        def _():
            to_server(m).wait_send()

        @pl.when(4 * served + m != me)
        def _():
            join_copy(m).wait_send()

    for step in range(1, n):
        owner_copy(step).wait_send()
        column_copy(step).wait_send()


def layer(n, planes, small, large):
    own, width = small[0].shape
    rows = own * n
    piece = large[4].shape[0]
    dma = pltpu.SemaphoreType.DMA

    def bf(*shape):
        return pltpu.VMEM(shape, BF16)

    def f32(*shape):
        return pltpu.VMEM(shape, F32)

    slots = planes * SLOTS
    scratch = [
        *(bf(*a.shape) for a in large),
        bf(2, own, width),
        bf(2, n, own, width),
        bf(rows, width),
        bf(KV_HEADS * piece, HEAD_DIM),
        bf(KV_HEADS * piece, HEAD_DIM),
        bf(rows, HEAD_DIM),
        bf(n, own, HEAD_DIM),
        bf(n, own, HEAD_DIM),
        bf(2, rows, HEAD_DIM),
        bf(slots, WIDE),
        bf(slots, WIDE),
        bf(slots, WIDE),
        bf(slots, WIDE),
        f32(own, HEADS, HEAD_DIM),
        f32(own, HEADS, HEAD_DIM),
        f32(own, HEADS, HEAD_DIM),
        f32(HEADS, own, HEAD_DIM + 128),
        bf(n, own, HEAD_DIM),
        bf(n, own, HEAD_DIM),
        f32(rows, HEAD_DIM),
        bf(4, rows, HEAD_DIM),
        bf(4, rows, HEAD_DIM),
        bf(2, 2, CHIPS, own, width),
        bf(2, CHIPS, own, width),
        bf(2, CHIPS, own, width),
        bf(2, CHIPS, own, width),
        dma((8,)),
        dma((2, CHIPS)),
        dma((2, CHIPS)),
        dma((2, CHIPS)),
        dma((2, CHIPS)),
        dma((2, KV_HEADS)),
        dma((2, KV_HEADS)),
        dma((n,)),
        dma((n,)),
        dma((4,)),
        dma((2,)),
        dma((2, planes)),
        dma((2, planes)),
        dma((n,)),
        dma((n,)),
        dma((4,)),
        dma((4,)),
        dma((2, 4)),
        dma((2, 4)),
        dma((2, CHIPS)),
        dma((2, CHIPS)),
        dma((2,)),
    ]
    return pl.pallas_call(
        functools.partial(layer_kernel, n, planes),
        out_shape=jax.ShapeDtypeStruct((own, width), BF16),
        in_specs=[pl.BlockSpec(memory_space=pltpu.VMEM)] * len(small)
        + [pl.BlockSpec(memory_space=pl.ANY)] * len(large),
        out_specs=pl.BlockSpec(memory_space=pltpu.VMEM),
        scratch_shapes=scratch,
        compiler_params=pltpu.CompilerParams(
            collective_id=0, has_side_effects=True, vmem_limit_bytes=60 * 1024 * 1024
        ),
        name="layer",
    )(*small, *large)


def per_device(
    n,
    planes,
    hidden_in,
    norm_gains,
    w_qkv,
    w_out,
    w_gate_up,
    w_down,
    prompt_keys,
    prompt_values,
    tail_keys,
    tail_values,
    prompt_len,
    group_home,
    req_group,
    tail_len,
):
    me = lax.axis_index("tp")
    own = hidden_in.shape[0]
    rows = own * n
    req_len = lookup(prompt_len, req_group)
    position = req_len + tail_len
    frequency = jnp.exp(jnp.arange(HALF).astype(F32) * (-math.log(10000.0) / HALF))
    angles = position.astype(F32)[:, None] * frequency[None, :]
    req_home = lookup(group_home, req_group)
    req_start = lookup(group_starts(prompt_len, group_home), req_group)
    order = jnp.arange(rows, dtype=jnp.int32)
    before = (req_home[None, :] == req_home[:, None]) & (order[None, :] < order[:, None])
    slot = req_home * SLOTS + jnp.sum(before.astype(jnp.int32), axis=1)
    slot_ids = jnp.arange(planes * SLOTS, dtype=jnp.int32)
    pick = (slot_ids[:, None] == slot[None, :]).astype(BF16)
    pick_t = (slot_ids[None, :] == slot[:, None]).astype(BF16)
    stop = req_start + req_len
    bounds = jnp.stack([req_start // 64, req_start % 64, stop // 64, stop % 64], axis=1).astype(BF16)
    bounds = jnp.pad(bounds, ((0, 0), (0, 124)))
    own_len = lax.dynamic_slice_in_dim(tail_len, me * own, own, 0)
    tail = tail_keys.shape[1]
    seen = (jnp.arange(tail, dtype=jnp.int32)[None, :] < own_len[:, None]).astype(F32)
    return layer(
        n,
        planes,
        (hidden_in, norm_gains, jnp.cos(angles), jnp.sin(angles), pick, pick_t, bounds, seen),
        (w_qkv, w_out, w_gate_up, w_down, prompt_keys, prompt_values, tail_keys, tail_values),
    )


def solution(mesh):
    in_specs = (
        P(("grp", "tp"), None),
        P(),
        P(None, "tp"),
        P("tp", None),
        P(None, None, "tp"),
        P("tp", None),
        P(("grp", "tp"), None),
        P(("grp", "tp"), None),
        P(("grp", "tp"), None, None),
        P(("grp", "tp"), None, None),
        P(),
        P(),
        P("grp"),
        P("grp"),
    )
    return jax.shard_map(
        functools.partial(per_device, mesh.shape["tp"], mesh.shape["grp"]),
        mesh=mesh,
        in_specs=in_specs,
        out_specs=P(("grp", "tp"), None),
        check_vma=False,
    )
```

```python
import functools
import math

import jax
import jax.numpy as jnp
from jax import lax
from jax.experimental import pallas as pl
from jax.experimental.pallas import tpu as pltpu
from jax.sharding import PartitionSpec as P

HEADS = 16
KV_HEADS = 8
HEAD_DIM = 256
HALF = HEAD_DIM // 2
SLOTS = 32
CHIPS = 16
NORM_EPS = 1e-06
SOFT_CAP = 50.0
WIDE = 2 * HEAD_DIM + 128
MESH = pl.DeviceIdType.MESH
F32 = jnp.float32
BF16 = jnp.bfloat16
CHIP_STEPS = (1, 15, 2, 14, 3, 13, 4, 12, 5, 11, 6, 10, 7, 9, 8)
PLANE_STEPS = (4, 3, 5, 2, 6, 1, 7)


def rms_scale(values, gain_row):
    values = values.astype(F32)
    return (
        values * lax.rsqrt(jnp.mean(values * values, axis=-1, keepdims=True) + NORM_EPS) * gain_row
    )


def capped_exp(scores):
    return jnp.exp(SOFT_CAP * jnp.tanh(scores * (HEAD_DIM ** (-0.5) / SOFT_CAP)))


def remote(src, dst, send_sem, recv_sem, axis, peer):
    return pltpu.make_async_remote_copy(
        src_ref=src,
        dst_ref=dst,
        send_sem=send_sem,
        recv_sem=recv_sem,
        device_id={axis: peer},
        device_id_type=MESH,
    )


def server_of(head, m):
    return jnp.where(head < 4, (m * 4 + head) * 2, ((head - 4) * 4 + m) * 2 + 1)


def layer_kernel(
    n,
    planes,
    hidden_ref,
    gains_ref,
    prompt_len_ref,
    group_home_ref,
    req_group_ref,
    tail_len_ref,
    w_qkv_hbm,
    w_out_hbm,
    w_gate_up_hbm,
    w_down_hbm,
    keys_hbm,
    values_hbm,
    tail_keys_hbm,
    tail_values_hbm,
    out_ref,
    w_qkv_ref,
    w_out_ref,
    w_gate_up_ref,
    w_down_ref,
    keys_ref,
    values_ref,
    tail_keys_ref,
    tail_values_ref,
    slab_ref,
    slabs_ref,
    rows_ref,
    key_blocks,
    value_blocks,
    head_ref,
    head_slabs,
    own_heads,
    pair_ref,
    visit_ref,
    guest_ref,
    reply_ref,
    answer_ref,
    query_f,
    key_f,
    value_f,
    own_f,
    own_out,
    mine_ref,
    mine_f,
    parts_ref,
    sums_ref,
    part_ref,
    half_ref,
    chip_ref,
    got_ref,
    word_ref,
    words_ref,
    bound_ref,
    limit_ref,
    table_ref,
    load_sem,
    ag_send,
    ag_recv,
    fw_send,
    fw_recv,
    kv_send,
    kv_recv,
    sp_send,
    sp_recv,
    pr_send,
    pr_recv,
    z_send,
    z_recv,
    own_send,
    own_recv,
    jn_send,
    jn_recv,
    hf_send,
    hf_recv,
    rs_send,
    rs_recv,
    self_sem,
    wd_send,
    wd_recv,
    lm_send,
    lm_recv,
):
    me = lax.axis_index("tp")
    plane = lax.axis_index("grp")
    chip, core = me // 2, lax.rem(me, 2)
    x, y = chip // 4, lax.rem(chip, 4)
    partner = chip * 2 + 1 - core
    served = jnp.where(core == 0, y, 4 + x)
    quarter = jnp.where(core == 0, x, y)
    own, width = hidden_ref.shape
    rows = own * n

    loads = [
        pltpu.make_async_copy(src, dst, load_sem.at[i])
        for i, (src, dst) in enumerate(
            (
                (keys_hbm, keys_ref),
                (values_hbm, values_ref),
                (w_qkv_hbm, w_qkv_ref),
                (tail_keys_hbm, tail_keys_ref),
                (tail_values_hbm, tail_values_ref),
                (w_out_hbm, w_out_ref),
                (w_gate_up_hbm, w_gate_up_ref),
                (w_down_hbm, w_down_ref),
            )
        )
    ]
    for load in loads:
        load.start()

    barrier = pltpu.get_barrier_semaphore()
    for step in range(1, n):
        pl.semaphore_signal(
            barrier, inc=1, device_id={"tp": lax.rem(me + step, n)}, device_id_type=MESH
        )
    for step in range(1, planes):
        pl.semaphore_signal(
            barrier, inc=1, device_id={"grp": lax.rem(plane + step, planes)}, device_id_type=MESH
        )
    slab_ref[0] = rms_scale(hidden_ref[...], gains_ref[0:1, :]).astype(BF16)
    pl.semaphore_wait(barrier, n - 1 + planes - 1)

    def at_chip(step):
        return lax.rem(chip + step, CHIPS) * 2 + core

    def from_chip(step):
        return lax.rem(chip + CHIPS - step, CHIPS) * 2 + core

    def gather_copy(turn, step):
        return remote(
            slab_ref.at[turn],
            slabs_ref.at[turn, me],
            ag_send.at[turn, step],
            ag_recv.at[turn, step],
            "tp",
            at_chip(step),
        )

    def forward_copy(turn, step):
        source = from_chip(step)
        return remote(
            slab_ref.at[turn] if step == 0 else slabs_ref.at[turn, source],
            slabs_ref.at[turn, source],
            fw_send.at[turn, step],
            fw_recv.at[turn, step],
            "tp",
            partner,
        )

    def gather_start(turn):
        for step in CHIP_STEPS:
            gather_copy(turn, step).start()
        forward_copy(turn, 0).start()
        slabs_ref[turn, me] = slab_ref[turn]

    def gather_finish(turn):
        for step in CHIP_STEPS:
            gather_copy(turn, step).wait_recv()
            forward_copy(turn, step).start()
        for step in (0, *CHIP_STEPS):
            forward_copy(turn, step).wait_recv()
        for group in range(rows // 16):
            four = [slabs_ref[turn, group * 4 + i].astype(F32) for i in range(4)]
            rows_ref[group * 16 : group * 16 + 16, :] = jnp.concatenate(four, axis=0).astype(BF16)

    def gather_drain(turn):
        for step in CHIP_STEPS:
            gather_copy(turn, step).wait_send()
        for step in (0, *CHIP_STEPS):
            forward_copy(turn, step).wait_send()

    def half_copy(turn, step):
        group = pl.ds(lax.rem(x + step, 4) * 4, 4)
        return remote(
            part_ref.at[turn, 1 - core, group],
            half_ref.at[turn, group],
            hf_send.at[turn, step],
            hf_recv.at[turn, step],
            "tp",
            partner,
        )

    def scatter_copy(turn, step):
        target = lax.rem(chip + step, CHIPS)
        return remote(
            chip_ref.at[turn, target],
            got_ref.at[turn, chip],
            rs_send.at[turn, step],
            rs_recv.at[turn, step],
            "tp",
            target * 2 + core,
        )

    def project(turn, left, weight_ref):
        def chunk(j, carry):
            columns = pl.ds(pl.multiple_of(j * 512, 512), 512)
            block = jnp.dot(left, weight_ref[:, columns], preferred_element_type=F32)
            for d in range(n):
                part_ref[turn, d % 2, d // 2, :, columns] = block[own * d : own * d + own, :].astype(BF16)
            return carry

        lax.fori_loop(0, width // 512, chunk, 0)

    def reduce_scatter(turn):
        for step in (0, 1, 2, 3):
            half_copy(turn, step).start()
        for step in (0, 1, 2, 3):
            half_copy(turn, step).wait_recv()
        for step in (0, *CHIP_STEPS):
            target = lax.rem(chip + step, CHIPS)
            both = part_ref[turn, core, target].astype(F32) + half_ref[turn, target].astype(F32)
            chip_ref[turn, target] = both.astype(BF16)
            if step:
                scatter_copy(turn, step).start()
        total = chip_ref[turn, chip].astype(F32)
        for step in CHIP_STEPS:
            scatter_copy(turn, step).wait_recv()
            total = total + got_ref[turn, lax.rem(chip + CHIPS - step, CHIPS)].astype(F32)
        return total

    def scatter_drain(turn):
        for step in (0, 1, 2, 3):
            half_copy(turn, step).wait_send()
        for step in CHIP_STEPS:
            scatter_copy(turn, step).wait_send()

    gather_start(0)

    table_ref[...] = jnp.full((8, 128), -1.0, F32)
    groups = prompt_len_ref.shape[1]
    table_ref[0:1, :groups] = prompt_len_ref[...].astype(F32)
    table_ref[1:2, :groups] = group_home_ref[...].astype(F32)
    table_ref[2:3, :] = req_group_ref[...].astype(F32)
    table_ref[3:4, :] = tail_len_ref[...].astype(F32)
    len_row, home_row = table_ref[0:1, :], table_ref[1:2, :]
    tail_row = table_ref[3:4, :]
    down = lax.broadcasted_iota(jnp.int32, (128, 128), 0)
    along = lax.broadcasted_iota(jnp.int32, (128, 128), 1)
    unit = (down == along).astype(BF16)
    line = lax.broadcasted_iota(jnp.int32, (8, 128), 0)

    def stacked(*lines):
        total = jnp.zeros((8, 128), F32)
        for i, value in enumerate(lines):
            total = jnp.where(line == i, value, total)
        return total.astype(BF16)

    def split(value):
        high = jnp.floor(value * (1 / 64))
        return high, value - 64 * high

    def turned(left, right):
        return lax.dot_general(left, right, (((1,), (1,)), ((), ())), preferred_element_type=F32)

    columns = turned(unit, stacked(*split(len_row), home_row, table_ref[2:3, :], tail_row))
    len_column = columns[:, 0:1] * 64 + columns[:, 1:2]
    earlier = (columns[:, 2:3] == home_row) & (down < along)
    start_row = jnp.sum(jnp.where(earlier, len_column, 0.0), axis=0, keepdims=True)
    of_group = stacked(*split(len_row), home_row, *split(start_row))
    chosen = (columns[:, 3:4] == along.astype(F32)).astype(BF16)
    req = turned(chosen, of_group)
    req_row = turned(of_group, chosen)
    req_len = req[:, 0:1] * 64 + req[:, 1:2]
    req_stop = req[:, 3:4] * 64 + req[:, 4:5] + req_len
    same = req[:, 2:3] == req_row[2:3, :]
    rank = jnp.sum(jnp.where(same & (along < down), 1.0, 0.0), axis=1, keepdims=True)
    rank_row = jnp.sum(jnp.where(same & (down < along), 1.0, 0.0), axis=0, keepdims=True)
    slots = planes * SLOTS
    slot_down = lax.broadcasted_iota(jnp.int32, (slots, rows), 0).astype(F32)
    slot_along = lax.broadcasted_iota(jnp.int32, (rows, slots), 1).astype(F32)
    pick = (slot_down == req_row[2:3, :] * SLOTS + rank_row).astype(BF16)
    pick_t = (slot_along == req[:, 2:3] * SLOTS + rank).astype(BF16)
    bounds = jnp.zeros((rows, 128), F32)
    for i, value in enumerate((req[:, 3:4], req[:, 4:5], *split(req_stop))):
        bounds = jnp.where(along == i, value, bounds)
    bound_ref[...] = jnp.dot(pick, bounds.astype(BF16), preferred_element_type=F32).astype(BF16)

    def limit_copy(step):
        peer = lax.rem(plane + step, planes)
        return remote(
            bound_ref.at[pl.ds(peer * SLOTS, SLOTS)],
            limit_ref.at[pl.ds(plane * SLOTS, SLOTS)],
            lm_send.at[step],
            lm_recv.at[step],
            "grp",
            peer,
        )

    here = pl.ds(pl.multiple_of(plane * SLOTS, SLOTS), SLOTS)
    for step in PLANE_STEPS:
        limit_copy(step).start()
    limit_ref[here, :] = bound_ref[here, :]
    frequency = jnp.exp(along[0:1, :].astype(F32) * (-math.log(10000.0) / HALF))
    angles = (req_len + columns[:, 4:5]) * frequency
    cosine, sine = jnp.cos(angles), jnp.sin(angles)

    def kv_server(head):
        return jnp.where(head < 4, (x * 4 + head) * 2, ((head - 4) * 4 + y) * 2 + 1)

    def kv_source(slot):
        mate = lax.rem(slot, 2)
        return jnp.where(core == 0, (x * 4 + slot // 2) * 2 + mate, (slot // 2 * 4 + y) * 2 + mate)

    pieces = ((keys_ref, key_blocks), (values_ref, value_blocks))
    piece = keys_ref.shape[0]

    def kv_copy(i, head):
        slot = (y if head < 4 else x) * 2 + core
        return remote(
            pieces[i][0].at[:, head * HEAD_DIM : (head + 1) * HEAD_DIM],
            pieces[i][1].at[pl.ds(slot * piece, piece)],
            kv_send.at[i, head],
            kv_recv.at[i, slot],
            "tp",
            kv_server(head),
        )

    def kv_local(i, head):
        slot = (y if head < 4 else x) * 2 + core
        return pltpu.make_async_copy(
            pieces[i][0].at[:, head * HEAD_DIM : (head + 1) * HEAD_DIM],
            pieces[i][1].at[pl.ds(slot * piece, piece)],
            self_sem.at[i],
        )

    def kv_arrival(i, slot):
        return remote(
            pieces[i][0].at[:, :HEAD_DIM],
            pieces[i][1].at[slot * piece : (slot + 1) * piece],
            kv_send.at[i, 0],
            kv_recv.at[i, slot],
            "tp",
            kv_source(slot),
        )

    gather_finish(0)
    loads[2].wait()
    head_rows = jnp.dot(rows_ref[...], w_qkv_ref[...], preferred_element_type=F32)
    head_rows = head_rows.astype(BF16).astype(F32)
    first, second = head_rows[:, :HALF], head_rows[:, HALF:]
    rotated = jnp.concatenate(
        [first * cosine - second * sine, second * cosine + first * sine], axis=-1
    )
    head_rows = jnp.where(me < HEADS + KV_HEADS, rotated, head_rows)
    head_ref[...] = head_rows.astype(BF16)

    index = lax.rem(me, 2)

    def to_server(m):
        return remote(
            head_ref,
            pair_ref.at[index],
            pr_send.at[m],
            pr_recv.at[index],
            "tp",
            server_of(chip, m),
        )

    for m in range(4):

        @pl.when((me < HEADS) & (server_of(chip, m) != me))
        def _():
            to_server(m).start()

    for d in range(n):
        head_slabs[d] = head_rows[own * d : own * d + own, :].astype(BF16)

    def owner_copy(step):
        peer = lax.rem(me + step, n)
        return remote(
            head_slabs.at[peer], own_heads.at[me], sp_send.at[step], sp_recv.at[step], "tp", peer
        )

    for step in range(1, n):
        owner_copy(step).start()
    own_heads[me] = head_slabs[me]

    for i in range(2):

        @pl.when(2 * served + i == me)
        def _():
            pair_ref[i] = head_ref[...]

        @pl.when(2 * served + i != me)
        def _():
            remote(
                head_ref, pair_ref.at[i], pr_send.at[0], pr_recv.at[i], "tp", 2 * served + i
            ).wait_recv()

    for i in range(2):
        chosen = jnp.dot(pick, pair_ref[i], preferred_element_type=F32)
        visit_ref[:, i * HEAD_DIM : (i + 1) * HEAD_DIM] = chosen.astype(BF16)

    def z_copy(turn, step):
        peer = lax.rem(plane + step, planes)
        src, dst = ((visit_ref, guest_ref), (reply_ref, answer_ref))[turn]
        return remote(
            src.at[pl.ds(peer * SLOTS, SLOTS)],
            dst.at[pl.ds(plane * SLOTS, SLOTS)],
            z_send.at[turn, step],
            z_recv.at[turn, step],
            "grp",
            peer,
        )

    for step in PLANE_STEPS:
        z_copy(0, step).start()
    guest_ref[here, :] = visit_ref[here, :]

    for i in range(2):
        loads[i].wait()
        for head in range(KV_HEADS):

            @pl.when(kv_server(head) != me)
            def _():
                kv_copy(i, head).start()

            @pl.when(kv_server(head) == me)
            def _():
                kv_local(i, head).start()

    for step in range(1, n):
        owner_copy(step).wait_recv()
    for head in range(HEADS):
        block = own_heads[head].astype(F32)
        for r in range(own):
            query_f[r, head : head + 1, :] = block[r : r + 1, :]
    for head in range(KV_HEADS):
        new_key = own_heads[HEADS + head].astype(F32)
        new_value = own_heads[HEADS + KV_HEADS + head].astype(F32)
        for r in range(own):
            for i in range(2):
                spot = 2 * head + i
                key_f[r, spot : spot + 1, :] = new_key[r : r + 1, :]
                value_f[r, spot : spot + 1, :] = new_value[r : r + 1, :]
    loads[3].wait()
    loads[4].wait()
    tail_at = lax.broadcasted_iota(jnp.int32, (HEADS, tail_keys_ref.shape[1]), 1).astype(F32)
    head_of_row = lax.broadcasted_iota(jnp.int32, (HEADS, HEAD_DIM), 0) // 2
    for r in range(own):
        query = query_f[r]
        spread = jnp.concatenate(
            [jnp.where(head_of_row == k, query, 0.0) for k in range(KV_HEADS)], axis=1
        ).astype(BF16)
        scores = lax.dot_general(
            spread, tail_keys_ref[r], (((1,), (1,)), ((), ())), preferred_element_type=F32
        )
        length = jnp.sum(
            jnp.where(along[0:1, :] == me * own + r, tail_row, 0.0), axis=-1, keepdims=True
        )
        expo = jnp.where(tail_at < length, capped_exp(scores), 0.0)
        every = jnp.dot(expo.astype(BF16), tail_values_ref[r], preferred_element_type=F32)
        num = jnp.zeros((HEADS, HEAD_DIM), F32)
        for k in range(KV_HEADS):
            num = jnp.where(head_of_row == k, every[:, k * HEAD_DIM : (k + 1) * HEAD_DIM], num)
        self_exp = capped_exp(jnp.sum(query * key_f[r], axis=-1, keepdims=True))
        num = num + self_exp.astype(BF16).astype(F32) * value_f[r]
        den = jnp.sum(expo, axis=-1, keepdims=True) + self_exp
        den = jnp.broadcast_to(den, (HEADS, 128))
        for head in range(HEADS):
            own_f[head, r : r + 1, :HEAD_DIM] = num[head : head + 1, :]
            own_f[head, r : r + 1, HEAD_DIM:] = den[head : head + 1, :]
    lane = lax.broadcasted_iota(jnp.int32, (own, 128), 1)
    for head in range(HEADS):
        den = own_f[head, :, HEAD_DIM:]
        high = den.astype(BF16).astype(F32)
        words = jnp.where(lane == 0, high, jnp.where(lane == 1, den - high, 0.0)).astype(BF16)
        for i in range(2):
            own_out[2 * head + i, :, :128] = own_f[head, :, i * 128 : (i + 1) * 128].astype(BF16)
            own_out[2 * head + i, :, 128:] = words

    def column_copy(step):
        peer = lax.rem(me + step, n)
        return remote(
            own_out.at[peer], mine_ref.at[me], own_send.at[step], own_recv.at[step], "tp", peer
        )

    for step in range(1, n):
        column_copy(step).start()
    mine_ref[me] = own_out[me]

    for i in range(2):
        for head in range(KV_HEADS):

            @pl.when(kv_server(head) == me)
            def _():
                kv_local(i, head).wait()

        for slot in range(KV_HEADS):

            @pl.when(kv_source(slot) != me)
            def _():
                kv_arrival(i, slot).wait_recv()

    for step in PLANE_STEPS:
        z_copy(0, step).wait_recv()
    for step in PLANE_STEPS:
        limit_copy(step).wait_recv()
    at = lax.broadcasted_iota(jnp.int32, (1, KV_HEADS * piece), 1)
    block = at // piece
    pair_of, mate = block // 2, lax.rem(block, 2)
    device = jnp.where(core == 0, (x * 4 + pair_of) * 2 + mate, (pair_of * 4 + y) * 2 + mate)
    spot = (device * piece + lax.rem(at, piece)).astype(F32)
    many = planes * SLOTS // 2
    lanes = lax.broadcasted_iota(jnp.int32, (many, 128), 1)
    for j in range(2):
        part = slice(j * many, (j + 1) * many)
        limits = limit_ref[part, :].astype(F32)
        begin = limits[:, 0:1] * 64 + limits[:, 1:2]
        end = limits[:, 2:3] * 64 + limits[:, 3:4]
        visible = (spot >= begin) & (spot < end)
        words = jnp.zeros((many, 128), F32)
        for i in range(2):
            span = slice(i * HEAD_DIM, (i + 1) * HEAD_DIM)
            scores = lax.dot_general(
                guest_ref[part, span],
                key_blocks[...],
                (((1,), (1,)), ((), ())),
                preferred_element_type=F32,
            )
            expo = jnp.where(visible, capped_exp(scores), 0.0)
            num = jnp.dot(expo.astype(BF16), value_blocks[...], preferred_element_type=F32)
            reply_ref[part, span] = num.astype(BF16)
            den = jnp.sum(expo, axis=-1, keepdims=True)
            high = den.astype(BF16).astype(F32)
            words = jnp.where(lanes == 2 * i, high, words)
            words = jnp.where(lanes == 2 * i + 1, den - high, words)
        reply_ref[part, 2 * HEAD_DIM :] = words.astype(BF16)
    for step in PLANE_STEPS:
        z_copy(1, step).start()
    answer_ref[here, :] = reply_ref[here, :]
    for step in PLANE_STEPS:
        z_copy(1, step).wait_recv()

    back = jnp.dot(pick_t, answer_ref[...], preferred_element_type=F32).astype(BF16)
    for i in range(4):
        parts_ref[i] = back[:, i * 128 : (i + 1) * 128]
    word_ref[...] = turned(unit[:16, :], back[:, 2 * HEAD_DIM :]).astype(BF16)

    def join_copy(i):
        return remote(
            parts_ref.at[i],
            sums_ref.at[quarter],
            jn_send.at[i],
            jn_recv.at[quarter],
            "tp",
            4 * served + i,
        )

    def word_copy(i):
        return remote(
            word_ref,
            words_ref.at[quarter],
            wd_send.at[i],
            wd_recv.at[quarter],
            "tp",
            4 * served + i,
        )

    for i in range(4):

        @pl.when(4 * served + i != me)
        def _():
            join_copy(i).start()
            word_copy(i).start()

        @pl.when(4 * served + i == me)
        def _():
            sums_ref[quarter] = parts_ref[i]
            words_ref[quarter] = word_ref[...]

    for step in range(1, n):
        column_copy(step).wait_recv()
    for p in range(n // 2):
        mine_f[2 * own * p : 2 * own * (p + 1), :] = jnp.concatenate(
            [mine_ref[2 * p].astype(F32), mine_ref[2 * p + 1].astype(F32)], axis=0
        )
    for m in range(4):

        @pl.when(server_of(me // 4, m) != me)
        def _():
            remote(
                parts_ref.at[0],
                sums_ref.at[m],
                jn_send.at[0],
                jn_recv.at[m],
                "tp",
                server_of(me // 4, m),
            ).wait_recv()
            remote(
                word_ref,
                words_ref.at[m],
                wd_send.at[0],
                wd_recv.at[m],
                "tp",
                server_of(me // 4, m),
            ).wait_recv()

    num = mine_f[:, :128]
    den = mine_f[:, 128:129] + mine_f[:, 129:130]
    for m in range(4):
        num = num + sums_ref[m].astype(F32)
        words = turned(unit, words_ref[m])
        which = lax.broadcasted_iota(jnp.int32, words.shape, 1)
        words = jnp.where(which // 2 == lax.rem(me, 4) // 2, words, 0.0)
        den = den + jnp.sum(words, axis=-1, keepdims=True)
    attn = (num / den).astype(BF16)

    loads[5].wait()
    project(0, attn, w_out_ref)
    attn_proj = reduce_scatter(0)
    resid = hidden_ref[...].astype(F32) + rms_scale(attn_proj, gains_ref[1:2, :])
    resid = resid.astype(BF16).astype(F32)
    slab_ref[1] = rms_scale(resid, gains_ref[2:3, :]).astype(BF16)
    gather_start(1)
    gather_finish(1)
    loads[6].wait()
    loads[7].wait()
    gate = jnp.dot(rows_ref[...], w_gate_up_ref[0], preferred_element_type=F32)
    up = jnp.dot(rows_ref[...], w_gate_up_ref[1], preferred_element_type=F32)
    bent = jnp.tanh(math.sqrt(2.0 / math.pi) * (gate + 0.044715 * gate * gate * gate))
    hidden_units = (0.5 * gate * (1.0 + bent) * up).astype(BF16)
    project(1, hidden_units, w_down_ref)
    ffn_proj = reduce_scatter(1)
    out_ref[...] = resid + rms_scale(ffn_proj, gains_ref[3:4, :])

    for turn in range(2):
        gather_drain(turn)
        scatter_drain(turn)
        for step in PLANE_STEPS:
            z_copy(turn, step).wait_send()
    for step in PLANE_STEPS:
        limit_copy(step).wait_send()
    for i in range(2):
        for head in range(KV_HEADS):

            @pl.when(kv_server(head) != me)
            def _():
                kv_copy(i, head).wait_send()

    for m in range(4):

        @pl.when((me < HEADS) & (server_of(chip, m) != me))
        def _():
            to_server(m).wait_send()

        @pl.when(4 * served + m != me)
        def _():
            join_copy(m).wait_send()
            word_copy(m).wait_send()

    for step in range(1, n):
        owner_copy(step).wait_send()
        column_copy(step).wait_send()


def layer(n, planes, small, large):
    own, width = small[0].shape
    rows = own * n
    piece = large[4].shape[0]
    dma = pltpu.SemaphoreType.DMA

    def bf(*shape):
        return pltpu.VMEM(shape, BF16)

    def f32(*shape):
        return pltpu.VMEM(shape, F32)

    slots = planes * SLOTS
    scratch = [
        *(bf(*a.shape) for a in large),
        bf(2, own, width),
        bf(2, n, own, width),
        bf(rows, width),
        bf(KV_HEADS * piece, HEAD_DIM),
        bf(KV_HEADS * piece, HEAD_DIM),
        bf(rows, HEAD_DIM),
        bf(n, own, HEAD_DIM),
        bf(n, own, HEAD_DIM),
        bf(2, rows, HEAD_DIM),
        bf(slots, 2 * HEAD_DIM),
        bf(slots, 2 * HEAD_DIM),
        bf(slots, WIDE),
        bf(slots, WIDE),
        f32(own, HEADS, HEAD_DIM),
        f32(own, HEADS, HEAD_DIM),
        f32(own, HEADS, HEAD_DIM),
        f32(HEADS, own, HEAD_DIM + 128),
        bf(n, own, HEAD_DIM),
        bf(n, own, HEAD_DIM),
        f32(rows, HEAD_DIM),
        bf(4, rows, 128),
        bf(4, rows, 128),
        bf(2, 2, CHIPS, own, width),
        bf(2, CHIPS, own, width),
        bf(2, CHIPS, own, width),
        bf(2, CHIPS, own, width),
        bf(16, 128),
        bf(4, 16, 128),
        bf(slots, 128),
        bf(slots, 128),
        f32(8, 128),
        dma((8,)),
        dma((2, CHIPS)),
        dma((2, CHIPS)),
        dma((2, CHIPS)),
        dma((2, CHIPS)),
        dma((2, KV_HEADS)),
        dma((2, KV_HEADS)),
        dma((n,)),
        dma((n,)),
        dma((4,)),
        dma((2,)),
        dma((2, planes)),
        dma((2, planes)),
        dma((n,)),
        dma((n,)),
        dma((4,)),
        dma((4,)),
        dma((2, 4)),
        dma((2, 4)),
        dma((2, CHIPS)),
        dma((2, CHIPS)),
        dma((2,)),
        dma((4,)),
        dma((4,)),
        dma((planes,)),
        dma((planes,)),
    ]
    return pl.pallas_call(
        functools.partial(layer_kernel, n, planes),
        out_shape=jax.ShapeDtypeStruct((own, width), F32),
        in_specs=[pl.BlockSpec(memory_space=pltpu.VMEM)] * len(small)
        + [pl.BlockSpec(memory_space=pl.ANY)] * len(large),
        out_specs=pl.BlockSpec(memory_space=pltpu.VMEM),
        scratch_shapes=scratch,
        compiler_params=pltpu.CompilerParams(
            collective_id=0, has_side_effects=True, vmem_limit_bytes=60 * 1024 * 1024
        ),
        name="layer",
    )(*small, *large)


def per_device(
    n,
    planes,
    hidden_in,
    norm_gains,
    w_qkv,
    w_out,
    w_gate_up,
    w_down,
    prompt_keys,
    prompt_values,
    tail_keys,
    tail_values,
    prompt_len,
    group_home,
    req_group,
    tail_len,
):
    return layer(
        n,
        planes,
        (
            hidden_in,
            norm_gains,
            prompt_len[None],
            group_home[None],
            req_group[None],
            tail_len[None],
        ),
        (w_qkv, w_out, w_gate_up, w_down, prompt_keys, prompt_values, tail_keys, tail_values),
    ).astype(BF16)


def solution(mesh):
    in_specs = (
        P(("grp", "tp"), None),
        P(),
        P(None, "tp"),
        P("tp", None),
        P(None, None, "tp"),
        P("tp", None),
        P(("grp", "tp"), None),
        P(("grp", "tp"), None),
        P(("grp", "tp"), None, None),
        P(("grp", "tp"), None, None),
        P(),
        P(),
        P("grp"),
        P("grp"),
    )
    return jax.shard_map(
        functools.partial(per_device, mesh.shape["tp"], mesh.shape["grp"]),
        mesh=mesh,
        in_specs=in_specs,
        out_specs=P(("grp", "tp"), None),
        check_vma=False,
    )
```

```python
import functools
import math

import jax
import jax.numpy as jnp
from jax import lax
from jax.experimental import pallas as pl
from jax.experimental.pallas import tpu as pltpu
from jax.sharding import PartitionSpec as P

HEADS = 16
KV_HEADS = 8
HEAD_DIM = 256
HALF = HEAD_DIM // 2
SLOTS = 32
CHIPS = 16
NORM_EPS = 1e-06
SOFT_CAP = 50.0
WIDE = 2 * HEAD_DIM + 128
MESH = pl.DeviceIdType.MESH
F32 = jnp.float32
BF16 = jnp.bfloat16
CHIP_STEPS = (10, 6, 9, 14, 11, 5, 7, 13, 15, 2, 8, 1, 4, 3, 12)
PLANE_STEPS = (4, 3, 5, 2, 6, 1, 7)


def rms_scale(values, gain_row):
    values = values.astype(F32)
    return (
        values * lax.rsqrt(jnp.mean(values * values, axis=-1, keepdims=True) + NORM_EPS) * gain_row
    )


def capped_exp(scores):
    return jnp.exp(SOFT_CAP * jnp.tanh(scores * (HEAD_DIM ** (-0.5) / SOFT_CAP)))


def remote(src, dst, send_sem, recv_sem, axis, peer):
    return pltpu.make_async_remote_copy(
        src_ref=src,
        dst_ref=dst,
        send_sem=send_sem,
        recv_sem=recv_sem,
        device_id={axis: peer},
        device_id_type=MESH,
    )


def server_of(head, m):
    column, line = column_of(head), row_of(head)
    return jnp.where(lax.rem(head, 4) < 2, (m * 4 + column) * 2, (line * 4 + m) * 2 + 1)


def column_of(head):
    return 2 * (head % 4) + head // 4 if isinstance(head, int) else 2 * lax.rem(head, 4) + head // 4


def row_of(head):
    return 2 * (head // 4) + (head % 4 if isinstance(head, int) else lax.rem(head, 4)) - 2


def layer_kernel(
    n,
    planes,
    hidden_ref,
    gains_ref,
    prompt_len_ref,
    group_home_ref,
    req_group_ref,
    tail_len_ref,
    w_qkv_hbm,
    w_out_hbm,
    w_gate_up_hbm,
    w_down_hbm,
    keys_hbm,
    values_hbm,
    tail_keys_hbm,
    tail_values_hbm,
    out_ref,
    w_qkv_ref,
    w_out_ref,
    w_gate_up_ref,
    w_down_ref,
    keys_ref,
    values_ref,
    tail_keys_ref,
    tail_values_ref,
    slab_ref,
    slabs_ref,
    rows_ref,
    key_blocks,
    value_blocks,
    head_ref,
    head_slabs,
    own_heads,
    pair_ref,
    visit_ref,
    guest_ref,
    reply_ref,
    answer_ref,
    query_f,
    key_f,
    value_f,
    own_f,
    own_out,
    mine_ref,
    mine_f,
    parts_ref,
    sums_ref,
    part_ref,
    half_ref,
    chip_ref,
    got_ref,
    word_ref,
    words_ref,
    bound_ref,
    limit_ref,
    table_ref,
    load_sem,
    ag_send,
    ag_recv,
    fw_send,
    fw_recv,
    kv_send,
    kv_recv,
    sp_send,
    sp_recv,
    pr_send,
    pr_recv,
    z_send,
    z_recv,
    own_send,
    own_recv,
    jn_send,
    jn_recv,
    hf_send,
    hf_recv,
    rs_send,
    rs_recv,
    self_sem,
    wd_send,
    wd_recv,
    lm_send,
    lm_recv,
):
    me = lax.axis_index("tp")
    plane = lax.axis_index("grp")
    chip, core = me // 2, lax.rem(me, 2)
    x, y = chip // 4, lax.rem(chip, 4)
    partner = chip * 2 + 1 - core
    served = jnp.where(core == 0, y // 2 + 4 * lax.rem(y, 2), 2 + lax.rem(x, 2) + 4 * (x // 2))
    quarter = jnp.where(core == 0, x, y)
    own, width = hidden_ref.shape
    rows = own * n

    loads = [
        pltpu.make_async_copy(src, dst, load_sem.at[i])
        for i, (src, dst) in enumerate(
            (
                (keys_hbm, keys_ref),
                (values_hbm, values_ref),
                (w_qkv_hbm, w_qkv_ref),
                (tail_keys_hbm, tail_keys_ref),
                (tail_values_hbm, tail_values_ref),
                (w_out_hbm, w_out_ref),
                (w_gate_up_hbm, w_gate_up_ref),
                (w_down_hbm, w_down_ref),
            )
        )
    ]
    for load in loads:
        load.start()

    barrier = pltpu.get_barrier_semaphore()
    for step in range(1, n):
        pl.semaphore_signal(
            barrier, inc=1, device_id={"tp": lax.rem(me + step, n)}, device_id_type=MESH
        )
    for step in range(1, planes):
        pl.semaphore_signal(
            barrier, inc=1, device_id={"grp": lax.rem(plane + step, planes)}, device_id_type=MESH
        )
    slab_ref[0] = rms_scale(hidden_ref[...], gains_ref[0:1, :]).astype(BF16)
    pl.semaphore_wait(barrier, n - 1 + planes - 1)

    def chip_at(step):
        return lax.rem(x + step // 4, 4) * 4 + lax.rem(y + step % 4, 4)

    def chip_from(step):
        return lax.rem(x + 4 - step // 4, 4) * 4 + lax.rem(y + 4 - step % 4, 4)

    def at_chip(step):
        return chip_at(step) * 2 + core

    def from_chip(step):
        return chip_from(step) * 2 + core

    def gather_copy(turn, step):
        return remote(
            slab_ref.at[turn],
            slabs_ref.at[turn, me],
            ag_send.at[turn, step],
            ag_recv.at[turn, step],
            "tp",
            at_chip(step),
        )

    def forward_copy(turn, step):
        source = from_chip(step)
        return remote(
            slab_ref.at[turn] if step == 0 else slabs_ref.at[turn, source],
            slabs_ref.at[turn, source],
            fw_send.at[turn, step],
            fw_recv.at[turn, step],
            "tp",
            partner,
        )

    def gather_start(turn):
        for step in CHIP_STEPS:
            gather_copy(turn, step).start()
        forward_copy(turn, 0).start()
        slabs_ref[turn, me] = slab_ref[turn]

    def gather_finish(turn):
        for step in CHIP_STEPS:
            gather_copy(turn, step).wait_recv()
            forward_copy(turn, step).start()
        for step in (0, *CHIP_STEPS):
            forward_copy(turn, step).wait_recv()
        for group in range(rows // 16):
            four = [slabs_ref[turn, group * 4 + i].astype(F32) for i in range(4)]
            rows_ref[group * 16 : group * 16 + 16, :] = jnp.concatenate(four, axis=0).astype(BF16)

    def gather_drain(turn):
        for step in CHIP_STEPS:
            gather_copy(turn, step).wait_send()
        for step in (0, *CHIP_STEPS):
            forward_copy(turn, step).wait_send()

    middle = width // 2

    def half_copy(turn, side):
        span = slice(side * middle, (side + 1) * middle)
        return remote(
            part_ref.at[turn, 1 - core, :, :, span],
            half_ref.at[turn, :, :, span],
            hf_send.at[turn, side],
            hf_recv.at[turn, side],
            "tp",
            partner,
        )

    def scatter_copy(turn, side, step):
        span = slice(side * middle, (side + 1) * middle)
        return remote(
            chip_ref.at[turn, chip_at(step), :, span],
            got_ref.at[turn, chip, :, span],
            rs_send.at[turn, side, step],
            rs_recv.at[turn, side, step],
            "tp",
            at_chip(step),
        )

    def project(turn, left, weight_ref):
        piece = middle // 2
        for side in range(2):

            def chunk(j, carry):
                columns = pl.ds(pl.multiple_of((2 * side + j) * piece, 128), piece)
                block = jnp.dot(left, weight_ref[:, columns], preferred_element_type=F32)
                for d in range(n):
                    part_ref[turn, d % 2, d // 2, :, columns] = block[own * d : own * d + own, :].astype(BF16)
                return carry

            lax.fori_loop(0, 2, chunk, 0)
            half_copy(turn, side).start()

    def reduce_scatter(turn):
        for side in range(2):
            span = slice(side * middle, (side + 1) * middle)
            half_copy(turn, side).wait_recv()
            for step in (*CHIP_STEPS, 0):
                target = chip_at(step)
                both = part_ref[turn, core, target, :, span].astype(F32)
                both = both + half_ref[turn, target, :, span].astype(F32)
                chip_ref[turn, target, :, span] = both.astype(BF16)
                if step:
                    scatter_copy(turn, side, step).start()
        total = chip_ref[turn, chip].astype(F32)
        for step in CHIP_STEPS:
            scatter_copy(turn, 0, step).wait_recv()
            scatter_copy(turn, 1, step).wait_recv()
            total = total + got_ref[turn, chip_from(step)].astype(F32)
        return total

    def scatter_drain(turn):
        for side in range(2):
            half_copy(turn, side).wait_send()
            for step in CHIP_STEPS:
                scatter_copy(turn, side, step).wait_send()

    gather_start(0)

    table_ref[...] = jnp.full((8, 128), -1.0, F32)
    groups = prompt_len_ref.shape[1]
    table_ref[0:1, :groups] = prompt_len_ref[...].astype(F32)
    table_ref[1:2, :groups] = group_home_ref[...].astype(F32)
    table_ref[2:3, :] = req_group_ref[...].astype(F32)
    table_ref[3:4, :] = tail_len_ref[...].astype(F32)
    len_row, home_row = table_ref[0:1, :], table_ref[1:2, :]
    tail_row = table_ref[3:4, :]
    down = lax.broadcasted_iota(jnp.int32, (128, 128), 0)
    along = lax.broadcasted_iota(jnp.int32, (128, 128), 1)
    unit = (down == along).astype(BF16)
    line = lax.broadcasted_iota(jnp.int32, (8, 128), 0)

    def stacked(*lines):
        total = jnp.zeros((8, 128), F32)
        for i, value in enumerate(lines):
            total = jnp.where(line == i, value, total)
        return total.astype(BF16)

    def split(value):
        high = jnp.floor(value * (1 / 64))
        return high, value - 64 * high

    def turned(left, right):
        return lax.dot_general(left, right, (((1,), (1,)), ((), ())), preferred_element_type=F32)

    columns = turned(unit, stacked(*split(len_row), home_row, table_ref[2:3, :], tail_row))
    len_column = columns[:, 0:1] * 64 + columns[:, 1:2]
    earlier = (columns[:, 2:3] == home_row) & (down < along)
    start_row = jnp.sum(jnp.where(earlier, len_column, 0.0), axis=0, keepdims=True)
    of_group = stacked(*split(len_row), home_row, *split(start_row))
    chosen = (columns[:, 3:4] == along.astype(F32)).astype(BF16)
    req = turned(chosen, of_group)
    req_row = turned(of_group, chosen)
    req_len = req[:, 0:1] * 64 + req[:, 1:2]
    req_stop = req[:, 3:4] * 64 + req[:, 4:5] + req_len
    same = req[:, 2:3] == req_row[2:3, :]
    rank = jnp.sum(jnp.where(same & (along < down), 1.0, 0.0), axis=1, keepdims=True)
    rank_row = jnp.sum(jnp.where(same & (down < along), 1.0, 0.0), axis=0, keepdims=True)
    slots = planes * SLOTS
    slot_down = lax.broadcasted_iota(jnp.int32, (slots, rows), 0).astype(F32)
    slot_along = lax.broadcasted_iota(jnp.int32, (rows, slots), 1).astype(F32)
    pick = (slot_down == req_row[2:3, :] * SLOTS + rank_row).astype(BF16)
    pick_t = (slot_along == req[:, 2:3] * SLOTS + rank).astype(BF16)
    bounds = jnp.zeros((rows, 128), F32)
    for i, value in enumerate((req[:, 3:4], req[:, 4:5], *split(req_stop))):
        bounds = jnp.where(along == i, value, bounds)
    bound_ref[...] = jnp.dot(pick, bounds.astype(BF16), preferred_element_type=F32).astype(BF16)

    def limit_copy(step):
        peer = lax.rem(plane + step, planes)
        return remote(
            bound_ref.at[pl.ds(peer * SLOTS, SLOTS)],
            limit_ref.at[pl.ds(plane * SLOTS, SLOTS)],
            lm_send.at[step],
            lm_recv.at[step],
            "grp",
            peer,
        )

    here = pl.ds(pl.multiple_of(plane * SLOTS, SLOTS), SLOTS)
    for step in PLANE_STEPS:
        limit_copy(step).start()
    limit_ref[here, :] = bound_ref[here, :]
    frequency = jnp.exp(along[0:1, :].astype(F32) * (-math.log(10000.0) / HALF))
    angles = (req_len + columns[:, 4:5]) * frequency
    cosine, sine = jnp.cos(angles), jnp.sin(angles)

    def kv_server(head):
        if head % 4 < 2:
            return (x * 4 + column_of(head)) * 2
        return (row_of(head) * 4 + y) * 2 + 1

    def kv_source(slot):
        mate = lax.rem(slot, 2)
        return jnp.where(core == 0, (x * 4 + slot // 2) * 2 + mate, (slot // 2 * 4 + y) * 2 + mate)

    pieces = ((keys_ref, key_blocks), (values_ref, value_blocks))
    piece = keys_ref.shape[0]

    def kv_copy(i, head):
        slot = (y if head % 4 < 2 else x) * 2 + core
        return remote(
            pieces[i][0].at[:, head * HEAD_DIM : (head + 1) * HEAD_DIM],
            pieces[i][1].at[pl.ds(slot * piece, piece)],
            kv_send.at[i, head],
            kv_recv.at[i, slot],
            "tp",
            kv_server(head),
        )

    def kv_local(i, head):
        slot = (y if head % 4 < 2 else x) * 2 + core
        return pltpu.make_async_copy(
            pieces[i][0].at[:, head * HEAD_DIM : (head + 1) * HEAD_DIM],
            pieces[i][1].at[pl.ds(slot * piece, piece)],
            self_sem.at[i],
        )

    def kv_arrival(i, slot):
        return remote(
            pieces[i][0].at[:, :HEAD_DIM],
            pieces[i][1].at[slot * piece : (slot + 1) * piece],
            kv_send.at[i, 0],
            kv_recv.at[i, slot],
            "tp",
            kv_source(slot),
        )

    gather_finish(0)
    loads[2].wait()
    head_rows = jnp.dot(rows_ref[...], w_qkv_ref[...], preferred_element_type=F32)
    head_rows = head_rows.astype(BF16).astype(F32)
    first, second = head_rows[:, :HALF], head_rows[:, HALF:]
    rotated = jnp.concatenate(
        [first * cosine - second * sine, second * cosine + first * sine], axis=-1
    )
    head_rows = jnp.where(me < HEADS + KV_HEADS, rotated, head_rows)
    head_ref[...] = head_rows.astype(BF16)

    index = lax.rem(me, 2)

    def to_server(m):
        return remote(
            head_ref,
            pair_ref.at[index],
            pr_send.at[m],
            pr_recv.at[index],
            "tp",
            server_of(chip, m),
        )

    for m in range(4):

        @pl.when((me < HEADS) & (server_of(chip, m) != me))
        def _():
            to_server(m).start()

    for d in range(n):
        head_slabs[d] = head_rows[own * d : own * d + own, :].astype(BF16)

    def owner_copy(step):
        peer = lax.rem(me + step, n)
        return remote(
            head_slabs.at[peer], own_heads.at[me], sp_send.at[step], sp_recv.at[step], "tp", peer
        )

    for step in range(1, n):
        owner_copy(step).start()
    own_heads[me] = head_slabs[me]

    for i in range(2):
        loads[i].wait()
        for head in range(KV_HEADS):

            @pl.when(kv_server(head) != me)
            def _():
                kv_copy(i, head).start()

            @pl.when(kv_server(head) == me)
            def _():
                kv_local(i, head).start()

    for i in range(2):

        @pl.when(2 * served + i == me)
        def _():
            pair_ref[i] = head_ref[...]

        @pl.when(2 * served + i != me)
        def _():
            remote(
                head_ref, pair_ref.at[i], pr_send.at[0], pr_recv.at[i], "tp", 2 * served + i
            ).wait_recv()

    for i in range(2):
        chosen = jnp.dot(pick, pair_ref[i], preferred_element_type=F32)
        visit_ref[:, i * HEAD_DIM : (i + 1) * HEAD_DIM] = chosen.astype(BF16)

    def z_copy(turn, step):
        peer = lax.rem(plane + step, planes)
        src, dst = ((visit_ref, guest_ref), (reply_ref, answer_ref))[turn]
        return remote(
            src.at[pl.ds(peer * SLOTS, SLOTS)],
            dst.at[pl.ds(plane * SLOTS, SLOTS)],
            z_send.at[turn, step],
            z_recv.at[turn, step],
            "grp",
            peer,
        )

    for step in PLANE_STEPS:
        z_copy(0, step).start()
    guest_ref[here, :] = visit_ref[here, :]

    for step in range(1, n):
        owner_copy(step).wait_recv()
    for head in range(HEADS):
        block = own_heads[head].astype(F32)
        for r in range(own):
            query_f[r, head : head + 1, :] = block[r : r + 1, :]
    for head in range(KV_HEADS):
        new_key = own_heads[HEADS + head].astype(F32)
        new_value = own_heads[HEADS + KV_HEADS + head].astype(F32)
        for r in range(own):
            for i in range(2):
                spot = 2 * head + i
                key_f[r, spot : spot + 1, :] = new_key[r : r + 1, :]
                value_f[r, spot : spot + 1, :] = new_value[r : r + 1, :]
    loads[3].wait()
    loads[4].wait()
    tail_at = lax.broadcasted_iota(jnp.int32, (HEADS, tail_keys_ref.shape[1]), 1).astype(F32)
    head_of_row = lax.broadcasted_iota(jnp.int32, (HEADS, HEAD_DIM), 0) // 2
    for r in range(own):
        query = query_f[r]
        spread = jnp.concatenate(
            [jnp.where(head_of_row == k, query, 0.0) for k in range(KV_HEADS)], axis=1
        ).astype(BF16)
        scores = lax.dot_general(
            spread, tail_keys_ref[r], (((1,), (1,)), ((), ())), preferred_element_type=F32
        )
        length = jnp.sum(
            jnp.where(along[0:1, :] == me * own + r, tail_row, 0.0), axis=-1, keepdims=True
        )
        expo = jnp.where(tail_at < length, capped_exp(scores), 0.0)
        every = jnp.dot(expo.astype(BF16), tail_values_ref[r], preferred_element_type=F32)
        num = jnp.zeros((HEADS, HEAD_DIM), F32)
        for k in range(KV_HEADS):
            num = jnp.where(head_of_row == k, every[:, k * HEAD_DIM : (k + 1) * HEAD_DIM], num)
        self_exp = capped_exp(jnp.sum(query * key_f[r], axis=-1, keepdims=True))
        num = num + self_exp.astype(BF16).astype(F32) * value_f[r]
        den = jnp.sum(expo, axis=-1, keepdims=True) + self_exp
        den = jnp.broadcast_to(den, (HEADS, 128))
        for head in range(HEADS):
            own_f[head, r : r + 1, :HEAD_DIM] = num[head : head + 1, :]
            own_f[head, r : r + 1, HEAD_DIM:] = den[head : head + 1, :]
    lane = lax.broadcasted_iota(jnp.int32, (own, 128), 1)
    for head in range(HEADS):
        den = own_f[head, :, HEAD_DIM:]
        high = den.astype(BF16).astype(F32)
        words = jnp.where(lane == 0, high, jnp.where(lane == 1, den - high, 0.0)).astype(BF16)
        for i in range(2):
            own_out[2 * head + i, :, :128] = own_f[head, :, i * 128 : (i + 1) * 128].astype(BF16)
            own_out[2 * head + i, :, 128:] = words

    def column_copy(step):
        peer = lax.rem(me + step, n)
        return remote(
            own_out.at[peer], mine_ref.at[me], own_send.at[step], own_recv.at[step], "tp", peer
        )

    for step in range(1, n):
        column_copy(step).start()
    mine_ref[me] = own_out[me]

    for i in range(2):
        for head in range(KV_HEADS):

            @pl.when(kv_server(head) == me)
            def _():
                kv_local(i, head).wait()

        for slot in range(KV_HEADS):

            @pl.when(kv_source(slot) != me)
            def _():
                kv_arrival(i, slot).wait_recv()

    for step in PLANE_STEPS:
        z_copy(0, step).wait_recv()
    for step in PLANE_STEPS:
        limit_copy(step).wait_recv()
    at = lax.broadcasted_iota(jnp.int32, (1, KV_HEADS * piece), 1)
    block = at // piece
    pair_of, mate = block // 2, lax.rem(block, 2)
    device = jnp.where(core == 0, (x * 4 + pair_of) * 2 + mate, (pair_of * 4 + y) * 2 + mate)
    spot = (device * piece + lax.rem(at, piece)).astype(F32)
    many = planes * SLOTS // 2
    lanes = lax.broadcasted_iota(jnp.int32, (many, 128), 1)
    for j in range(2):
        part = slice(j * many, (j + 1) * many)
        limits = limit_ref[part, :].astype(F32)
        begin = limits[:, 0:1] * 64 + limits[:, 1:2]
        end = limits[:, 2:3] * 64 + limits[:, 3:4]
        visible = (spot >= begin) & (spot < end)
        words = jnp.zeros((many, 128), F32)
        for i in range(2):
            span = slice(i * HEAD_DIM, (i + 1) * HEAD_DIM)
            scores = lax.dot_general(
                guest_ref[part, span],
                key_blocks[...],
                (((1,), (1,)), ((), ())),
                preferred_element_type=F32,
            )
            expo = jnp.where(visible, capped_exp(scores), 0.0)
            num = jnp.dot(expo.astype(BF16), value_blocks[...], preferred_element_type=F32)
            reply_ref[part, span] = num.astype(BF16)
            den = jnp.sum(expo, axis=-1, keepdims=True)
            high = den.astype(BF16).astype(F32)
            words = jnp.where(lanes == 2 * i, high, words)
            words = jnp.where(lanes == 2 * i + 1, den - high, words)
        reply_ref[part, 2 * HEAD_DIM :] = words.astype(BF16)
    for step in PLANE_STEPS:
        z_copy(1, step).start()
    answer_ref[here, :] = reply_ref[here, :]
    for step in PLANE_STEPS:
        z_copy(1, step).wait_recv()

    back = jnp.dot(pick_t, answer_ref[...], preferred_element_type=F32).astype(BF16)
    for i in range(4):
        parts_ref[i] = back[:, i * 128 : (i + 1) * 128]
    word_ref[...] = turned(unit[:16, :], back[:, 2 * HEAD_DIM :]).astype(BF16)

    def join_copy(i):
        return remote(
            parts_ref.at[i],
            sums_ref.at[quarter],
            jn_send.at[i],
            jn_recv.at[quarter],
            "tp",
            4 * served + i,
        )

    def word_copy(i):
        return remote(
            word_ref,
            words_ref.at[quarter],
            wd_send.at[i],
            wd_recv.at[quarter],
            "tp",
            4 * served + i,
        )

    for i in range(4):

        @pl.when(4 * served + i != me)
        def _():
            join_copy(i).start()
            word_copy(i).start()

        @pl.when(4 * served + i == me)
        def _():
            sums_ref[quarter] = parts_ref[i]
            words_ref[quarter] = word_ref[...]

    for step in range(1, n):
        column_copy(step).wait_recv()
    for p in range(n // 2):
        mine_f[2 * own * p : 2 * own * (p + 1), :] = jnp.concatenate(
            [mine_ref[2 * p].astype(F32), mine_ref[2 * p + 1].astype(F32)], axis=0
        )
    for m in range(4):

        @pl.when(server_of(me // 4, m) != me)
        def _():
            remote(
                parts_ref.at[0],
                sums_ref.at[m],
                jn_send.at[0],
                jn_recv.at[m],
                "tp",
                server_of(me // 4, m),
            ).wait_recv()
            remote(
                word_ref,
                words_ref.at[m],
                wd_send.at[0],
                wd_recv.at[m],
                "tp",
                server_of(me // 4, m),
            ).wait_recv()

    num = mine_f[:, :128]
    den = mine_f[:, 128:129] + mine_f[:, 129:130]
    for m in range(4):
        num = num + sums_ref[m].astype(F32)
        words = turned(unit, words_ref[m])
        which = lax.broadcasted_iota(jnp.int32, words.shape, 1)
        words = jnp.where(which // 2 == lax.rem(me, 4) // 2, words, 0.0)
        den = den + jnp.sum(words, axis=-1, keepdims=True)
    attn = (num / den).astype(BF16)

    loads[5].wait()
    project(0, attn, w_out_ref)
    attn_proj = reduce_scatter(0)
    resid = hidden_ref[...].astype(F32) + rms_scale(attn_proj, gains_ref[1:2, :])
    resid = resid.astype(BF16).astype(F32)
    slab_ref[1] = rms_scale(resid, gains_ref[2:3, :]).astype(BF16)
    gather_start(1)
    gather_finish(1)
    loads[6].wait()
    loads[7].wait()
    gate = jnp.dot(rows_ref[...], w_gate_up_ref[0], preferred_element_type=F32)
    up = jnp.dot(rows_ref[...], w_gate_up_ref[1], preferred_element_type=F32)
    bent = jnp.tanh(math.sqrt(2.0 / math.pi) * (gate + 0.044715 * gate * gate * gate))
    hidden_units = (0.5 * gate * (1.0 + bent) * up).astype(BF16)
    project(1, hidden_units, w_down_ref)
    ffn_proj = reduce_scatter(1)
    out_ref[...] = resid + rms_scale(ffn_proj, gains_ref[3:4, :])

    for turn in range(2):
        gather_drain(turn)
        scatter_drain(turn)
        for step in PLANE_STEPS:
            z_copy(turn, step).wait_send()
    for step in PLANE_STEPS:
        limit_copy(step).wait_send()
    for i in range(2):
        for head in range(KV_HEADS):

            @pl.when(kv_server(head) != me)
            def _():
                kv_copy(i, head).wait_send()

    for m in range(4):

        @pl.when((me < HEADS) & (server_of(chip, m) != me))
        def _():
            to_server(m).wait_send()

        @pl.when(4 * served + m != me)
        def _():
            join_copy(m).wait_send()
            word_copy(m).wait_send()

    for step in range(1, n):
        owner_copy(step).wait_send()
        column_copy(step).wait_send()


def layer(n, planes, small, large):
    own, width = small[0].shape
    rows = own * n
    piece = large[4].shape[0]
    dma = pltpu.SemaphoreType.DMA

    def bf(*shape):
        return pltpu.VMEM(shape, BF16)

    def f32(*shape):
        return pltpu.VMEM(shape, F32)

    slots = planes * SLOTS
    scratch = [
        *(bf(*a.shape) for a in large),
        bf(2, own, width),
        bf(2, n, own, width),
        bf(rows, width),
        bf(KV_HEADS * piece, HEAD_DIM),
        bf(KV_HEADS * piece, HEAD_DIM),
        bf(rows, HEAD_DIM),
        bf(n, own, HEAD_DIM),
        bf(n, own, HEAD_DIM),
        bf(2, rows, HEAD_DIM),
        bf(slots, 2 * HEAD_DIM),
        bf(slots, 2 * HEAD_DIM),
        bf(slots, WIDE),
        bf(slots, WIDE),
        f32(own, HEADS, HEAD_DIM),
        f32(own, HEADS, HEAD_DIM),
        f32(own, HEADS, HEAD_DIM),
        f32(HEADS, own, HEAD_DIM + 128),
        bf(n, own, HEAD_DIM),
        bf(n, own, HEAD_DIM),
        f32(rows, HEAD_DIM),
        bf(4, rows, 128),
        bf(4, rows, 128),
        bf(2, 2, CHIPS, own, width),
        bf(2, CHIPS, own, width),
        bf(2, CHIPS, own, width),
        bf(2, CHIPS, own, width),
        bf(16, 128),
        bf(4, 16, 128),
        bf(slots, 128),
        bf(slots, 128),
        f32(8, 128),
        dma((8,)),
        dma((2, CHIPS)),
        dma((2, CHIPS)),
        dma((2, CHIPS)),
        dma((2, CHIPS)),
        dma((2, KV_HEADS)),
        dma((2, KV_HEADS)),
        dma((n,)),
        dma((n,)),
        dma((4,)),
        dma((2,)),
        dma((2, planes)),
        dma((2, planes)),
        dma((n,)),
        dma((n,)),
        dma((4,)),
        dma((4,)),
        dma((2, 2)),
        dma((2, 2)),
        dma((2, 2, CHIPS)),
        dma((2, 2, CHIPS)),
        dma((2,)),
        dma((4,)),
        dma((4,)),
        dma((planes,)),
        dma((planes,)),
    ]
    return pl.pallas_call(
        functools.partial(layer_kernel, n, planes),
        out_shape=jax.ShapeDtypeStruct((own, width), F32),
        in_specs=[pl.BlockSpec(memory_space=pltpu.VMEM)] * len(small)
        + [pl.BlockSpec(memory_space=pl.ANY)] * len(large),
        out_specs=pl.BlockSpec(memory_space=pltpu.VMEM),
        scratch_shapes=scratch,
        compiler_params=pltpu.CompilerParams(
            collective_id=0, has_side_effects=True, vmem_limit_bytes=60 * 1024 * 1024
        ),
        name="layer",
    )(*small, *large)


def per_device(
    n,
    planes,
    hidden_in,
    norm_gains,
    w_qkv,
    w_out,
    w_gate_up,
    w_down,
    prompt_keys,
    prompt_values,
    tail_keys,
    tail_values,
    prompt_len,
    group_home,
    req_group,
    tail_len,
):
    return layer(
        n,
        planes,
        (
            hidden_in,
            norm_gains,
            prompt_len[None],
            group_home[None],
            req_group[None],
            tail_len[None],
        ),
        (w_qkv, w_out, w_gate_up, w_down, prompt_keys, prompt_values, tail_keys, tail_values),
    ).astype(BF16)


def solution(mesh):
    in_specs = (
        P(("grp", "tp"), None),
        P(),
        P(None, "tp"),
        P("tp", None),
        P(None, None, "tp"),
        P("tp", None),
        P(("grp", "tp"), None),
        P(("grp", "tp"), None),
        P(("grp", "tp"), None, None),
        P(("grp", "tp"), None, None),
        P(),
        P(),
        P("grp"),
        P("grp"),
    )
    return jax.shard_map(
        functools.partial(per_device, mesh.shape["tp"], mesh.shape["grp"]),
        mesh=mesh,
        in_specs=in_specs,
        out_specs=P(("grp", "tp"), None),
        check_vma=False,
    )
```

```python
import functools
import math

import jax
import jax.numpy as jnp
from jax import lax
from jax.experimental import pallas as pl
from jax.experimental.pallas import tpu as pltpu
from jax.sharding import PartitionSpec as P

HEADS = 16
KV_HEADS = 8
HEAD_DIM = 256
HALF = HEAD_DIM // 2
SLOTS = 32
CHIPS = 16
NORM_EPS = 1e-06
SOFT_CAP = 50.0
WIDE = 2 * HEAD_DIM + 128
MESH = pl.DeviceIdType.MESH
F32 = jnp.float32
BF16 = jnp.bfloat16
DIRECT_STEPS = (14, 13, 15, 12, 6, 5, 7, 4, 2, 1, 3)
PLANE_STEPS = (4, 3, 5, 2, 6, 1, 7)


def rms_scale(values, gain_row):
    values = values.astype(F32)
    return (
        values * lax.rsqrt(jnp.mean(values * values, axis=-1, keepdims=True) + NORM_EPS) * gain_row
    )


def capped_exp(scores):
    return jnp.exp(SOFT_CAP * jnp.tanh(scores * (HEAD_DIM ** (-0.5) / SOFT_CAP)))


def remote(src, dst, send_sem, recv_sem, axis, peer):
    return pltpu.make_async_remote_copy(
        src_ref=src,
        dst_ref=dst,
        send_sem=send_sem,
        recv_sem=recv_sem,
        device_id={axis: peer},
        device_id_type=MESH,
    )


def server_of(head, m):
    column, line = column_of(head), row_of(head)
    return jnp.where(lax.rem(head, 4) < 2, (m * 4 + column) * 2, (line * 4 + m) * 2 + 1)


def column_of(head):
    return 2 * (head % 4) + head // 4 if isinstance(head, int) else 2 * lax.rem(head, 4) + head // 4


def row_of(head):
    return 2 * (head // 4) + (head % 4 if isinstance(head, int) else lax.rem(head, 4)) - 2


def layer_kernel(
    n,
    planes,
    hidden_ref,
    gains_ref,
    prompt_len_ref,
    group_home_ref,
    req_group_ref,
    tail_len_ref,
    w_qkv_hbm,
    w_out_hbm,
    w_gate_up_hbm,
    w_down_hbm,
    keys_hbm,
    values_hbm,
    tail_keys_hbm,
    tail_values_hbm,
    out_ref,
    w_qkv_ref,
    w_out_ref,
    w_gate_up_ref,
    w_down_ref,
    keys_ref,
    values_ref,
    tail_keys_ref,
    tail_values_ref,
    slab_ref,
    slabs_ref,
    rows_ref,
    key_blocks,
    value_blocks,
    head_ref,
    head_slabs,
    own_heads,
    pair_ref,
    visit_ref,
    guest_ref,
    reply_ref,
    answer_ref,
    query_f,
    key_f,
    value_f,
    own_f,
    own_out,
    mine_ref,
    mine_f,
    parts_ref,
    sums_ref,
    part_ref,
    half_ref,
    chip_ref,
    got_ref,
    relay_ref,
    word_ref,
    words_ref,
    bound_ref,
    limit_ref,
    table_ref,
    load_sem,
    ag_send,
    ag_recv,
    fw_send,
    fw_recv,
    kv_send,
    kv_recv,
    sp_send,
    sp_recv,
    pr_send,
    pr_recv,
    z_send,
    z_recv,
    own_send,
    own_recv,
    jn_send,
    jn_recv,
    hf_send,
    hf_recv,
    rs_send,
    rs_recv,
    self_sem,
    wd_send,
    wd_recv,
    lm_send,
    lm_recv,
):
    me = lax.axis_index("tp")
    plane = lax.axis_index("grp")
    chip, core = me // 2, lax.rem(me, 2)
    x, y = chip // 4, lax.rem(chip, 4)
    partner = chip * 2 + 1 - core
    served = jnp.where(core == 0, y // 2 + 4 * lax.rem(y, 2), 2 + lax.rem(x, 2) + 4 * (x // 2))
    quarter = jnp.where(core == 0, x, y)
    own, width = hidden_ref.shape
    rows = own * n

    loads = [
        pltpu.make_async_copy(src, dst, load_sem.at[i])
        for i, (src, dst) in enumerate(
            (
                (keys_hbm, keys_ref),
                (values_hbm, values_ref),
                (w_qkv_hbm, w_qkv_ref),
                (tail_keys_hbm, tail_keys_ref),
                (tail_values_hbm, tail_values_ref),
                (w_out_hbm, w_out_ref),
                (w_gate_up_hbm, w_gate_up_ref),
                (w_down_hbm, w_down_ref),
            )
        )
    ]
    for load in loads:
        load.start()

    barrier = pltpu.get_barrier_semaphore()
    for step in range(1, n):
        pl.semaphore_signal(
            barrier, inc=1, device_id={"tp": lax.rem(me + step, n)}, device_id_type=MESH
        )
    for step in range(1, planes):
        pl.semaphore_signal(
            barrier, inc=1, device_id={"grp": lax.rem(plane + step, planes)}, device_id_type=MESH
        )
    slab_ref[0] = rms_scale(hidden_ref[...], gains_ref[0:1, :]).astype(BF16)
    pl.semaphore_wait(barrier, n - 1 + planes - 1)

    a, b = jnp.where(core == 0, x, y), jnp.where(core == 0, y, x)

    def chip_of(i, j):
        return jnp.where(core == 0, i * 4 + j, j * 4 + i)

    def chip_at(step):
        return chip_of(lax.rem(a + step // 4, 4), lax.rem(b + step % 4, 4))

    def chip_from(step):
        return chip_of(lax.rem(a + 4 - step // 4, 4), lax.rem(b + 4 - step % 4, 4))

    neighbour = chip_of(lax.rem(a + 3, 4), b) * 2 + core

    def at_chip(step):
        return chip_at(step) * 2 + core

    def from_chip(step):
        return chip_from(step) * 2 + core

    def gather_copy(turn, step):
        return remote(
            slab_ref.at[turn],
            slabs_ref.at[turn, me],
            ag_send.at[turn, step],
            ag_recv.at[turn, step],
            "tp",
            at_chip(step),
        )

    def forward_copy(turn, step):
        source = from_chip(step)
        return remote(
            slab_ref.at[turn] if step == 0 else slabs_ref.at[turn, source],
            slabs_ref.at[turn, source],
            fw_send.at[turn, step],
            fw_recv.at[turn, step],
            "tp",
            partner,
        )

    def relay_copy(turn, j):
        source = from_chip(12 + j)
        return remote(
            slabs_ref.at[turn, source],
            slabs_ref.at[turn, source],
            ag_send.at[turn, 8 + j],
            ag_recv.at[turn, 8 + j],
            "tp",
            neighbour,
        )

    def gather_start(turn):
        for step in DIRECT_STEPS:
            gather_copy(turn, step).start()
        forward_copy(turn, 0).start()
        slabs_ref[turn, me] = slab_ref[turn]

    def gather_finish(turn):
        for step in DIRECT_STEPS:
            gather_copy(turn, step).wait_recv()
            if step >= 12:
                relay_copy(turn, step - 12).start()
            forward_copy(turn, step).start()
        for j in (2, 1, 3, 0):
            gather_copy(turn, 8 + j).wait_recv()
            forward_copy(turn, 8 + j).start()
        for step in range(CHIPS):
            forward_copy(turn, step).wait_recv()
        for group in range(rows // 16):
            four = [slabs_ref[turn, group * 4 + i].astype(F32) for i in range(4)]
            rows_ref[group * 16 : group * 16 + 16, :] = jnp.concatenate(four, axis=0).astype(BF16)

    def gather_drain(turn):
        for step in DIRECT_STEPS:
            gather_copy(turn, step).wait_send()
        for j in range(4):
            relay_copy(turn, j).wait_send()
        for step in range(CHIPS):
            forward_copy(turn, step).wait_send()

    middle = width // 2

    def half_copy(turn, side):
        span = slice(side * middle, (side + 1) * middle)
        return remote(
            part_ref.at[turn, 1 - core, :, :, span],
            half_ref.at[turn, :, :, span],
            hf_send.at[turn, side],
            hf_recv.at[turn, side],
            "tp",
            partner,
        )

    def scatter_copy(turn, side, step):
        span = slice(side * middle, (side + 1) * middle)
        return remote(
            chip_ref.at[turn, chip_at(step), :, span],
            got_ref.at[turn, chip, :, span],
            rs_send.at[turn, side, step],
            rs_recv.at[turn, side, step],
            "tp",
            at_chip(step),
        )

    def project(turn, left, weight_ref):
        piece = middle // 2
        for side in range(2):

            def chunk(j, carry):
                columns = pl.ds(pl.multiple_of((2 * side + j) * piece, 128), piece)
                block = jnp.dot(left, weight_ref[:, columns], preferred_element_type=F32)
                for d in range(n):
                    part_ref[turn, d % 2, d // 2, :, columns] = block[own * d : own * d + own, :].astype(BF16)
                return carry

            lax.fori_loop(0, 2, chunk, 0)
            half_copy(turn, side).start()

    def lift_copy(turn, side, j):
        span = slice(side * middle, (side + 1) * middle)
        return remote(
            chip_ref.at[turn, chip_at(8 + j), :, span],
            relay_ref.at[turn, j, :, span],
            rs_send.at[turn, side, 8 + j],
            rs_recv.at[turn, side, 8 + j],
            "tp",
            neighbour,
        )

    def reduce_scatter(turn):
        for side in range(2):
            span = slice(side * middle, (side + 1) * middle)
            half_copy(turn, side).wait_recv()

            def both(step):
                target = chip_at(step)
                total = part_ref[turn, core, target, :, span].astype(F32)
                return target, total + half_ref[turn, target, :, span].astype(F32)

            for step in (10, 9, 11, 8, 6, 5, 7, 4, 2, 1, 3, 0):
                target, total = both(step)
                chip_ref[turn, target, :, span] = total.astype(BF16)
                if step >= 8:
                    lift_copy(turn, side, step - 8).start()
                elif step:
                    scatter_copy(turn, side, step).start()
        for side in range(2):
            span = slice(side * middle, (side + 1) * middle)
            for j in (2, 1, 3, 0):
                lift_copy(turn, side, j).wait_recv()
                target = chip_at(12 + j)
                total = part_ref[turn, core, target, :, span].astype(F32)
                total = total + half_ref[turn, target, :, span].astype(F32)
                total = total + relay_ref[turn, j, :, span].astype(F32)
                chip_ref[turn, target, :, span] = total.astype(BF16)
                scatter_copy(turn, side, 12 + j).start()
        total = chip_ref[turn, chip].astype(F32)
        for step in (6, 5, 7, 4, 2, 1, 3, 14, 13, 15, 12):
            scatter_copy(turn, 0, step).wait_recv()
            scatter_copy(turn, 1, step).wait_recv()
            total = total + got_ref[turn, chip_from(step)].astype(F32)
        return total

    def scatter_drain(turn):
        for side in range(2):
            half_copy(turn, side).wait_send()
            for step in DIRECT_STEPS:
                scatter_copy(turn, side, step).wait_send()
            for j in range(4):
                lift_copy(turn, side, j).wait_send()

    gather_start(0)

    table_ref[...] = jnp.full((8, 128), -1.0, F32)
    groups = prompt_len_ref.shape[1]
    table_ref[0:1, :groups] = prompt_len_ref[...].astype(F32)
    table_ref[1:2, :groups] = group_home_ref[...].astype(F32)
    table_ref[2:3, :] = req_group_ref[...].astype(F32)
    table_ref[3:4, :] = tail_len_ref[...].astype(F32)
    len_row, home_row = table_ref[0:1, :], table_ref[1:2, :]
    tail_row = table_ref[3:4, :]
    down = lax.broadcasted_iota(jnp.int32, (128, 128), 0)
    along = lax.broadcasted_iota(jnp.int32, (128, 128), 1)
    unit = (down == along).astype(BF16)
    line = lax.broadcasted_iota(jnp.int32, (8, 128), 0)

    def stacked(*lines):
        total = jnp.zeros((8, 128), F32)
        for i, value in enumerate(lines):
            total = jnp.where(line == i, value, total)
        return total.astype(BF16)

    def split(value):
        high = jnp.floor(value * (1 / 64))
        return high, value - 64 * high

    def turned(left, right):
        return lax.dot_general(left, right, (((1,), (1,)), ((), ())), preferred_element_type=F32)

    columns = turned(unit, stacked(*split(len_row), home_row, table_ref[2:3, :], tail_row))
    len_column = columns[:, 0:1] * 64 + columns[:, 1:2]
    earlier = (columns[:, 2:3] == home_row) & (down < along)
    start_row = jnp.sum(jnp.where(earlier, len_column, 0.0), axis=0, keepdims=True)
    of_group = stacked(*split(len_row), home_row, *split(start_row))
    chosen = (columns[:, 3:4] == along.astype(F32)).astype(BF16)
    req = turned(chosen, of_group)
    req_row = turned(of_group, chosen)
    req_len = req[:, 0:1] * 64 + req[:, 1:2]
    req_stop = req[:, 3:4] * 64 + req[:, 4:5] + req_len
    same = req[:, 2:3] == req_row[2:3, :]
    rank = jnp.sum(jnp.where(same & (along < down), 1.0, 0.0), axis=1, keepdims=True)
    rank_row = jnp.sum(jnp.where(same & (down < along), 1.0, 0.0), axis=0, keepdims=True)
    slots = planes * SLOTS
    slot_down = lax.broadcasted_iota(jnp.int32, (slots, rows), 0).astype(F32)
    slot_along = lax.broadcasted_iota(jnp.int32, (rows, slots), 1).astype(F32)
    pick = (slot_down == req_row[2:3, :] * SLOTS + rank_row).astype(BF16)
    pick_t = (slot_along == req[:, 2:3] * SLOTS + rank).astype(BF16)
    bounds = jnp.zeros((rows, 128), F32)
    for i, value in enumerate((req[:, 3:4], req[:, 4:5], *split(req_stop))):
        bounds = jnp.where(along == i, value, bounds)
    bound_ref[...] = jnp.dot(pick, bounds.astype(BF16), preferred_element_type=F32).astype(BF16)

    def limit_copy(step):
        peer = lax.rem(plane + step, planes)
        return remote(
            bound_ref.at[pl.ds(peer * SLOTS, SLOTS)],
            limit_ref.at[pl.ds(plane * SLOTS, SLOTS)],
            lm_send.at[step],
            lm_recv.at[step],
            "grp",
            peer,
        )

    here = pl.ds(pl.multiple_of(plane * SLOTS, SLOTS), SLOTS)
    for step in PLANE_STEPS:
        limit_copy(step).start()
    limit_ref[here, :] = bound_ref[here, :]
    frequency = jnp.exp(along[0:1, :].astype(F32) * (-math.log(10000.0) / HALF))
    angles = (req_len + columns[:, 4:5]) * frequency
    cosine, sine = jnp.cos(angles), jnp.sin(angles)

    def kv_server(head):
        if head % 4 < 2:
            return (x * 4 + column_of(head)) * 2
        return (row_of(head) * 4 + y) * 2 + 1

    def kv_source(slot):
        mate = lax.rem(slot, 2)
        return jnp.where(core == 0, (x * 4 + slot // 2) * 2 + mate, (slot // 2 * 4 + y) * 2 + mate)

    pieces = ((keys_ref, key_blocks), (values_ref, value_blocks))
    piece = keys_ref.shape[0]

    def kv_copy(i, head):
        slot = (y if head % 4 < 2 else x) * 2 + core
        return remote(
            pieces[i][0].at[:, head * HEAD_DIM : (head + 1) * HEAD_DIM],
            pieces[i][1].at[pl.ds(slot * piece, piece)],
            kv_send.at[i, head],
            kv_recv.at[i, slot],
            "tp",
            kv_server(head),
        )

    def kv_local(i, head):
        slot = (y if head % 4 < 2 else x) * 2 + core
        return pltpu.make_async_copy(
            pieces[i][0].at[:, head * HEAD_DIM : (head + 1) * HEAD_DIM],
            pieces[i][1].at[pl.ds(slot * piece, piece)],
            self_sem.at[i],
        )

    def kv_arrival(i, slot):
        return remote(
            pieces[i][0].at[:, :HEAD_DIM],
            pieces[i][1].at[slot * piece : (slot + 1) * piece],
            kv_send.at[i, 0],
            kv_recv.at[i, slot],
            "tp",
            kv_source(slot),
        )

    gather_finish(0)
    loads[2].wait()
    head_rows = jnp.dot(rows_ref[...], w_qkv_ref[...], preferred_element_type=F32)
    head_rows = head_rows.astype(BF16).astype(F32)
    first, second = head_rows[:, :HALF], head_rows[:, HALF:]
    rotated = jnp.concatenate(
        [first * cosine - second * sine, second * cosine + first * sine], axis=-1
    )
    head_rows = jnp.where(me < HEADS + KV_HEADS, rotated, head_rows)
    head_ref[...] = head_rows.astype(BF16)

    index = lax.rem(me, 2)

    def to_server(m):
        return remote(
            head_ref,
            pair_ref.at[index],
            pr_send.at[m],
            pr_recv.at[index],
            "tp",
            server_of(chip, m),
        )

    for m in range(4):

        @pl.when((me < HEADS) & (server_of(chip, m) != me))
        def _():
            to_server(m).start()

    for d in range(n):
        head_slabs[d] = head_rows[own * d : own * d + own, :].astype(BF16)

    def owner_copy(step):
        peer = lax.rem(me + step, n)
        return remote(
            head_slabs.at[peer], own_heads.at[me], sp_send.at[step], sp_recv.at[step], "tp", peer
        )

    for step in range(1, n):
        owner_copy(step).start()
    own_heads[me] = head_slabs[me]

    for i in range(2):
        loads[i].wait()
        for head in range(KV_HEADS):

            @pl.when(kv_server(head) != me)
            def _():
                kv_copy(i, head).start()

            @pl.when(kv_server(head) == me)
            def _():
                kv_local(i, head).start()

    for i in range(2):

        @pl.when(2 * served + i == me)
        def _():
            pair_ref[i] = head_ref[...]

        @pl.when(2 * served + i != me)
        def _():
            remote(
                head_ref, pair_ref.at[i], pr_send.at[0], pr_recv.at[i], "tp", 2 * served + i
            ).wait_recv()

    for i in range(2):
        chosen = jnp.dot(pick, pair_ref[i], preferred_element_type=F32)
        visit_ref[:, i * HEAD_DIM : (i + 1) * HEAD_DIM] = chosen.astype(BF16)

    def z_copy(turn, step):
        peer = lax.rem(plane + step, planes)
        src, dst = ((visit_ref, guest_ref), (reply_ref, answer_ref))[turn]
        return remote(
            src.at[pl.ds(peer * SLOTS, SLOTS)],
            dst.at[pl.ds(plane * SLOTS, SLOTS)],
            z_send.at[turn, step],
            z_recv.at[turn, step],
            "grp",
            peer,
        )

    for step in PLANE_STEPS:
        z_copy(0, step).start()
    guest_ref[here, :] = visit_ref[here, :]

    for step in range(1, n):
        owner_copy(step).wait_recv()
    for head in range(HEADS):
        block = own_heads[head].astype(F32)
        for r in range(own):
            query_f[r, head : head + 1, :] = block[r : r + 1, :]
    for head in range(KV_HEADS):
        new_key = own_heads[HEADS + head].astype(F32)
        new_value = own_heads[HEADS + KV_HEADS + head].astype(F32)
        for r in range(own):
            for i in range(2):
                spot = 2 * head + i
                key_f[r, spot : spot + 1, :] = new_key[r : r + 1, :]
                value_f[r, spot : spot + 1, :] = new_value[r : r + 1, :]
    loads[3].wait()
    loads[4].wait()
    tail_at = lax.broadcasted_iota(jnp.int32, (HEADS, tail_keys_ref.shape[1]), 1).astype(F32)
    head_of_row = lax.broadcasted_iota(jnp.int32, (HEADS, HEAD_DIM), 0) // 2
    for r in range(own):
        query = query_f[r]
        spread = jnp.concatenate(
            [jnp.where(head_of_row == k, query, 0.0) for k in range(KV_HEADS)], axis=1
        ).astype(BF16)
        scores = lax.dot_general(
            spread, tail_keys_ref[r], (((1,), (1,)), ((), ())), preferred_element_type=F32
        )
        length = jnp.sum(
            jnp.where(along[0:1, :] == me * own + r, tail_row, 0.0), axis=-1, keepdims=True
        )
        expo = jnp.where(tail_at < length, capped_exp(scores), 0.0)
        every = jnp.dot(expo.astype(BF16), tail_values_ref[r], preferred_element_type=F32)
        num = jnp.zeros((HEADS, HEAD_DIM), F32)
        for k in range(KV_HEADS):
            num = jnp.where(head_of_row == k, every[:, k * HEAD_DIM : (k + 1) * HEAD_DIM], num)
        self_exp = capped_exp(jnp.sum(query * key_f[r], axis=-1, keepdims=True))
        num = num + self_exp.astype(BF16).astype(F32) * value_f[r]
        den = jnp.sum(expo, axis=-1, keepdims=True) + self_exp
        den = jnp.broadcast_to(den, (HEADS, 128))
        for head in range(HEADS):
            own_f[head, r : r + 1, :HEAD_DIM] = num[head : head + 1, :]
            own_f[head, r : r + 1, HEAD_DIM:] = den[head : head + 1, :]
    lane = lax.broadcasted_iota(jnp.int32, (own, 128), 1)
    for head in range(HEADS):
        den = own_f[head, :, HEAD_DIM:]
        high = den.astype(BF16).astype(F32)
        words = jnp.where(lane == 0, high, jnp.where(lane == 1, den - high, 0.0)).astype(BF16)
        for i in range(2):
            own_out[2 * head + i, :, :128] = own_f[head, :, i * 128 : (i + 1) * 128].astype(BF16)
            own_out[2 * head + i, :, 128:] = words

    def column_copy(step):
        peer = lax.rem(me + step, n)
        return remote(
            own_out.at[peer], mine_ref.at[me], own_send.at[step], own_recv.at[step], "tp", peer
        )

    for step in range(1, n):
        column_copy(step).start()
    mine_ref[me] = own_out[me]

    for i in range(2):
        for head in range(KV_HEADS):

            @pl.when(kv_server(head) == me)
            def _():
                kv_local(i, head).wait()

        for slot in range(KV_HEADS):

            @pl.when(kv_source(slot) != me)
            def _():
                kv_arrival(i, slot).wait_recv()

    for step in PLANE_STEPS:
        z_copy(0, step).wait_recv()
    for step in PLANE_STEPS:
        limit_copy(step).wait_recv()
    at = lax.broadcasted_iota(jnp.int32, (1, KV_HEADS * piece), 1)
    block = at // piece
    pair_of, mate = block // 2, lax.rem(block, 2)
    device = jnp.where(core == 0, (x * 4 + pair_of) * 2 + mate, (pair_of * 4 + y) * 2 + mate)
    spot = (device * piece + lax.rem(at, piece)).astype(F32)
    many = planes * SLOTS // 2
    lanes = lax.broadcasted_iota(jnp.int32, (many, 128), 1)
    for j in range(2):
        part = slice(j * many, (j + 1) * many)
        limits = limit_ref[part, :].astype(F32)
        begin = limits[:, 0:1] * 64 + limits[:, 1:2]
        end = limits[:, 2:3] * 64 + limits[:, 3:4]
        visible = (spot >= begin) & (spot < end)
        words = jnp.zeros((many, 128), F32)
        for i in range(2):
            span = slice(i * HEAD_DIM, (i + 1) * HEAD_DIM)
            scores = lax.dot_general(
                guest_ref[part, span],
                key_blocks[...],
                (((1,), (1,)), ((), ())),
                preferred_element_type=F32,
            )
            expo = jnp.where(visible, capped_exp(scores), 0.0)
            num = jnp.dot(expo.astype(BF16), value_blocks[...], preferred_element_type=F32)
            reply_ref[part, span] = num.astype(BF16)
            den = jnp.sum(expo, axis=-1, keepdims=True)
            high = den.astype(BF16).astype(F32)
            words = jnp.where(lanes == 2 * i, high, words)
            words = jnp.where(lanes == 2 * i + 1, den - high, words)
        reply_ref[part, 2 * HEAD_DIM :] = words.astype(BF16)
    for step in PLANE_STEPS:
        z_copy(1, step).start()
    answer_ref[here, :] = reply_ref[here, :]
    for step in PLANE_STEPS:
        z_copy(1, step).wait_recv()

    back = jnp.dot(pick_t, answer_ref[...], preferred_element_type=F32).astype(BF16)
    for i in range(4):
        parts_ref[i] = back[:, i * 128 : (i + 1) * 128]
    word_ref[...] = turned(unit[:16, :], back[:, 2 * HEAD_DIM :]).astype(BF16)

    def join_copy(i):
        return remote(
            parts_ref.at[i],
            sums_ref.at[quarter],
            jn_send.at[i],
            jn_recv.at[quarter],
            "tp",
            4 * served + i,
        )

    def word_copy(i):
        return remote(
            word_ref,
            words_ref.at[quarter],
            wd_send.at[i],
            wd_recv.at[quarter],
            "tp",
            4 * served + i,
        )

    for i in range(4):

        @pl.when(4 * served + i != me)
        def _():
            join_copy(i).start()
            word_copy(i).start()

        @pl.when(4 * served + i == me)
        def _():
            sums_ref[quarter] = parts_ref[i]
            words_ref[quarter] = word_ref[...]

    for step in range(1, n):
        column_copy(step).wait_recv()
    for p in range(n // 2):
        mine_f[2 * own * p : 2 * own * (p + 1), :] = jnp.concatenate(
            [mine_ref[2 * p].astype(F32), mine_ref[2 * p + 1].astype(F32)], axis=0
        )
    for m in range(4):

        @pl.when(server_of(me // 4, m) != me)
        def _():
            remote(
                parts_ref.at[0],
                sums_ref.at[m],
                jn_send.at[0],
                jn_recv.at[m],
                "tp",
                server_of(me // 4, m),
            ).wait_recv()
            remote(
                word_ref,
                words_ref.at[m],
                wd_send.at[0],
                wd_recv.at[m],
                "tp",
                server_of(me // 4, m),
            ).wait_recv()

    num = mine_f[:, :128]
    den = mine_f[:, 128:129] + mine_f[:, 129:130]
    for m in range(4):
        num = num + sums_ref[m].astype(F32)
        words = turned(unit, words_ref[m])
        which = lax.broadcasted_iota(jnp.int32, words.shape, 1)
        words = jnp.where(which // 2 == lax.rem(me, 4) // 2, words, 0.0)
        den = den + jnp.sum(words, axis=-1, keepdims=True)
    attn = (num / den).astype(BF16)

    loads[5].wait()
    project(0, attn, w_out_ref)
    attn_proj = reduce_scatter(0)
    resid = hidden_ref[...].astype(F32) + rms_scale(attn_proj, gains_ref[1:2, :])
    resid = resid.astype(BF16).astype(F32)
    slab_ref[1] = rms_scale(resid, gains_ref[2:3, :]).astype(BF16)
    gather_start(1)
    gather_finish(1)
    loads[6].wait()
    loads[7].wait()
    gate = jnp.dot(rows_ref[...], w_gate_up_ref[0], preferred_element_type=F32)
    up = jnp.dot(rows_ref[...], w_gate_up_ref[1], preferred_element_type=F32)
    bent = jnp.tanh(math.sqrt(2.0 / math.pi) * (gate + 0.044715 * gate * gate * gate))
    hidden_units = (0.5 * gate * (1.0 + bent) * up).astype(BF16)
    project(1, hidden_units, w_down_ref)
    ffn_proj = reduce_scatter(1)
    out_ref[...] = resid + rms_scale(ffn_proj, gains_ref[3:4, :])

    for turn in range(2):
        gather_drain(turn)
        scatter_drain(turn)
        for step in PLANE_STEPS:
            z_copy(turn, step).wait_send()
    for step in PLANE_STEPS:
        limit_copy(step).wait_send()
    for i in range(2):
        for head in range(KV_HEADS):

            @pl.when(kv_server(head) != me)
            def _():
                kv_copy(i, head).wait_send()

    for m in range(4):

        @pl.when((me < HEADS) & (server_of(chip, m) != me))
        def _():
            to_server(m).wait_send()

        @pl.when(4 * served + m != me)
        def _():
            join_copy(m).wait_send()
            word_copy(m).wait_send()

    for step in range(1, n):
        owner_copy(step).wait_send()
        column_copy(step).wait_send()


def layer(n, planes, small, large):
    own, width = small[0].shape
    rows = own * n
    piece = large[4].shape[0]
    dma = pltpu.SemaphoreType.DMA

    def bf(*shape):
        return pltpu.VMEM(shape, BF16)

    def f32(*shape):
        return pltpu.VMEM(shape, F32)

    slots = planes * SLOTS
    scratch = [
        *(bf(*a.shape) for a in large),
        bf(2, own, width),
        bf(2, n, own, width),
        bf(rows, width),
        bf(KV_HEADS * piece, HEAD_DIM),
        bf(KV_HEADS * piece, HEAD_DIM),
        bf(rows, HEAD_DIM),
        bf(n, own, HEAD_DIM),
        bf(n, own, HEAD_DIM),
        bf(2, rows, HEAD_DIM),
        bf(slots, 2 * HEAD_DIM),
        bf(slots, 2 * HEAD_DIM),
        bf(slots, WIDE),
        bf(slots, WIDE),
        f32(own, HEADS, HEAD_DIM),
        f32(own, HEADS, HEAD_DIM),
        f32(own, HEADS, HEAD_DIM),
        f32(HEADS, own, HEAD_DIM + 128),
        bf(n, own, HEAD_DIM),
        bf(n, own, HEAD_DIM),
        f32(rows, HEAD_DIM),
        bf(4, rows, 128),
        bf(4, rows, 128),
        bf(2, 2, CHIPS, own, width),
        bf(2, CHIPS, own, width),
        bf(2, CHIPS, own, width),
        bf(2, CHIPS, own, width),
        bf(2, 4, own, width),
        bf(16, 128),
        bf(4, 16, 128),
        bf(slots, 128),
        bf(slots, 128),
        f32(8, 128),
        dma((8,)),
        dma((2, CHIPS)),
        dma((2, CHIPS)),
        dma((2, CHIPS)),
        dma((2, CHIPS)),
        dma((2, KV_HEADS)),
        dma((2, KV_HEADS)),
        dma((n,)),
        dma((n,)),
        dma((4,)),
        dma((2,)),
        dma((2, planes)),
        dma((2, planes)),
        dma((n,)),
        dma((n,)),
        dma((4,)),
        dma((4,)),
        dma((2, 2)),
        dma((2, 2)),
        dma((2, 2, CHIPS)),
        dma((2, 2, CHIPS)),
        dma((2,)),
        dma((4,)),
        dma((4,)),
        dma((planes,)),
        dma((planes,)),
    ]
    return pl.pallas_call(
        functools.partial(layer_kernel, n, planes),
        out_shape=jax.ShapeDtypeStruct((own, width), F32),
        in_specs=[pl.BlockSpec(memory_space=pltpu.VMEM)] * len(small)
        + [pl.BlockSpec(memory_space=pl.ANY)] * len(large),
        out_specs=pl.BlockSpec(memory_space=pltpu.VMEM),
        scratch_shapes=scratch,
        compiler_params=pltpu.CompilerParams(
            collective_id=0, has_side_effects=True, vmem_limit_bytes=60 * 1024 * 1024
        ),
        name="layer",
    )(*small, *large)


def per_device(
    n,
    planes,
    hidden_in,
    norm_gains,
    w_qkv,
    w_out,
    w_gate_up,
    w_down,
    prompt_keys,
    prompt_values,
    tail_keys,
    tail_values,
    prompt_len,
    group_home,
    req_group,
    tail_len,
):
    return layer(
        n,
        planes,
        (
            hidden_in,
            norm_gains,
            prompt_len[None],
            group_home[None],
            req_group[None],
            tail_len[None],
        ),
        (w_qkv, w_out, w_gate_up, w_down, prompt_keys, prompt_values, tail_keys, tail_values),
    ).astype(BF16)


def solution(mesh):
    in_specs = (
        P(("grp", "tp"), None),
        P(),
        P(None, "tp"),
        P("tp", None),
        P(None, None, "tp"),
        P("tp", None),
        P(("grp", "tp"), None),
        P(("grp", "tp"), None),
        P(("grp", "tp"), None, None),
        P(("grp", "tp"), None, None),
        P(),
        P(),
        P("grp"),
        P("grp"),
    )
    return jax.shard_map(
        functools.partial(per_device, mesh.shape["tp"], mesh.shape["grp"]),
        mesh=mesh,
        in_specs=in_specs,
        out_specs=P(("grp", "tp"), None),
        check_vma=False,
    )
```

```python
import functools
import math

import jax
import jax.numpy as jnp
from jax import lax
from jax.experimental import pallas as pl
from jax.experimental.pallas import tpu as pltpu
from jax.sharding import PartitionSpec as P

HEADS = 16
KV_HEADS = 8
HEAD_DIM = 256
HALF = HEAD_DIM // 2
SLOTS = 32
CHIPS = 16
NORM_EPS = 1e-06
SOFT_CAP = 50.0
MESH = pl.DeviceIdType.MESH
F32 = jnp.float32
BF16 = jnp.bfloat16
CHIP_STEPS = (10, 6, 9, 14, 11, 5, 7, 13, 15, 2, 8, 1, 4, 3, 12)
PLANE_STEPS = (4, 3, 5, 2, 6, 1, 7)


def rms_scale(values, gain_row):
    values = values.astype(F32)
    return (
        values * lax.rsqrt(jnp.mean(values * values, axis=-1, keepdims=True) + NORM_EPS) * gain_row
    )


def capped_exp(scores):
    return jnp.exp(SOFT_CAP * jnp.tanh(scores * (HEAD_DIM ** (-0.5) / SOFT_CAP)))


def remote(src, dst, send_sem, recv_sem, axis, peer):
    return pltpu.make_async_remote_copy(
        src_ref=src,
        dst_ref=dst,
        send_sem=send_sem,
        recv_sem=recv_sem,
        device_id={axis: peer},
        device_id_type=MESH,
    )


def server_of(head, m):
    column, line = column_of(head), row_of(head)
    return jnp.where(lax.rem(head, 4) < 2, (m * 4 + column) * 2, (line * 4 + m) * 2 + 1)


def column_of(head):
    return 2 * (head % 4) + head // 4 if isinstance(head, int) else 2 * lax.rem(head, 4) + head // 4


def row_of(head):
    return 2 * (head // 4) + (head % 4 if isinstance(head, int) else lax.rem(head, 4)) - 2


def layer_kernel(
    n,
    planes,
    hidden_ref,
    gains_ref,
    prompt_len_ref,
    group_home_ref,
    req_group_ref,
    tail_len_ref,
    w_qkv_hbm,
    w_out_hbm,
    w_gate_up_hbm,
    w_down_hbm,
    keys_hbm,
    values_hbm,
    tail_keys_hbm,
    tail_values_hbm,
    out_ref,
    w_qkv_ref,
    w_out_ref,
    w_gate_up_ref,
    w_down_ref,
    keys_ref,
    values_ref,
    tail_keys_ref,
    tail_values_ref,
    slab_ref,
    slabs_ref,
    rows_ref,
    key_blocks,
    value_blocks,
    head_ref,
    head_slabs,
    own_heads,
    pair_ref,
    visit_ref,
    guest_ref,
    reply_ref,
    answer_ref,
    query_f,
    key_f,
    value_f,
    own_f,
    own_out,
    mine_ref,
    mine_f,
    parts_ref,
    sums_ref,
    part_ref,
    half_ref,
    chip_ref,
    got_ref,
    word_ref,
    words_ref,
    bound_ref,
    limit_ref,
    table_ref,
    reply_words,
    answer_words,
    select_ref,
    load_sem,
    ag_send,
    ag_recv,
    fw_send,
    fw_recv,
    kv_send,
    kv_recv,
    sp_send,
    sp_recv,
    pr_send,
    pr_recv,
    z_send,
    z_recv,
    own_send,
    own_recv,
    jn_send,
    jn_recv,
    hf_send,
    hf_recv,
    rs_send,
    rs_recv,
    self_sem,
    wd_send,
    wd_recv,
    lm_send,
    lm_recv,
    bw_send,
    bw_recv,
):
    me = lax.axis_index("tp")
    plane = lax.axis_index("grp")
    chip, core = me // 2, lax.rem(me, 2)
    x, y = chip // 4, lax.rem(chip, 4)
    partner = chip * 2 + 1 - core
    served = jnp.where(core == 0, y // 2 + 4 * lax.rem(y, 2), 2 + lax.rem(x, 2) + 4 * (x // 2))
    quarter = jnp.where(core == 0, x, y)
    own, width = hidden_ref.shape
    rows = own * n

    loads = [
        pltpu.make_async_copy(src, dst, load_sem.at[i])
        for i, (src, dst) in enumerate(
            (
                (keys_hbm, keys_ref),
                (values_hbm, values_ref),
                (w_qkv_hbm, w_qkv_ref),
                (tail_keys_hbm, tail_keys_ref),
                (tail_values_hbm, tail_values_ref),
                (w_out_hbm, w_out_ref),
                (w_gate_up_hbm, w_gate_up_ref),
                (w_down_hbm, w_down_ref),
            )
        )
    ]
    for load in loads:
        load.start()

    barrier = pltpu.get_barrier_semaphore()
    for step in range(1, n):
        pl.semaphore_signal(
            barrier, inc=1, device_id={"tp": lax.rem(me + step, n)}, device_id_type=MESH
        )
    for step in range(1, planes):
        pl.semaphore_signal(
            barrier, inc=1, device_id={"grp": lax.rem(plane + step, planes)}, device_id_type=MESH
        )
    slab_ref[0] = rms_scale(hidden_ref[...], gains_ref[0:1, :]).astype(BF16)
    pl.semaphore_wait(barrier, n - 1 + planes - 1)

    def chip_at(step):
        return lax.rem(x + step // 4, 4) * 4 + lax.rem(y + step % 4, 4)

    def chip_from(step):
        return lax.rem(x + 4 - step // 4, 4) * 4 + lax.rem(y + 4 - step % 4, 4)

    def at_chip(step):
        return chip_at(step) * 2 + core

    def from_chip(step):
        return chip_from(step) * 2 + core

    def gather_copy(turn, step):
        return remote(
            slab_ref.at[turn],
            slabs_ref.at[turn, me],
            ag_send.at[turn, step],
            ag_recv.at[turn, step],
            "tp",
            at_chip(step),
        )

    def forward_copy(turn, step):
        source = from_chip(step)
        return remote(
            slab_ref.at[turn] if step == 0 else slabs_ref.at[turn, source],
            slabs_ref.at[turn, source],
            fw_send.at[turn, step],
            fw_recv.at[turn, step],
            "tp",
            partner,
        )

    def gather_start(turn):
        for step in CHIP_STEPS:
            gather_copy(turn, step).start()
        forward_copy(turn, 0).start()
        slabs_ref[turn, me] = slab_ref[turn]

    def gather_finish(turn):
        for step in CHIP_STEPS:
            gather_copy(turn, step).wait_recv()
            forward_copy(turn, step).start()
        for step in (0, *CHIP_STEPS):
            forward_copy(turn, step).wait_recv()
        for group in range(rows // 16):
            four = [slabs_ref[turn, group * 4 + i].astype(F32) for i in range(4)]
            rows_ref[group * 16 : group * 16 + 16, :] = jnp.concatenate(four, axis=0).astype(BF16)

    def gather_drain(turn):
        for step in CHIP_STEPS:
            gather_copy(turn, step).wait_send()
        for step in (0, *CHIP_STEPS):
            forward_copy(turn, step).wait_send()

    middle = width // 2

    def half_copy(turn, side):
        span = slice(side * middle, (side + 1) * middle)
        return remote(
            part_ref.at[turn, 1 - core, :, :, span],
            half_ref.at[turn, :, :, span],
            hf_send.at[turn, side],
            hf_recv.at[turn, side],
            "tp",
            partner,
        )

    def scatter_copy(turn, side, step):
        span = slice(side * middle, (side + 1) * middle)
        return remote(
            chip_ref.at[turn, chip_at(step), :, span],
            got_ref.at[turn, chip, :, span],
            rs_send.at[turn, side, step],
            rs_recv.at[turn, side, step],
            "tp",
            at_chip(step),
        )

    def project(turn, left, weight_ref):
        piece = middle // 2
        for side in range(2):

            def chunk(j, carry):
                columns = pl.ds(pl.multiple_of((2 * side + j) * piece, 128), piece)
                block = jnp.dot(left, weight_ref[:, columns], preferred_element_type=F32)
                for d in range(n):
                    part_ref[turn, d % 2, d // 2, :, columns] = block[own * d : own * d + own, :].astype(BF16)
                return carry

            lax.fori_loop(0, 2, chunk, 0)
            half_copy(turn, side).start()

    def reduce_scatter(turn):
        for side in range(2):
            span = slice(side * middle, (side + 1) * middle)
            half_copy(turn, side).wait_recv()
            for step in (*CHIP_STEPS, 0):
                target = chip_at(step)
                both = part_ref[turn, core, target, :, span].astype(F32)
                both = both + half_ref[turn, target, :, span].astype(F32)
                chip_ref[turn, target, :, span] = both.astype(BF16)
                if step:
                    scatter_copy(turn, side, step).start()
        total = chip_ref[turn, chip].astype(F32)
        for step in CHIP_STEPS:
            scatter_copy(turn, 0, step).wait_recv()
            scatter_copy(turn, 1, step).wait_recv()
            total = total + got_ref[turn, chip_from(step)].astype(F32)
        return total

    def scatter_drain(turn):
        for side in range(2):
            half_copy(turn, side).wait_send()
            for step in CHIP_STEPS:
                scatter_copy(turn, side, step).wait_send()

    gather_start(0)

    table_ref[...] = jnp.full((8, 128), -1.0, F32)
    groups = prompt_len_ref.shape[1]
    table_ref[0:1, :groups] = prompt_len_ref[...].astype(F32)
    table_ref[1:2, :groups] = group_home_ref[...].astype(F32)
    table_ref[2:3, :] = req_group_ref[...].astype(F32)
    table_ref[3:4, :] = tail_len_ref[...].astype(F32)
    len_row, home_row = table_ref[0:1, :], table_ref[1:2, :]
    tail_row = table_ref[3:4, :]
    down = lax.broadcasted_iota(jnp.int32, (128, 128), 0)
    along = lax.broadcasted_iota(jnp.int32, (128, 128), 1)
    unit = (down == along).astype(BF16)
    line = lax.broadcasted_iota(jnp.int32, (8, 128), 0)

    def stacked(*lines):
        total = jnp.zeros((8, 128), F32)
        for i, value in enumerate(lines):
            total = jnp.where(line == i, value, total)
        return total.astype(BF16)

    def split(value):
        high = jnp.floor(value * (1 / 64))
        return high, value - 64 * high

    def turned(left, right):
        return lax.dot_general(left, right, (((1,), (1,)), ((), ())), preferred_element_type=F32)

    columns = turned(unit, stacked(*split(len_row), home_row, table_ref[2:3, :], tail_row))
    len_column = columns[:, 0:1] * 64 + columns[:, 1:2]
    earlier = (columns[:, 2:3] == home_row) & (down < along)
    start_row = jnp.sum(jnp.where(earlier, len_column, 0.0), axis=0, keepdims=True)
    of_group = stacked(*split(len_row), home_row, *split(start_row))
    chosen = (columns[:, 3:4] == along.astype(F32)).astype(BF16)
    req = turned(chosen, of_group)
    req_row = turned(of_group, chosen)
    req_len = req[:, 0:1] * 64 + req[:, 1:2]
    req_stop = req[:, 3:4] * 64 + req[:, 4:5] + req_len
    same = req[:, 2:3] == req_row[2:3, :]
    rank = jnp.sum(jnp.where(same & (along < down), 1.0, 0.0), axis=1, keepdims=True)
    rank_row = jnp.sum(jnp.where(same & (down < along), 1.0, 0.0), axis=0, keepdims=True)
    slots = planes * SLOTS
    slot_down = lax.broadcasted_iota(jnp.int32, (slots, rows), 0).astype(F32)
    slot_along = lax.broadcasted_iota(jnp.int32, (rows, slots), 1).astype(F32)
    pick = (slot_down == req_row[2:3, :] * SLOTS + rank_row).astype(BF16)
    pick_t = (slot_along == req[:, 2:3] * SLOTS + rank).astype(BF16)
    bounds = jnp.zeros((rows, 128), F32)
    for i, value in enumerate((req[:, 3:4], req[:, 4:5], *split(req_stop))):
        bounds = jnp.where(along == i, value, bounds)
    at = lax.broadcasted_iota(jnp.int32, (1, planes * 128), 1)
    of_home = req[:, 2:3] == (at // 128).astype(F32)
    shift = (lax.rem(plane, planes // 2) * SLOTS).astype(F32)
    of_slot = rank + shift == lax.rem(at, 128).astype(F32)
    select_ref[...] = (of_home & of_slot).astype(BF16)
    bound_ref[...] = jnp.dot(pick, bounds.astype(BF16), preferred_element_type=F32).astype(BF16)

    def limit_copy(step):
        peer = lax.rem(plane + step, planes)
        return remote(
            bound_ref.at[pl.ds(peer * SLOTS, SLOTS)],
            limit_ref.at[pl.ds(plane * SLOTS, SLOTS)],
            lm_send.at[step],
            lm_recv.at[step],
            "grp",
            peer,
        )

    here = pl.ds(pl.multiple_of(plane * SLOTS, SLOTS), SLOTS)
    for step in PLANE_STEPS:
        limit_copy(step).start()
    limit_ref[here, :] = bound_ref[here, :]
    frequency = jnp.exp(along[0:1, :].astype(F32) * (-math.log(10000.0) / HALF))
    angles = (req_len + columns[:, 4:5]) * frequency
    cosine, sine = jnp.cos(angles), jnp.sin(angles)

    def kv_server(head):
        if head % 4 < 2:
            return (x * 4 + column_of(head)) * 2
        return (row_of(head) * 4 + y) * 2 + 1

    def kv_source(slot):
        mate = lax.rem(slot, 2)
        return jnp.where(core == 0, (x * 4 + slot // 2) * 2 + mate, (slot // 2 * 4 + y) * 2 + mate)

    pieces = ((keys_ref, key_blocks), (values_ref, value_blocks))
    piece = keys_ref.shape[0]

    def kv_copy(i, head):
        slot = (y if head % 4 < 2 else x) * 2 + core
        return remote(
            pieces[i][0].at[:, head * HEAD_DIM : (head + 1) * HEAD_DIM],
            pieces[i][1].at[pl.ds(slot * piece, piece)],
            kv_send.at[i, head],
            kv_recv.at[i, slot],
            "tp",
            kv_server(head),
        )

    def kv_local(i, head):
        slot = (y if head % 4 < 2 else x) * 2 + core
        return pltpu.make_async_copy(
            pieces[i][0].at[:, head * HEAD_DIM : (head + 1) * HEAD_DIM],
            pieces[i][1].at[pl.ds(slot * piece, piece)],
            self_sem.at[i],
        )

    def kv_arrival(i, slot):
        return remote(
            pieces[i][0].at[:, :HEAD_DIM],
            pieces[i][1].at[slot * piece : (slot + 1) * piece],
            kv_send.at[i, 0],
            kv_recv.at[i, slot],
            "tp",
            kv_source(slot),
        )

    gather_finish(0)
    loads[2].wait()
    head_rows = jnp.dot(rows_ref[...], w_qkv_ref[...], preferred_element_type=F32)
    head_rows = head_rows.astype(BF16).astype(F32)
    first, second = head_rows[:, :HALF], head_rows[:, HALF:]
    rotated = jnp.concatenate(
        [first * cosine - second * sine, second * cosine + first * sine], axis=-1
    )
    head_rows = jnp.where(me < HEADS + KV_HEADS, rotated, head_rows)
    head_ref[...] = head_rows.astype(BF16)

    index = lax.rem(me, 2)

    def to_server(m):
        return remote(
            head_ref,
            pair_ref.at[index],
            pr_send.at[m],
            pr_recv.at[index],
            "tp",
            server_of(chip, m),
        )

    for m in range(4):

        @pl.when((me < HEADS) & (server_of(chip, m) != me))
        def _():
            to_server(m).start()

    for d in range(n):
        head_slabs[d] = head_rows[own * d : own * d + own, :].astype(BF16)

    def owner_copy(step):
        peer = lax.rem(me + step, n)
        return remote(
            head_slabs.at[peer], own_heads.at[me], sp_send.at[step], sp_recv.at[step], "tp", peer
        )

    for step in range(1, n):
        owner_copy(step).start()
    own_heads[me] = head_slabs[me]

    for i in range(2):
        loads[i].wait()
        for head in range(KV_HEADS):

            @pl.when(kv_server(head) != me)
            def _():
                kv_copy(i, head).start()

            @pl.when(kv_server(head) == me)
            def _():
                kv_local(i, head).start()

    for i in range(2):

        @pl.when(2 * served + i == me)
        def _():
            pair_ref[i] = head_ref[...]

        @pl.when(2 * served + i != me)
        def _():
            remote(
                head_ref, pair_ref.at[i], pr_send.at[0], pr_recv.at[i], "tp", 2 * served + i
            ).wait_recv()

    for i in range(2):
        chosen = jnp.dot(pick, pair_ref[i], preferred_element_type=F32)
        visit_ref[:, i * HEAD_DIM : (i + 1) * HEAD_DIM] = chosen.astype(BF16)

    def z_copy(turn, step):
        peer = lax.rem(plane + step, planes)
        src, dst = ((visit_ref, guest_ref), (reply_ref, answer_ref))[turn]
        return remote(
            src.at[pl.ds(peer * SLOTS, SLOTS)],
            dst.at[pl.ds(plane * SLOTS, SLOTS)],
            z_send.at[turn, step],
            z_recv.at[turn, step],
            "grp",
            peer,
        )

    for step in PLANE_STEPS:
        z_copy(0, step).start()
    guest_ref[here, :] = visit_ref[here, :]

    for step in range(1, n):
        owner_copy(step).wait_recv()
    for head in range(HEADS):
        block = own_heads[head].astype(F32)
        for r in range(own):
            query_f[r, head : head + 1, :] = block[r : r + 1, :]
    for head in range(KV_HEADS):
        new_key = own_heads[HEADS + head].astype(F32)
        new_value = own_heads[HEADS + KV_HEADS + head].astype(F32)
        for r in range(own):
            for i in range(2):
                spot = 2 * head + i
                key_f[r, spot : spot + 1, :] = new_key[r : r + 1, :]
                value_f[r, spot : spot + 1, :] = new_value[r : r + 1, :]
    loads[3].wait()
    loads[4].wait()
    tail_at = lax.broadcasted_iota(jnp.int32, (HEADS, tail_keys_ref.shape[1]), 1).astype(F32)
    head_of_row = lax.broadcasted_iota(jnp.int32, (HEADS, HEAD_DIM), 0) // 2
    for r in range(own):
        query = query_f[r]
        spread = jnp.concatenate(
            [jnp.where(head_of_row == k, query, 0.0) for k in range(KV_HEADS)], axis=1
        ).astype(BF16)
        scores = lax.dot_general(
            spread, tail_keys_ref[r], (((1,), (1,)), ((), ())), preferred_element_type=F32
        )
        length = jnp.sum(
            jnp.where(along[0:1, :] == me * own + r, tail_row, 0.0), axis=-1, keepdims=True
        )
        expo = jnp.where(tail_at < length, capped_exp(scores), 0.0)
        every = jnp.dot(expo.astype(BF16), tail_values_ref[r], preferred_element_type=F32)
        num = jnp.zeros((HEADS, HEAD_DIM), F32)
        for k in range(KV_HEADS):
            num = jnp.where(head_of_row == k, every[:, k * HEAD_DIM : (k + 1) * HEAD_DIM], num)
        self_exp = capped_exp(jnp.sum(query * key_f[r], axis=-1, keepdims=True))
        num = num + self_exp.astype(BF16).astype(F32) * value_f[r]
        den = jnp.sum(expo, axis=-1, keepdims=True) + self_exp
        den = jnp.broadcast_to(den, (HEADS, 128))
        for head in range(HEADS):
            own_f[head, r : r + 1, :HEAD_DIM] = num[head : head + 1, :]
            own_f[head, r : r + 1, HEAD_DIM:] = den[head : head + 1, :]
    lane = lax.broadcasted_iota(jnp.int32, (own, 128), 1)
    for head in range(HEADS):
        den = own_f[head, :, HEAD_DIM:]
        high = den.astype(BF16).astype(F32)
        words = jnp.where(lane == 0, high, jnp.where(lane == 1, den - high, 0.0)).astype(BF16)
        for i in range(2):
            own_out[2 * head + i, :, :128] = own_f[head, :, i * 128 : (i + 1) * 128].astype(BF16)
            own_out[2 * head + i, :, 128:] = words

    def column_copy(step):
        peer = lax.rem(me + step, n)
        return remote(
            own_out.at[peer], mine_ref.at[me], own_send.at[step], own_recv.at[step], "tp", peer
        )

    for step in range(1, n):
        column_copy(step).start()
    mine_ref[me] = own_out[me]

    for i in range(2):
        for head in range(KV_HEADS):

            @pl.when(kv_server(head) == me)
            def _():
                kv_local(i, head).wait()

        for slot in range(KV_HEADS):

            @pl.when(kv_source(slot) != me)
            def _():
                kv_arrival(i, slot).wait_recv()

    for step in PLANE_STEPS:
        z_copy(0, step).wait_recv()
    for step in PLANE_STEPS:
        limit_copy(step).wait_recv()
    at = lax.broadcasted_iota(jnp.int32, (1, KV_HEADS * piece), 1)
    block = at // piece
    pair_of, mate = block // 2, lax.rem(block, 2)
    device = jnp.where(core == 0, (x * 4 + pair_of) * 2 + mate, (pair_of * 4 + y) * 2 + mate)
    spot = (device * piece + lax.rem(at, piece)).astype(F32)
    many = planes * SLOTS // 2

    def back_copy(step):
        peer = lax.rem(plane + step, planes)
        return remote(
            reply_words.at[peer // (planes // 2)],
            answer_words.at[plane],
            bw_send.at[step],
            bw_recv.at[step],
            "grp",
            peer,
        )

    lanes = lax.broadcasted_iota(jnp.int32, (many, 128), 1)
    for j in range(2):
        part = slice(j * many, (j + 1) * many)
        limits = limit_ref[part, :].astype(F32)
        begin = limits[:, 0:1] * 64 + limits[:, 1:2]
        end = limits[:, 2:3] * 64 + limits[:, 3:4]
        visible = (spot >= begin) & (spot < end)
        words = jnp.zeros((many, 128), F32)
        for i in range(2):
            span = slice(i * HEAD_DIM, (i + 1) * HEAD_DIM)
            scores = lax.dot_general(
                guest_ref[part, span],
                key_blocks[...],
                (((1,), (1,)), ((), ())),
                preferred_element_type=F32,
            )
            expo = jnp.where(visible, capped_exp(scores), 0.0)
            num = jnp.dot(expo.astype(BF16), value_blocks[...], preferred_element_type=F32)
            reply_ref[part, span] = num.astype(BF16)
            den = jnp.sum(expo, axis=-1, keepdims=True)
            high = den.astype(BF16).astype(F32)
            words = jnp.where(lanes == 2 * i, high, words)
            words = jnp.where(lanes == 2 * i + 1, den - high, words)
        reply_words[j] = turned(unit[:16, :], words.astype(BF16))[:4, :].astype(BF16)
        for i in range(planes // 2):
            guest = j * (planes // 2) + i
            away = lax.rem(guest + planes - plane, planes)

            @pl.when(guest != plane)
            def _():
                z_copy(1, away).start()
                back_copy(away).start()

    answer_ref[here, :] = reply_ref[here, :]
    answer_words[plane] = reply_words[plane // (planes // 2)]
    for step in PLANE_STEPS:
        z_copy(1, step).wait_recv()
        back_copy(step).wait_recv()

    back = jnp.dot(pick_t, answer_ref[...], preferred_element_type=F32).astype(BF16)
    for i in range(4):
        parts_ref[i] = back[:, i * 128 : (i + 1) * 128]
    lines = jnp.concatenate([answer_words[p].astype(F32) for p in range(planes)], axis=1)
    lines = jnp.concatenate([lines, jnp.zeros((12, lines.shape[1]), F32)], axis=0).astype(BF16)
    word_ref[...] = turned(lines, select_ref[...]).astype(BF16)

    def join_copy(i):
        return remote(
            parts_ref.at[i],
            sums_ref.at[quarter],
            jn_send.at[i],
            jn_recv.at[quarter],
            "tp",
            4 * served + i,
        )

    def word_copy(i):
        return remote(
            word_ref,
            words_ref.at[quarter],
            wd_send.at[i],
            wd_recv.at[quarter],
            "tp",
            4 * served + i,
        )

    for i in range(4):

        @pl.when(4 * served + i != me)
        def _():
            join_copy(i).start()
            word_copy(i).start()

        @pl.when(4 * served + i == me)
        def _():
            sums_ref[quarter] = parts_ref[i]
            words_ref[quarter] = word_ref[...]

    for step in range(1, n):
        column_copy(step).wait_recv()
    for p in range(n // 2):
        mine_f[2 * own * p : 2 * own * (p + 1), :] = jnp.concatenate(
            [mine_ref[2 * p].astype(F32), mine_ref[2 * p + 1].astype(F32)], axis=0
        )
    for m in range(4):

        @pl.when(server_of(me // 4, m) != me)
        def _():
            remote(
                parts_ref.at[0],
                sums_ref.at[m],
                jn_send.at[0],
                jn_recv.at[m],
                "tp",
                server_of(me // 4, m),
            ).wait_recv()
            remote(
                word_ref,
                words_ref.at[m],
                wd_send.at[0],
                wd_recv.at[m],
                "tp",
                server_of(me // 4, m),
            ).wait_recv()

    num = mine_f[:, :128]
    den = mine_f[:, 128:129] + mine_f[:, 129:130]
    for m in range(4):
        num = num + sums_ref[m].astype(F32)
        words = turned(unit, words_ref[m])
        which = lax.broadcasted_iota(jnp.int32, words.shape, 1)
        words = jnp.where(which // 2 == lax.rem(me, 4) // 2, words, 0.0)
        den = den + jnp.sum(words, axis=-1, keepdims=True)
    attn = (num / den).astype(BF16)

    loads[5].wait()
    project(0, attn, w_out_ref)
    attn_proj = reduce_scatter(0)
    resid = hidden_ref[...].astype(F32) + rms_scale(attn_proj, gains_ref[1:2, :])
    resid = resid.astype(BF16).astype(F32)
    slab_ref[1] = rms_scale(resid, gains_ref[2:3, :]).astype(BF16)
    gather_start(1)
    gather_finish(1)
    loads[6].wait()
    loads[7].wait()
    gate = jnp.dot(rows_ref[...], w_gate_up_ref[0], preferred_element_type=F32)
    up = jnp.dot(rows_ref[...], w_gate_up_ref[1], preferred_element_type=F32)
    bent = jnp.tanh(math.sqrt(2.0 / math.pi) * (gate + 0.044715 * gate * gate * gate))
    hidden_units = (0.5 * gate * (1.0 + bent) * up).astype(BF16)
    project(1, hidden_units, w_down_ref)
    ffn_proj = reduce_scatter(1)
    out_ref[...] = resid + rms_scale(ffn_proj, gains_ref[3:4, :])

    for turn in range(2):
        gather_drain(turn)
        scatter_drain(turn)
        for step in PLANE_STEPS:
            z_copy(turn, step).wait_send()
    for step in PLANE_STEPS:
        limit_copy(step).wait_send()
        back_copy(step).wait_send()
    for i in range(2):
        for head in range(KV_HEADS):

            @pl.when(kv_server(head) != me)
            def _():
                kv_copy(i, head).wait_send()

    for m in range(4):

        @pl.when((me < HEADS) & (server_of(chip, m) != me))
        def _():
            to_server(m).wait_send()

        @pl.when(4 * served + m != me)
        def _():
            join_copy(m).wait_send()
            word_copy(m).wait_send()

    for step in range(1, n):
        owner_copy(step).wait_send()
        column_copy(step).wait_send()


def layer(n, planes, small, large):
    own, width = small[0].shape
    rows = own * n
    piece = large[4].shape[0]
    dma = pltpu.SemaphoreType.DMA

    def bf(*shape):
        return pltpu.VMEM(shape, BF16)

    def f32(*shape):
        return pltpu.VMEM(shape, F32)

    slots = planes * SLOTS
    scratch = [
        *(bf(*a.shape) for a in large),
        bf(2, own, width),
        bf(2, n, own, width),
        bf(rows, width),
        bf(KV_HEADS * piece, HEAD_DIM),
        bf(KV_HEADS * piece, HEAD_DIM),
        bf(rows, HEAD_DIM),
        bf(n, own, HEAD_DIM),
        bf(n, own, HEAD_DIM),
        bf(2, rows, HEAD_DIM),
        bf(slots, 2 * HEAD_DIM),
        bf(slots, 2 * HEAD_DIM),
        bf(slots, 2 * HEAD_DIM),
        bf(slots, 2 * HEAD_DIM),
        f32(own, HEADS, HEAD_DIM),
        f32(own, HEADS, HEAD_DIM),
        f32(own, HEADS, HEAD_DIM),
        f32(HEADS, own, HEAD_DIM + 128),
        bf(n, own, HEAD_DIM),
        bf(n, own, HEAD_DIM),
        f32(rows, HEAD_DIM),
        bf(4, rows, 128),
        bf(4, rows, 128),
        bf(2, 2, CHIPS, own, width),
        bf(2, CHIPS, own, width),
        bf(2, CHIPS, own, width),
        bf(2, CHIPS, own, width),
        bf(16, 128),
        bf(4, 16, 128),
        bf(slots, 128),
        bf(slots, 128),
        f32(8, 128),
        bf(2, 4, 128),
        bf(planes, 4, 128),
        bf(rows, planes * 128),
        dma((8,)),
        dma((2, CHIPS)),
        dma((2, CHIPS)),
        dma((2, CHIPS)),
        dma((2, CHIPS)),
        dma((2, KV_HEADS)),
        dma((2, KV_HEADS)),
        dma((n,)),
        dma((n,)),
        dma((4,)),
        dma((2,)),
        dma((2, planes)),
        dma((2, planes)),
        dma((n,)),
        dma((n,)),
        dma((4,)),
        dma((4,)),
        dma((2, 2)),
        dma((2, 2)),
        dma((2, 2, CHIPS)),
        dma((2, 2, CHIPS)),
        dma((2,)),
        dma((4,)),
        dma((4,)),
        dma((planes,)),
        dma((planes,)),
        dma((planes,)),
        dma((planes,)),
    ]
    return pl.pallas_call(
        functools.partial(layer_kernel, n, planes),
        out_shape=jax.ShapeDtypeStruct((own, width), F32),
        in_specs=[pl.BlockSpec(memory_space=pltpu.VMEM)] * len(small)
        + [pl.BlockSpec(memory_space=pl.ANY)] * len(large),
        out_specs=pl.BlockSpec(memory_space=pltpu.VMEM),
        scratch_shapes=scratch,
        compiler_params=pltpu.CompilerParams(
            collective_id=0, has_side_effects=True, vmem_limit_bytes=60 * 1024 * 1024
        ),
        name="layer",
    )(*small, *large)


def per_device(
    n,
    planes,
    hidden_in,
    norm_gains,
    w_qkv,
    w_out,
    w_gate_up,
    w_down,
    prompt_keys,
    prompt_values,
    tail_keys,
    tail_values,
    prompt_len,
    group_home,
    req_group,
    tail_len,
):
    return layer(
        n,
        planes,
        (
            hidden_in,
            norm_gains,
            prompt_len[None],
            group_home[None],
            req_group[None],
            tail_len[None],
        ),
        (w_qkv, w_out, w_gate_up, w_down, prompt_keys, prompt_values, tail_keys, tail_values),
    ).astype(BF16)


def solution(mesh):
    in_specs = (
        P(("grp", "tp"), None),
        P(),
        P(None, "tp"),
        P("tp", None),
        P(None, None, "tp"),
        P("tp", None),
        P(("grp", "tp"), None),
        P(("grp", "tp"), None),
        P(("grp", "tp"), None, None),
        P(("grp", "tp"), None, None),
        P(),
        P(),
        P("grp"),
        P("grp"),
    )
    return jax.shard_map(
        functools.partial(per_device, mesh.shape["tp"], mesh.shape["grp"]),
        mesh=mesh,
        in_specs=in_specs,
        out_specs=P(("grp", "tp"), None),
        check_vma=False,
    )
```

```python
import functools
import math

import jax
import jax.numpy as jnp
from jax import lax
from jax.experimental import pallas as pl
from jax.experimental.pallas import tpu as pltpu
from jax.sharding import PartitionSpec as P

HEADS = 16
KV_HEADS = 8
HEAD_DIM = 256
HALF = HEAD_DIM // 2
SLOTS = 32
CHIPS = 16
NORM_EPS = 1e-06
SOFT_CAP = 50.0
MESH = pl.DeviceIdType.MESH
F32 = jnp.float32
BF16 = jnp.bfloat16
CHIP_STEPS = (10, 6, 9, 14, 11, 5, 7, 13, 15, 2, 8, 1, 4, 3, 12)
PLANE_STEPS = (4, 3, 5, 2, 6, 1, 7)


def rms_scale(values, gain_row):
    values = values.astype(F32)
    return (
        values * lax.rsqrt(jnp.mean(values * values, axis=-1, keepdims=True) + NORM_EPS) * gain_row
    )


def capped_exp(scores):
    return jnp.exp(SOFT_CAP * jnp.tanh(scores * (HEAD_DIM ** (-0.5) / SOFT_CAP)))


def remote(src, dst, send_sem, recv_sem, axis, peer):
    return pltpu.make_async_remote_copy(
        src_ref=src,
        dst_ref=dst,
        send_sem=send_sem,
        recv_sem=recv_sem,
        device_id={axis: peer},
        device_id_type=MESH,
    )


def server_of(head, m):
    column, line = column_of(head), row_of(head)
    return jnp.where(lax.rem(head, 4) < 2, (m * 4 + column) * 2, (line * 4 + m) * 2 + 1)


def column_of(head):
    return 2 * (head % 4) + head // 4 if isinstance(head, int) else 2 * lax.rem(head, 4) + head // 4


def row_of(head):
    return 2 * (head // 4) + (head % 4 if isinstance(head, int) else lax.rem(head, 4)) - 2


def layer_kernel(
    n,
    planes,
    hidden_ref,
    gains_ref,
    prompt_len_ref,
    group_home_ref,
    req_group_ref,
    tail_len_ref,
    w_qkv_hbm,
    w_out_hbm,
    w_gate_up_hbm,
    w_down_hbm,
    keys_hbm,
    values_hbm,
    tail_keys_hbm,
    tail_values_hbm,
    out_ref,
    w_qkv_ref,
    w_out_ref,
    w_gate_up_ref,
    w_down_ref,
    keys_ref,
    values_ref,
    tail_keys_ref,
    tail_values_ref,
    slab_ref,
    slabs_ref,
    rows_ref,
    key_blocks,
    value_blocks,
    head_ref,
    head_slabs,
    own_heads,
    pair_ref,
    visit_ref,
    guest_ref,
    reply_ref,
    answer_ref,
    query_f,
    key_f,
    value_f,
    own_f,
    own_out,
    mine_ref,
    mine_f,
    parts_ref,
    sums_ref,
    part_ref,
    half_ref,
    chip_ref,
    got_ref,
    word_ref,
    words_ref,
    bound_ref,
    limit_ref,
    table_ref,
    reply_words,
    answer_words,
    select_ref,
    load_sem,
    ag_send,
    ag_recv,
    fw_send,
    fw_recv,
    kv_send,
    kv_recv,
    sp_send,
    sp_recv,
    pr_send,
    pr_recv,
    z_send,
    z_recv,
    own_send,
    own_recv,
    jn_send,
    jn_recv,
    hf_send,
    hf_recv,
    rs_send,
    rs_recv,
    self_sem,
    wd_send,
    wd_recv,
    lm_send,
    lm_recv,
    bw_send,
    bw_recv,
):
    me = lax.axis_index("tp")
    plane = lax.axis_index("grp")
    chip, core = me // 2, lax.rem(me, 2)
    x, y = chip // 4, lax.rem(chip, 4)
    partner = chip * 2 + 1 - core
    served = jnp.where(core == 0, y // 2 + 4 * lax.rem(y, 2), 2 + lax.rem(x, 2) + 4 * (x // 2))
    quarter = jnp.where(core == 0, x, y)
    own, width = hidden_ref.shape
    rows = own * n

    loads = [
        pltpu.make_async_copy(src, dst, load_sem.at[i])
        for i, (src, dst) in enumerate(
            (
                (keys_hbm, keys_ref),
                (values_hbm, values_ref),
                (w_qkv_hbm, w_qkv_ref),
                (tail_keys_hbm, tail_keys_ref),
                (tail_values_hbm, tail_values_ref),
                (w_out_hbm, w_out_ref),
                (w_gate_up_hbm, w_gate_up_ref),
                (w_down_hbm, w_down_ref),
            )
        )
    ]
    for load in loads:
        load.start()

    barrier = pltpu.get_barrier_semaphore()
    for step in range(1, n):
        pl.semaphore_signal(
            barrier, inc=1, device_id={"tp": lax.rem(me + step, n)}, device_id_type=MESH
        )
    for step in range(1, planes):
        pl.semaphore_signal(
            barrier, inc=1, device_id={"grp": lax.rem(plane + step, planes)}, device_id_type=MESH
        )
    slab_ref[0] = rms_scale(hidden_ref[...], gains_ref[0:1, :]).astype(BF16)
    pl.semaphore_wait(barrier, n - 1 + planes - 1)

    def chip_at(step):
        return lax.rem(x + step // 4, 4) * 4 + lax.rem(y + step % 4, 4)

    def chip_from(step):
        return lax.rem(x + 4 - step // 4, 4) * 4 + lax.rem(y + 4 - step % 4, 4)

    def at_chip(step):
        return chip_at(step) * 2 + core

    def from_chip(step):
        return chip_from(step) * 2 + core

    def gather_copy(turn, step):
        return remote(
            slab_ref.at[turn],
            slabs_ref.at[turn, me],
            ag_send.at[turn, step],
            ag_recv.at[turn, step],
            "tp",
            at_chip(step),
        )

    def forward_copy(turn, step):
        source = from_chip(step)
        return remote(
            slab_ref.at[turn] if step == 0 else slabs_ref.at[turn, source],
            slabs_ref.at[turn, source],
            fw_send.at[turn, step],
            fw_recv.at[turn, step],
            "tp",
            partner,
        )

    def gather_start(turn):
        for step in CHIP_STEPS:
            gather_copy(turn, step).start()
        forward_copy(turn, 0).start()
        slabs_ref[turn, me] = slab_ref[turn]

    def gather_finish(turn):
        for step in CHIP_STEPS:
            gather_copy(turn, step).wait_recv()
            forward_copy(turn, step).start()
        for step in (0, *CHIP_STEPS):
            forward_copy(turn, step).wait_recv()
        for group in range(rows // 16):
            four = [slabs_ref[turn, group * 4 + i].astype(F32) for i in range(4)]
            rows_ref[group * 16 : group * 16 + 16, :] = jnp.concatenate(four, axis=0).astype(BF16)

    def gather_drain(turn):
        for step in CHIP_STEPS:
            gather_copy(turn, step).wait_send()
        for step in (0, *CHIP_STEPS):
            forward_copy(turn, step).wait_send()

    middle = width // 2

    def half_copy(turn, side):
        span = slice(side * middle, (side + 1) * middle)
        return remote(
            part_ref.at[turn, 1 - core, :, :, span],
            half_ref.at[turn, :, :, span],
            hf_send.at[turn, side],
            hf_recv.at[turn, side],
            "tp",
            partner,
        )

    def scatter_copy(turn, side, step):
        span = slice(side * middle, (side + 1) * middle)
        return remote(
            chip_ref.at[turn, chip_at(step), :, span],
            got_ref.at[turn, chip, :, span],
            rs_send.at[turn, side, step],
            rs_recv.at[turn, side, step],
            "tp",
            at_chip(step),
        )

    def project(turn, left, weight_ref):
        piece = middle // 2
        for side in range(2):

            def chunk(j, carry):
                columns = pl.ds(pl.multiple_of((2 * side + j) * piece, 128), piece)
                block = jnp.dot(left, weight_ref[:, columns], preferred_element_type=F32)
                for d in range(n):
                    part_ref[turn, d % 2, d // 2, :, columns] = block[own * d : own * d + own, :].astype(BF16)
                return carry

            lax.fori_loop(0, 2, chunk, 0)
            half_copy(turn, side).start()

    def reduce_scatter(turn):
        for side in range(2):
            span = slice(side * middle, (side + 1) * middle)
            half_copy(turn, side).wait_recv()
            for step in (*CHIP_STEPS, 0):
                target = chip_at(step)
                both = part_ref[turn, core, target, :, span].astype(F32)
                both = both + half_ref[turn, target, :, span].astype(F32)
                chip_ref[turn, target, :, span] = both.astype(BF16)
                if step:
                    scatter_copy(turn, side, step).start()
        total = chip_ref[turn, chip].astype(F32)
        for step in CHIP_STEPS:
            scatter_copy(turn, 0, step).wait_recv()
            scatter_copy(turn, 1, step).wait_recv()
            total = total + got_ref[turn, chip_from(step)].astype(F32)
        return total

    def scatter_drain(turn):
        for side in range(2):
            half_copy(turn, side).wait_send()
            for step in CHIP_STEPS:
                scatter_copy(turn, side, step).wait_send()

    gather_start(0)

    table_ref[...] = jnp.full((8, 128), -1.0, F32)
    groups = prompt_len_ref.shape[1]
    table_ref[0:1, :groups] = prompt_len_ref[...].astype(F32)
    table_ref[1:2, :groups] = group_home_ref[...].astype(F32)
    table_ref[2:3, :] = req_group_ref[...].astype(F32)
    table_ref[3:4, :] = tail_len_ref[...].astype(F32)
    len_row, home_row = table_ref[0:1, :], table_ref[1:2, :]
    tail_row = table_ref[3:4, :]
    down = lax.broadcasted_iota(jnp.int32, (128, 128), 0)
    along = lax.broadcasted_iota(jnp.int32, (128, 128), 1)
    unit = (down == along).astype(BF16)
    line = lax.broadcasted_iota(jnp.int32, (8, 128), 0)

    def stacked(*lines):
        total = jnp.zeros((8, 128), F32)
        for i, value in enumerate(lines):
            total = jnp.where(line == i, value, total)
        return total.astype(BF16)

    def split(value):
        high = jnp.floor(value * (1 / 64))
        return high, value - 64 * high

    def turned(left, right):
        return lax.dot_general(left, right, (((1,), (1,)), ((), ())), preferred_element_type=F32)

    columns = turned(unit, stacked(*split(len_row), home_row, table_ref[2:3, :], tail_row))
    len_column = columns[:, 0:1] * 64 + columns[:, 1:2]
    earlier = (columns[:, 2:3] == home_row) & (down < along)
    start_row = jnp.sum(jnp.where(earlier, len_column, 0.0), axis=0, keepdims=True)
    of_group = stacked(*split(len_row), home_row, *split(start_row))
    chosen = (columns[:, 3:4] == along.astype(F32)).astype(BF16)
    req = turned(chosen, of_group)
    req_row = turned(of_group, chosen)
    req_len = req[:, 0:1] * 64 + req[:, 1:2]
    req_stop = req[:, 3:4] * 64 + req[:, 4:5] + req_len
    same = req[:, 2:3] == req_row[2:3, :]
    rank = jnp.sum(jnp.where(same & (along < down), 1.0, 0.0), axis=1, keepdims=True)
    rank_row = jnp.sum(jnp.where(same & (down < along), 1.0, 0.0), axis=0, keepdims=True)
    slots = planes * SLOTS
    slot_down = lax.broadcasted_iota(jnp.int32, (slots, rows), 0).astype(F32)
    slot_along = lax.broadcasted_iota(jnp.int32, (rows, slots), 1).astype(F32)
    pick = (slot_down == req_row[2:3, :] * SLOTS + rank_row).astype(BF16)
    pick_t = (slot_along == req[:, 2:3] * SLOTS + rank).astype(BF16)
    bounds = jnp.zeros((rows, 128), F32)
    for i, value in enumerate((req[:, 3:4], req[:, 4:5], *split(req_stop))):
        bounds = jnp.where(along == i, value, bounds)
    at = lax.broadcasted_iota(jnp.int32, (1, planes * 128), 1)
    of_home = req[:, 2:3] == (at // 128).astype(F32)
    shift = (lax.rem(plane, planes // 2) * SLOTS).astype(F32)
    of_slot = rank + shift == lax.rem(at, 128).astype(F32)
    select_ref[...] = (of_home & of_slot).astype(BF16)
    bound_ref[...] = jnp.dot(pick, bounds.astype(BF16), preferred_element_type=F32).astype(BF16)

    def limit_copy(step):
        peer = lax.rem(plane + step, planes)
        return remote(
            bound_ref.at[pl.ds(peer * SLOTS, SLOTS)],
            limit_ref.at[pl.ds(plane * SLOTS, SLOTS)],
            lm_send.at[step],
            lm_recv.at[step],
            "grp",
            peer,
        )

    here = pl.ds(pl.multiple_of(plane * SLOTS, SLOTS), SLOTS)
    for step in PLANE_STEPS:
        limit_copy(step).start()
    limit_ref[here, :] = bound_ref[here, :]
    frequency = jnp.exp(along[0:1, :].astype(F32) * (-math.log(10000.0) / HALF))
    angles = (req_len + columns[:, 4:5]) * frequency
    cosine, sine = jnp.cos(angles), jnp.sin(angles)

    def kv_server(head):
        if head % 4 < 2:
            return (x * 4 + column_of(head)) * 2
        return (row_of(head) * 4 + y) * 2 + 1

    def kv_source(slot):
        mate = lax.rem(slot, 2)
        return jnp.where(core == 0, (x * 4 + slot // 2) * 2 + mate, (slot // 2 * 4 + y) * 2 + mate)

    pieces = ((keys_ref, key_blocks), (values_ref, value_blocks))
    piece = keys_ref.shape[0]

    def kv_copy(i, head):
        slot = (y if head % 4 < 2 else x) * 2 + core
        return remote(
            pieces[i][0].at[:, head * HEAD_DIM : (head + 1) * HEAD_DIM],
            pieces[i][1].at[pl.ds(slot * piece, piece)],
            kv_send.at[i, head],
            kv_recv.at[i, slot],
            "tp",
            kv_server(head),
        )

    def kv_local(i, head):
        slot = (y if head % 4 < 2 else x) * 2 + core
        return pltpu.make_async_copy(
            pieces[i][0].at[:, head * HEAD_DIM : (head + 1) * HEAD_DIM],
            pieces[i][1].at[pl.ds(slot * piece, piece)],
            self_sem.at[i],
        )

    def kv_arrival(i, slot):
        return remote(
            pieces[i][0].at[:, :HEAD_DIM],
            pieces[i][1].at[slot * piece : (slot + 1) * piece],
            kv_send.at[i, 0],
            kv_recv.at[i, slot],
            "tp",
            kv_source(slot),
        )

    gather_finish(0)
    loads[2].wait()
    head_rows = jnp.dot(rows_ref[...], w_qkv_ref[...], preferred_element_type=F32)
    head_rows = head_rows.astype(BF16).astype(F32)
    first, second = head_rows[:, :HALF], head_rows[:, HALF:]
    rotated = jnp.concatenate(
        [first * cosine - second * sine, second * cosine + first * sine], axis=-1
    )
    head_rows = jnp.where(me < HEADS + KV_HEADS, rotated, head_rows)
    head_ref[...] = head_rows.astype(BF16)

    index = lax.rem(me, 2)

    def to_server(m):
        return remote(
            head_ref,
            pair_ref.at[index],
            pr_send.at[m],
            pr_recv.at[index],
            "tp",
            server_of(chip, m),
        )

    base = jnp.where(lax.rem(chip, 4) < 2, x, y)
    for away in (2, 1, 3, 0):
        m = lax.rem(base + away, 4)

        @pl.when((me < HEADS) & (server_of(chip, m) != me))
        def _():
            to_server(m).start()

    for d in range(n):
        head_slabs[d] = head_rows[own * d : own * d + own, :].astype(BF16)

    def owner_copy(step):
        peer = lax.rem(me + step, n)
        return remote(
            head_slabs.at[peer], own_heads.at[me], sp_send.at[step], sp_recv.at[step], "tp", peer
        )

    for step in range(1, n):
        owner_copy(step).start()
    own_heads[me] = head_slabs[me]

    for i in range(2):
        loads[i].wait()
        for head in range(KV_HEADS):

            @pl.when(kv_server(head) != me)
            def _():
                kv_copy(i, head).start()

            @pl.when(kv_server(head) == me)
            def _():
                kv_local(i, head).start()

    for i in range(2):

        @pl.when(2 * served + i == me)
        def _():
            pair_ref[i] = head_ref[...]

        @pl.when(2 * served + i != me)
        def _():
            remote(
                head_ref, pair_ref.at[i], pr_send.at[0], pr_recv.at[i], "tp", 2 * served + i
            ).wait_recv()

    for i in range(2):
        chosen = jnp.dot(pick, pair_ref[i], preferred_element_type=F32)
        visit_ref[:, i * HEAD_DIM : (i + 1) * HEAD_DIM] = chosen.astype(BF16)

    def z_copy(turn, step):
        peer = lax.rem(plane + step, planes)
        src, dst = ((visit_ref, guest_ref), (reply_ref, answer_ref))[turn]
        return remote(
            src.at[pl.ds(peer * SLOTS, SLOTS)],
            dst.at[pl.ds(plane * SLOTS, SLOTS)],
            z_send.at[turn, step],
            z_recv.at[turn, step],
            "grp",
            peer,
        )

    for step in PLANE_STEPS:
        z_copy(0, step).start()
    guest_ref[here, :] = visit_ref[here, :]

    for step in range(1, n):
        owner_copy(step).wait_recv()
    for head in range(HEADS):
        block = own_heads[head].astype(F32)
        for r in range(own):
            query_f[r, head : head + 1, :] = block[r : r + 1, :]
    for head in range(KV_HEADS):
        new_key = own_heads[HEADS + head].astype(F32)
        new_value = own_heads[HEADS + KV_HEADS + head].astype(F32)
        for r in range(own):
            for i in range(2):
                spot = 2 * head + i
                key_f[r, spot : spot + 1, :] = new_key[r : r + 1, :]
                value_f[r, spot : spot + 1, :] = new_value[r : r + 1, :]
    loads[3].wait()
    loads[4].wait()
    tail_at = lax.broadcasted_iota(jnp.int32, (HEADS, tail_keys_ref.shape[1]), 1).astype(F32)
    head_of_row = lax.broadcasted_iota(jnp.int32, (HEADS, HEAD_DIM), 0) // 2
    for r in range(own):
        query = query_f[r]
        spread = jnp.concatenate(
            [jnp.where(head_of_row == k, query, 0.0) for k in range(KV_HEADS)], axis=1
        ).astype(BF16)
        scores = lax.dot_general(
            spread, tail_keys_ref[r], (((1,), (1,)), ((), ())), preferred_element_type=F32
        )
        length = jnp.sum(
            jnp.where(along[0:1, :] == me * own + r, tail_row, 0.0), axis=-1, keepdims=True
        )
        expo = jnp.where(tail_at < length, capped_exp(scores), 0.0)
        every = jnp.dot(expo.astype(BF16), tail_values_ref[r], preferred_element_type=F32)
        num = jnp.zeros((HEADS, HEAD_DIM), F32)
        for k in range(KV_HEADS):
            num = jnp.where(head_of_row == k, every[:, k * HEAD_DIM : (k + 1) * HEAD_DIM], num)
        self_exp = capped_exp(jnp.sum(query * key_f[r], axis=-1, keepdims=True))
        num = num + self_exp.astype(BF16).astype(F32) * value_f[r]
        den = jnp.sum(expo, axis=-1, keepdims=True) + self_exp
        den = jnp.broadcast_to(den, (HEADS, 128))
        for head in range(HEADS):
            own_f[head, r : r + 1, :HEAD_DIM] = num[head : head + 1, :]
            own_f[head, r : r + 1, HEAD_DIM:] = den[head : head + 1, :]
    lane = lax.broadcasted_iota(jnp.int32, (own, 128), 1)
    for head in range(HEADS):
        den = own_f[head, :, HEAD_DIM:]
        high = den.astype(BF16).astype(F32)
        words = jnp.where(lane == 0, high, jnp.where(lane == 1, den - high, 0.0)).astype(BF16)
        for i in range(2):
            own_out[2 * head + i, :, :128] = own_f[head, :, i * 128 : (i + 1) * 128].astype(BF16)
            own_out[2 * head + i, :, 128:] = words

    def column_copy(step):
        peer = lax.rem(me + step, n)
        return remote(
            own_out.at[peer], mine_ref.at[me], own_send.at[step], own_recv.at[step], "tp", peer
        )

    for step in range(1, n):
        column_copy(step).start()
    mine_ref[me] = own_out[me]

    for i in range(2):
        for head in range(KV_HEADS):

            @pl.when(kv_server(head) == me)
            def _():
                kv_local(i, head).wait()

        for slot in range(KV_HEADS):

            @pl.when(kv_source(slot) != me)
            def _():
                kv_arrival(i, slot).wait_recv()

    for step in PLANE_STEPS:
        z_copy(0, step).wait_recv()
    for step in PLANE_STEPS:
        limit_copy(step).wait_recv()
    at = lax.broadcasted_iota(jnp.int32, (1, KV_HEADS * piece), 1)
    block = at // piece
    pair_of, mate = block // 2, lax.rem(block, 2)
    device = jnp.where(core == 0, (x * 4 + pair_of) * 2 + mate, (pair_of * 4 + y) * 2 + mate)
    spot = (device * piece + lax.rem(at, piece)).astype(F32)
    many = planes * SLOTS // 2

    def back_copy(step):
        peer = lax.rem(plane + step, planes)
        return remote(
            reply_words.at[peer // (planes // 2)],
            answer_words.at[plane],
            bw_send.at[step],
            bw_recv.at[step],
            "grp",
            peer,
        )

    lanes = lax.broadcasted_iota(jnp.int32, (many, 128), 1)
    for j in range(2):
        part = slice(j * many, (j + 1) * many)
        limits = limit_ref[part, :].astype(F32)
        begin = limits[:, 0:1] * 64 + limits[:, 1:2]
        end = limits[:, 2:3] * 64 + limits[:, 3:4]
        visible = (spot >= begin) & (spot < end)
        words = jnp.zeros((many, 128), F32)
        for i in range(2):
            span = slice(i * HEAD_DIM, (i + 1) * HEAD_DIM)
            scores = lax.dot_general(
                guest_ref[part, span],
                key_blocks[...],
                (((1,), (1,)), ((), ())),
                preferred_element_type=F32,
            )
            expo = jnp.where(visible, capped_exp(scores), 0.0)
            num = jnp.dot(expo.astype(BF16), value_blocks[...], preferred_element_type=F32)
            reply_ref[part, span] = num.astype(BF16)
            den = jnp.sum(expo, axis=-1, keepdims=True)
            high = den.astype(BF16).astype(F32)
            words = jnp.where(lanes == 2 * i, high, words)
            words = jnp.where(lanes == 2 * i + 1, den - high, words)
        reply_words[j] = turned(unit[:16, :], words.astype(BF16))[:4, :].astype(BF16)
        for i in range(planes // 2):
            guest = j * (planes // 2) + i
            away = lax.rem(guest + planes - plane, planes)

            @pl.when(guest != plane)
            def _():
                z_copy(1, away).start()
                back_copy(away).start()

    answer_ref[here, :] = reply_ref[here, :]
    answer_words[plane] = reply_words[plane // (planes // 2)]
    for step in PLANE_STEPS:
        z_copy(1, step).wait_recv()
        back_copy(step).wait_recv()

    back = jnp.dot(pick_t, answer_ref[...], preferred_element_type=F32).astype(BF16)
    for i in range(4):
        parts_ref[i] = back[:, i * 128 : (i + 1) * 128]
    lines = jnp.concatenate([answer_words[p].astype(F32) for p in range(planes)], axis=1)
    lines = jnp.concatenate([lines, jnp.zeros((12, lines.shape[1]), F32)], axis=0).astype(BF16)
    word_ref[...] = turned(lines, select_ref[...]).astype(BF16)

    def join_copy(i):
        return remote(
            parts_ref.at[i],
            sums_ref.at[quarter],
            jn_send.at[i],
            jn_recv.at[quarter],
            "tp",
            4 * served + i,
        )

    def word_copy(i):
        return remote(
            word_ref,
            words_ref.at[quarter],
            wd_send.at[i],
            wd_recv.at[quarter],
            "tp",
            4 * served + i,
        )

    for i in range(4):

        @pl.when(4 * served + i != me)
        def _():
            join_copy(i).start()
            word_copy(i).start()

        @pl.when(4 * served + i == me)
        def _():
            sums_ref[quarter] = parts_ref[i]
            words_ref[quarter] = word_ref[...]

    for step in range(1, n):
        column_copy(step).wait_recv()
    for p in range(n // 2):
        mine_f[2 * own * p : 2 * own * (p + 1), :] = jnp.concatenate(
            [mine_ref[2 * p].astype(F32), mine_ref[2 * p + 1].astype(F32)], axis=0
        )
    for m in range(4):

        @pl.when(server_of(me // 4, m) != me)
        def _():
            remote(
                parts_ref.at[0],
                sums_ref.at[m],
                jn_send.at[0],
                jn_recv.at[m],
                "tp",
                server_of(me // 4, m),
            ).wait_recv()
            remote(
                word_ref,
                words_ref.at[m],
                wd_send.at[0],
                wd_recv.at[m],
                "tp",
                server_of(me // 4, m),
            ).wait_recv()

    num = mine_f[:, :128]
    den = mine_f[:, 128:129] + mine_f[:, 129:130]
    for m in range(4):
        num = num + sums_ref[m].astype(F32)
        words = turned(unit, words_ref[m])
        which = lax.broadcasted_iota(jnp.int32, words.shape, 1)
        words = jnp.where(which // 2 == lax.rem(me, 4) // 2, words, 0.0)
        den = den + jnp.sum(words, axis=-1, keepdims=True)
    attn = (num / den).astype(BF16)

    loads[5].wait()
    project(0, attn, w_out_ref)
    attn_proj = reduce_scatter(0)
    resid = hidden_ref[...].astype(F32) + rms_scale(attn_proj, gains_ref[1:2, :])
    resid = resid.astype(BF16).astype(F32)
    slab_ref[1] = rms_scale(resid, gains_ref[2:3, :]).astype(BF16)
    gather_start(1)
    gather_finish(1)
    loads[6].wait()
    loads[7].wait()
    gate = jnp.dot(rows_ref[...], w_gate_up_ref[0], preferred_element_type=F32)
    up = jnp.dot(rows_ref[...], w_gate_up_ref[1], preferred_element_type=F32)
    bent = jnp.tanh(math.sqrt(2.0 / math.pi) * (gate + 0.044715 * gate * gate * gate))
    hidden_units = (0.5 * gate * (1.0 + bent) * up).astype(BF16)
    project(1, hidden_units, w_down_ref)
    ffn_proj = reduce_scatter(1)
    out_ref[...] = resid + rms_scale(ffn_proj, gains_ref[3:4, :])

    for turn in range(2):
        gather_drain(turn)
        scatter_drain(turn)
        for step in PLANE_STEPS:
            z_copy(turn, step).wait_send()
    for step in PLANE_STEPS:
        limit_copy(step).wait_send()
        back_copy(step).wait_send()
    for i in range(2):
        for head in range(KV_HEADS):

            @pl.when(kv_server(head) != me)
            def _():
                kv_copy(i, head).wait_send()

    for m in range(4):

        @pl.when((me < HEADS) & (server_of(chip, m) != me))
        def _():
            to_server(m).wait_send()

        @pl.when(4 * served + m != me)
        def _():
            join_copy(m).wait_send()
            word_copy(m).wait_send()

    for step in range(1, n):
        owner_copy(step).wait_send()
        column_copy(step).wait_send()


def layer(n, planes, small, large):
    own, width = small[0].shape
    rows = own * n
    piece = large[4].shape[0]
    dma = pltpu.SemaphoreType.DMA

    def bf(*shape):
        return pltpu.VMEM(shape, BF16)

    def f32(*shape):
        return pltpu.VMEM(shape, F32)

    slots = planes * SLOTS
    scratch = [
        *(bf(*a.shape) for a in large),
        bf(2, own, width),
        bf(2, n, own, width),
        bf(rows, width),
        bf(KV_HEADS * piece, HEAD_DIM),
        bf(KV_HEADS * piece, HEAD_DIM),
        bf(rows, HEAD_DIM),
        bf(n, own, HEAD_DIM),
        bf(n, own, HEAD_DIM),
        bf(2, rows, HEAD_DIM),
        bf(slots, 2 * HEAD_DIM),
        bf(slots, 2 * HEAD_DIM),
        bf(slots, 2 * HEAD_DIM),
        bf(slots, 2 * HEAD_DIM),
        f32(own, HEADS, HEAD_DIM),
        f32(own, HEADS, HEAD_DIM),
        f32(own, HEADS, HEAD_DIM),
        f32(HEADS, own, HEAD_DIM + 128),
        bf(n, own, HEAD_DIM),
        bf(n, own, HEAD_DIM),
        f32(rows, HEAD_DIM),
        bf(4, rows, 128),
        bf(4, rows, 128),
        bf(2, 2, CHIPS, own, width),
        bf(2, CHIPS, own, width),
        bf(2, CHIPS, own, width),
        bf(2, CHIPS, own, width),
        bf(16, 128),
        bf(4, 16, 128),
        bf(slots, 128),
        bf(slots, 128),
        f32(8, 128),
        bf(2, 4, 128),
        bf(planes, 4, 128),
        bf(rows, planes * 128),
        dma((8,)),
        dma((2, CHIPS)),
        dma((2, CHIPS)),
        dma((2, CHIPS)),
        dma((2, CHIPS)),
        dma((2, KV_HEADS)),
        dma((2, KV_HEADS)),
        dma((n,)),
        dma((n,)),
        dma((4,)),
        dma((2,)),
        dma((2, planes)),
        dma((2, planes)),
        dma((n,)),
        dma((n,)),
        dma((4,)),
        dma((4,)),
        dma((2, 2)),
        dma((2, 2)),
        dma((2, 2, CHIPS)),
        dma((2, 2, CHIPS)),
        dma((2,)),
        dma((4,)),
        dma((4,)),
        dma((planes,)),
        dma((planes,)),
        dma((planes,)),
        dma((planes,)),
    ]
    return pl.pallas_call(
        functools.partial(layer_kernel, n, planes),
        out_shape=jax.ShapeDtypeStruct((own, width), F32),
        in_specs=[pl.BlockSpec(memory_space=pltpu.VMEM)] * len(small)
        + [pl.BlockSpec(memory_space=pl.ANY)] * len(large),
        out_specs=pl.BlockSpec(memory_space=pltpu.VMEM),
        scratch_shapes=scratch,
        compiler_params=pltpu.CompilerParams(
            collective_id=0, has_side_effects=True, vmem_limit_bytes=60 * 1024 * 1024
        ),
        name="layer",
    )(*small, *large)


def per_device(
    n,
    planes,
    hidden_in,
    norm_gains,
    w_qkv,
    w_out,
    w_gate_up,
    w_down,
    prompt_keys,
    prompt_values,
    tail_keys,
    tail_values,
    prompt_len,
    group_home,
    req_group,
    tail_len,
):
    return layer(
        n,
        planes,
        (
            hidden_in,
            norm_gains,
            prompt_len[None],
            group_home[None],
            req_group[None],
            tail_len[None],
        ),
        (w_qkv, w_out, w_gate_up, w_down, prompt_keys, prompt_values, tail_keys, tail_values),
    ).astype(BF16)


def solution(mesh):
    in_specs = (
        P(("grp", "tp"), None),
        P(),
        P(None, "tp"),
        P("tp", None),
        P(None, None, "tp"),
        P("tp", None),
        P(("grp", "tp"), None),
        P(("grp", "tp"), None),
        P(("grp", "tp"), None, None),
        P(("grp", "tp"), None, None),
        P(),
        P(),
        P("grp"),
        P("grp"),
    )
    return jax.shard_map(
        functools.partial(per_device, mesh.shape["tp"], mesh.shape["grp"]),
        mesh=mesh,
        in_specs=in_specs,
        out_specs=P(("grp", "tp"), None),
        check_vma=False,
    )
```
